32 devices in a mesh: ctx: 8 (over y, x, core), fsdp: 4 (over z).
Axes of the slice: x: 2, y: 2, z: 4, core: 2. Of those that a mesh axis runs over, the one named last changes fastest.
Arguments:
- tokens_in: bfloat16 [4, 4096, 1024], P('fsdp', 'ctx'), may hold values from -6 to 6
- value_first: bfloat16 [4, 4096, 1024], P('fsdp', 'ctx'), may hold values from -6 to 6
- out_grad: bfloat16 [4, 4096, 1024], P('fsdp', 'ctx'), may hold values from -6 to 6
- gain_attn: bfloat16 [1024], P('fsdp'), may hold values from 0.5 to 1.5
- w_qkv: bfloat16 [1024, 3072], P('fsdp'), may hold values from -0.1875 to 0.1875
- w_out: bfloat16 [1024, 1024], P('fsdp'), may hold values from -0.75 to 0.75
- gain_mlp: bfloat16 [1024], P('fsdp'), may hold values from 0.5 to 1.5
- w_gate_up: bfloat16 [1024, 5632], P('fsdp'), may hold values from -0.1875 to 0.1875
- w_down: bfloat16 [1024, 2816], P('fsdp'), may hold values from -0.109375 to 0.109375
- cont_lengths: int32 [4, 4], P('fsdp'), may hold values from 1 to 768, 2048 in all within a row
- row_token: int32 [4, 4096], P('fsdp', 'ctx'), may hold values from 0 to 4095, as said below
Outputs:
- mixed_out: bfloat16 [4, 4096, 1024], P('fsdp', 'ctx')
- input_grad: float32 [4, 4096, 1024], P('fsdp', 'ctx')
- first_value_grad: float32 [4, 4096, 1024], P('fsdp', 'ctx')
- gain_attn_grad: float32 [1024], P(('ctx', 'fsdp'))
- w_qkv_grad: float32 [1024, 3072], P(('ctx', 'fsdp'))
- w_out_grad: float32 [1024, 1024], P(('ctx', 'fsdp'))
- gain_mlp_grad: float32 [1024], P(('ctx', 'fsdp'))
- w_gate_up_grad: float32 [1024, 5632], P(('ctx', 'fsdp'))
- w_down_grad: float32 [1024, 2816], P(('ctx', 'fsdp'))
The draws below stay inside these ranges and needn't reach their ends.
Inputs may be any that keep to these rules, and one draw needn't show every extreme that they name: `cont_lengths`: the 4 lengths of a group sum to 2048; the longest is 768. Each group's row_token is a permutation of its tokens made of aligned runs of 256 consecutive tokens; each index of ctx holds 2 runs, exactly one of them from the prompt (tokens below 2048).
All inputs are finite; a program needn't handle non-finite values.
Results may differ from the reference program's by a relative error of at most 0.025.
Values may be sent and summed in bfloat16 or wider, within the bound.
No kernel may reach another device: no remote copies, remote signals or barrier semaphores. Data moves between devices by JAX's collectives and lax.ppermute only.
A program may use at most 512 MiB of HBM per device.

```python
import math
import jax
import jax.numpy as jnp
import numpy as np
from jax import lax

D = 1024
HEADS = 16
HEAD = 64
FF = 2816
ROWS_DEV = 512
PROMPT = 2048
LONGEST = 768
GROUP_ROWS = 4096
GROUPS = 4
NCONT = 4
BLOCK = 256


def draw_row_token(key, part):
    per_device = ROWS_DEV // BLOCK
    devices = GROUP_ROWS // ROWS_DEV
    blocks = GROUP_ROWS // BLOCK

    def one_group(subkey):
        first_key, second_key, third_key = jax.random.split(subkey, 3)
        prompt_order = jax.random.permutation(first_key, devices).astype(jnp.int32)
        prompt_slot = jax.random.randint(second_key, (devices,), 0, per_device).astype(jnp.int32)
        others = (devices + jax.random.permutation(third_key, blocks - devices)).astype(jnp.int32)
        slot_index = jnp.arange(per_device, dtype=jnp.int32)[None, :]
        device_index = jnp.arange(devices, dtype=jnp.int32)[:, None]
        later = (slot_index > prompt_slot[:, None]).astype(jnp.int32)
        other_index = jnp.clip(device_index * (per_device - 1) + slot_index - later, 0, blocks - devices - 1)
        block_id = jnp.where(slot_index == prompt_slot[:, None], prompt_order[:, None], others[other_index])
        tokens_of = block_id[:, :, None] * BLOCK + jnp.arange(BLOCK, dtype=jnp.int32)[None, None, :]
        return tokens_of.reshape(GROUP_ROWS).astype(jnp.int32)
    return jax.vmap(one_group)(jax.random.split(key, GROUPS))


def with_spikes(values, stream_key, source, target, parts, factor):
    owner, partner = [(jnp.arange(values.shape[dim]) // (values.shape[dim] // parts)).reshape([-1 if axis == dim else 1 for axis in range(values.ndim)]) for dim in (source, target)]
    chosen = jax.random.permutation(stream_key, parts)[partner]
    strong = (owner == chosen) | (owner == (partner + parts // 2) % parts)
    return jnp.where(strong, factor * values, values)


def steps_of(key, shape, cuts, low, largest):
    factor_of, own = 1.0, jax.random.fold_in(key, 6)
    for dim, parts in cuts:
        steps = jnp.exp(jax.random.uniform(jax.random.fold_in(own, dim), (parts,), jnp.float32, low / len(cuts), largest / len(cuts)))
        factor_of = factor_of * jnp.repeat(steps, shape[dim] // parts).reshape([-1 if axis == dim else 1 for axis in range(len(shape))])
    return factor_of


def profile(amount, total, limit, skew):
    portions = [(1 << 20) // math.isqrt(grade ** skew) + 1 for grade in range(2, amount + 1)]
    rest, given = total - limit - (amount - 1), [1] * (amount - 1)
    while rest > 0:
        candidates = [i for i in range(amount - 1) if given[i] < limit]
        whole, remaining = sum([portions[i] for i in candidates]), rest
        for i in candidates:
            more = min(limit - given[i], max(1, remaining * portions[i] // whole), rest)
            given[i] = given[i] + more
            rest = rest - more
    return np.array([limit] + given)


def uneven(rng, amount, total, limit, slope):
    if amount == 2:
        one = jax.random.randint(rng, (), max(1, total - limit), min(limit, total - 1) + 1)
        return jnp.stack([one, total - one])
    sizes = jnp.asarray(profile(amount, total, limit, slope), jnp.int32)
    pairs = (amount - 1) // 2
    donor, sink = sizes[1:1 + 2 * pairs:2], sizes[2:2 + 2 * pairs:2]
    margin = jnp.minimum(donor - 1, limit - sink)
    moved = jax.random.randint(jax.random.fold_in(rng, 1), (pairs,), 0, 1 << 20) % (margin + 1)
    sizes = sizes.at[1:1 + 2 * pairs:2].set(donor - moved).at[2:2 + 2 * pairs:2].set(sink + moved)
    return sizes[jax.random.permutation(jax.random.fold_in(rng, 2), amount)]


def gaussian(own_key, shape, deviation, most, cuts=(), kind=jnp.bfloat16):
    entries = deviation * jax.random.normal(own_key, shape, jnp.float32)
    if cuts:
        entries = entries * steps_of(own_key, shape, cuts, -0.22, 0.18)
    return jnp.clip(entries, -most, most).astype(kind)


def bell_draw_with(rng, shape, scale, limit, shards, heavy, held_as=jnp.bfloat16):
    array = scale * jax.random.normal(rng, shape, jnp.float32)
    if shards:
        array = array * steps_of(rng, shape, shards, -0.22, 0.18)
    return jnp.clip(with_spikes(array, jax.random.fold_in(rng, 3), *heavy), -limit, limit).astype(held_as)


def setup_inputs(seed: int = 0) -> dict:
    splits = jax.random.split(jax.random.key(seed), 12)
    return {
        "tokens_in": gaussian(splits[0], (GROUPS, GROUP_ROWS, D), 1.0, 6.0, ((0, 4), (1, 8))),
        "value_first": gaussian(splits[1], (GROUPS, GROUP_ROWS, D), 1.0, 6.0, ((0, 4), (1, 8))),
        "out_grad": bell_draw_with(splits[2], (GROUPS, GROUP_ROWS, D), 1.0, 6.0, ((0, 4), (1, 8)), (1, 2, 8, 2.0)),
        "gain_attn": jnp.clip(1.0 + 0.1 * jax.random.normal(splits[3], (D,), jnp.float32), 0.5, 1.5).astype(jnp.bfloat16),
        "w_qkv": gaussian(splits[4], (D, 3 * D), D ** -0.5, 0.1875, ((0, 4),)),
        "w_out": gaussian(splits[5], (D, D), (D // 16) ** -0.5, 0.75, ((0, 4),)),
        "gain_mlp": jnp.clip(1.0 + 0.1 * jax.random.normal(splits[6], (D,), jnp.float32), 0.5, 1.5).astype(jnp.bfloat16),
        "w_gate_up": gaussian(splits[7], (D, 2 * FF), D ** -0.5, 0.1875, ((0, 4),)),
        "w_down": gaussian(splits[8], (D, FF), FF ** -0.5, 0.109375, ((0, 4),)),
        "cont_lengths": jax.vmap(lambda own: uneven(own, NCONT, GROUP_ROWS - PROMPT, LONGEST, 1))(jax.random.split(splits[9], GROUPS)).reshape((GROUPS, NCONT)).astype(jnp.int32),
        "row_token": draw_row_token(jax.random.fold_in(splits[11], 71), 0),
    }


EPS = 1e-05
BASE = 10000.0
SCALE = 0.125
NEG = -1e+30
PRECISE = lax.Precision.HIGHEST

@jax.custom_vjp
def low(v):
    return lax.optimization_barrier(v.astype(jnp.bfloat16)).astype(jnp.float32)

@jax.custom_vjp
def low_back(v):
    return v

def low_keep(v):
    return (low(v), None)

def low_pass(kept, grad):
    return (grad,)

def back_keep(v):
    return (v, None)

def back_low(kept, grad):
    return (low(grad),)
low.defvjp(low_keep, low_pass)
low_back.defvjp(back_keep, back_low)

def places(token_index, lengths):
    token_index = token_index.astype(jnp.int32)
    lengths = lengths.astype(jnp.int32)
    starts = (PROMPT + jnp.cumsum(lengths) - lengths).astype(jnp.int32)
    passed = token_index[:, None] >= starts[None, :]
    segment = lax.optimization_barrier(jnp.sum(passed.astype(jnp.int32), axis=1)).astype(jnp.int32)
    opening = lax.optimization_barrier(jnp.max(jnp.where(passed, starts[None, :], 0), axis=1)).astype(jnp.int32)
    position = jnp.where(segment > 0, PROMPT + token_index - opening, token_index).astype(jnp.int32)
    return (segment, position)

def rotary(position):
    half_head = HEAD // 2
    frequency = BASE ** (-(jnp.arange(half_head, dtype=jnp.float32) * 2.0 / HEAD))
    angles = position.astype(jnp.float32)[:, None] * frequency[None, :]
    return (jnp.cos(angles)[:, None, :], jnp.sin(angles)[:, None, :])

def rotate(vectors, cos_table, sin_table):
    half_head = HEAD // 2
    leading = vectors[..., :half_head]
    trailing = vectors[..., half_head:]
    return jnp.concatenate([leading * cos_table - trailing * sin_table, trailing * cos_table + leading * sin_table], axis=-1)

def allowed(query_tokens, query_segment, key_tokens, key_segment):
    causal = key_tokens[None, :] <= query_tokens[:, None]
    shared = (key_segment[None, :] == 0) | (key_segment[None, :] == query_segment[:, None])
    return causal & shared

def matmul(operand, partner):
    return jnp.dot(operand, partner, precision=PRECISE, preferred_element_type=jnp.float32)

def normalize(values):
    return values * lax.rsqrt(lax.optimization_barrier(jnp.mean(values * values, axis=-1, keepdims=True)) + EPS)

def attend_group(packed):
    queries, keys_rot, values_low, tokens_of, segment = packed
    group_rows = queries.shape[0]
    block = min(512, group_rows)
    key_heads = keys_rot.reshape(group_rows, HEADS, HEAD)
    value_heads = values_low.reshape(group_rows, HEADS, HEAD)

    def one_block(blocked):
        query_blk, query_tokens, query_segment = blocked
        visible = allowed(query_tokens, query_segment, tokens_of, segment)[None]
        scores = low_back(jnp.einsum('qhd,khd->hqk', query_blk.reshape(block, HEADS, HEAD), key_heads, precision=PRECISE) * SCALE)
        scores = jnp.where(visible, scores, NEG)
        top_score = lax.optimization_barrier(jnp.max(scores, axis=2, keepdims=True))
        raised = jnp.where(visible, jnp.exp(scores - top_score), 0.0)
        probs = raised / lax.optimization_barrier(jnp.sum(raised, axis=2, keepdims=True))
        return jnp.einsum('hqk,khd->qhd', low(probs), value_heads, precision=PRECISE).reshape(block, D)
    blocked = (queries.reshape(group_rows // block, block, D), tokens_of.reshape(group_rows // block, block), segment.reshape(group_rows // block, block))
    return lax.map(jax.checkpoint(one_block), blocked).reshape(group_rows, D)

def reference(tokens_in, value_first, out_grad, gain_attn, w_qkv, w_out, gain_mlp, w_gate_up, w_down, cont_lengths, row_token):
    groups = row_token.shape[0]
    group_rows = row_token.shape[1]
    total_rows = groups * group_rows
    segment, position = jax.vmap(places)(row_token, cont_lengths)
    cos_table, sin_table = rotary(position.reshape(total_rows))

    def forward(inputs, first_value, gain_one, weight_qkv, weight_out, gain_two, weight_gate_up, weight_down):
        flat = inputs.reshape(total_rows, D)
        normed_one = low(normalize(flat) * gain_one)
        projected = low_back(matmul(normed_one, weight_qkv))
        queries = low(rotate(projected[:, :D].reshape(total_rows, HEADS, HEAD), cos_table, sin_table))
        keys_rot = low(rotate(projected[:, D:2 * D].reshape(total_rows, HEADS, HEAD), cos_table, sin_table))
        values_low = low(0.5 * projected[:, 2 * D:] + 0.5 * first_value.reshape(total_rows, D))
        attention = lax.map(attend_group, (queries.reshape(groups, group_rows, D), keys_rot.reshape(groups, group_rows, D), values_low.reshape(groups, group_rows, D), row_token.astype(jnp.int32), segment))
        attn_low = low(low_back(attention.reshape(total_rows, D)))
        middle = flat + low_back(matmul(attn_low, weight_out))
        normed_two = low(normalize(middle) * gain_two)
        gate_up = low_back(matmul(normed_two, weight_gate_up))
        hidden = low(jax.nn.silu(gate_up[:, :FF]) * gate_up[:, FF:])
        result = middle + low_back(matmul(hidden, weight_down.T))
        return result.reshape(groups, group_rows, D)
    result, pull = jax.vjp(forward, tokens_in.astype(jnp.float32), value_first.astype(jnp.float32), gain_attn.astype(jnp.float32), w_qkv.astype(jnp.float32), w_out.astype(jnp.float32), gain_mlp.astype(jnp.float32), w_gate_up.astype(jnp.float32), w_down.astype(jnp.float32))
    grads = pull(out_grad.astype(jnp.float32))
    return (result.astype(jnp.bfloat16), grads[0], grads[1], grads[2], grads[3], grads[4], grads[5], grads[6], grads[7])
```

```python
import jax
import jax.numpy as jnp
from jax import lax
from jax.experimental import pallas as pl
from jax.experimental.pallas import tpu as pltpu
from jax.sharding import Mesh, PartitionSpec as P

D = 1024
HEADS = 16
HEAD = 64
FF = 2816
PROMPT = 2048
EPS = 1e-05
BASE = 10000.0
LOG2E = 1.4426950408889634
NEG = -1e30
C2 = 0.125 * LOG2E
CTX = ("chip", "core")
BF = jnp.bfloat16
F32 = jnp.float32


def dot(a,b,dims): return lax.dot_general(a,b,(dims,((),())),preferred_element_type=jnp.float32)
NN=((1,),(0,)); NT=((1,),(1,)); TN=((0,),(0,))

def chunked(lo_, hi_, sizes, fn, c):
    for n in sizes:
        cnt=(hi_-lo_)//n
        c=lax.fori_loop(0,cnt,lambda t,c,n=n,lo_=lo_: fn(lo_+t*n,c,n),c)
        lo_=lo_+cnt*n
    return c

def attn_fwd(qT,kn,vT,lo,jlo,spos, *, run, nprompt, fsz=(4,2,1), msz=(2,1)):
    W,S=qT.shape; hl=W//HEAD; nb=S//run
    def kern(jlo_ref, spos_ref, q_ref,k_ref,v_ref,lo_ref,o_ref,of_ref,lse_ref):
        i=pl.program_id(0)
        qs=[q_ref[h*HEAD:(h+1)*HEAD,:] for h in range(hl)]
        def tile(j, carry, n, masked):
            kb=n*run
            off=pl.multiple_of(j*run,run)
            out=[]
            if masked:
                ct=j*run+lax.broadcasted_iota(jnp.int32,(kb,run),0)
                rt=i*run+lax.broadcasted_iota(jnp.int32,(kb,run),1)
                vis=(ct<=rt)&(ct>=lo_ref[...])
            for h in range(hl):
                m,l,acc=carry[h]
                s=dot(k_ref[h,pl.ds(off,kb),:],qs[h],NN)
                if masked: s=jnp.where(vis,s,NEG)
                mn=jnp.maximum(m,jnp.max(s,axis=0,keepdims=True)*C2)
                p=jnp.exp2(s*C2-mn)
                a=jnp.exp2(m-mn)
                l=l*a+jnp.sum(p,axis=0,keepdims=True)
                acc=acc*a+dot(v_ref[h*HEAD:(h+1)*HEAD,pl.ds(off,kb)],p.astype(jnp.bfloat16),NN)
                out.append((mn,l,acc))
            return tuple(out)
        init=tuple((jnp.full((1,run),NEG,jnp.float32),jnp.zeros((1,run),jnp.float32),jnp.zeros((HEAD,run),jnp.float32)) for _ in range(hl))
        c=chunked(0,jnp.minimum(i,nprompt),fsz,lambda j,c,n:tile(j,c,n,False),init)
        c=chunked(jlo_ref[i],i+1,msz,lambda j,c,n:tile(j,c,n,True),c)
        outs=[]
        for h in range(hl):
            m,l,acc=c[h]
            o=acc/l
            of_ref[h*HEAD:(h+1)*HEAD,:]=o
            lse_ref[h,:,:]=m+jnp.log2(l)
            outs.append(o)
        o=jnp.concatenate(outs,axis=0) if hl>1 else outs[0]
        o_ref[...]=o.T.astype(jnp.bfloat16)
    full=lambda *s: pl.BlockSpec(s,lambda i,*_:(0,)*len(s))
    return pl.pallas_call(kern,
        out_shape=(jax.ShapeDtypeStruct((S,W),jnp.bfloat16),jax.ShapeDtypeStruct((W,S),jnp.float32),jax.ShapeDtypeStruct((hl,1,S),jnp.float32)),
        grid_spec=pltpu.PrefetchScalarGridSpec(num_scalar_prefetch=2,grid=(nb,),
            in_specs=[pl.BlockSpec((W,run),lambda i,*_:(0,i)),full(hl,S,HEAD),full(W,S),pl.BlockSpec((1,run),lambda i,*_:(0,i))],
            out_specs=[pl.BlockSpec((run,W),lambda i,jl,sp:(sp[i],0)),pl.BlockSpec((W,run),lambda i,*_:(0,i)),pl.BlockSpec((hl,1,run),lambda i,*_:(0,0,i))]),
        compiler_params=pltpu.CompilerParams(vmem_limit_bytes=48<<20),
        name="attention_forward",
    )(jlo,spos,qT,kn,vT,lo)

def attn_bwd(qT,kn,kT,vn,don,of,lse,lo,jlo,spos,cosT,sinT, *, run, nprompt, fsz=(2,1), msz=(1,)):
    W,S=qT.shape; hl=W//HEAD; nb=S//run; hh=HEAD//2
    def unrot(g,cos,sin):
        parts=[]
        for h in range(hl):
            a=g[h*HEAD:h*HEAD+hh]; b=g[h*HEAD+hh:(h+1)*HEAD]
            parts += [a*cos+b*sin, b*cos-a*sin]
        return jnp.concatenate(parts,axis=0)
    def kern(jlo_ref, spos_ref, q_ref,k_ref,kT_ref,v_ref,do_ref,of_ref,lse_ref,lo_ref,cos_ref,sin_ref,dq_ref,dk_ref,dv_ref,dkT,dvT):
        i=pl.program_id(0)
        @pl.when(i==0)
        def _():
            dkT[...]=jnp.zeros_like(dkT); dvT[...]=jnp.zeros_like(dvT)
        doT=do_ref[...].T
        dof=doT.astype(jnp.float32)
        qs=[q_ref[h*HEAD:(h+1)*HEAD,:] for h in range(hl)]
        dos=[doT[h*HEAD:(h+1)*HEAD,:] for h in range(hl)]
        dl=[jnp.sum(dof[h*HEAD:(h+1)*HEAD]*of_ref[h*HEAD:(h+1)*HEAD,:],axis=0,keepdims=True) for h in range(hl)]
        ls=[lse_ref[h,:,:] for h in range(hl)]
        def tile(j, carry, n, masked):
            kb=n*run
            off=pl.multiple_of(j*run,run)
            if masked:
                ct=j*run+lax.broadcasted_iota(jnp.int32,(kb,run),0)
                rt=i*run+lax.broadcasted_iota(jnp.int32,(kb,run),1)
                vis=(ct<=rt)&(ct>=lo_ref[...])
            out=[]
            for h in range(hl):
                hs=slice(h*HEAD,(h+1)*HEAD)
                s=dot(k_ref[h,pl.ds(off,kb),:],qs[h],NN)
                p=jnp.exp2(s*C2-ls[h])
                if masked: p=jnp.where(vis,p,0.0)
                dp=dot(v_ref[h,pl.ds(off,kb),:],dos[h],NN)
                ds=(p*(dp-dl[h])).astype(jnp.bfloat16)
                dvT[hs,pl.ds(off,kb)]+=dot(dos[h],p.astype(jnp.bfloat16),NT)
                dkT[hs,pl.ds(off,kb)]+=dot(qs[h],ds,NT)
                out.append(carry[h]+dot(kT_ref[hs,pl.ds(off,kb)],ds,NN))
            return tuple(out)
        c=tuple(jnp.zeros((HEAD,run),jnp.float32) for _ in range(hl))
        c=chunked(0,jnp.minimum(i,nprompt),fsz,lambda j,c,n:tile(j,c,n,False),c)
        c=chunked(jlo_ref[i],i+1,msz,lambda j,c,n:tile(j,c,n,True),c)
        dq=jnp.concatenate(c,axis=0)*0.125
        off=pl.multiple_of(i*run,run)
        srow=pl.multiple_of(spos_ref[i]*run,run)
        dq_ref[pl.ds(srow,run),:]=unrot(dq,cos_ref[:,pl.ds(off,run)],sin_ref[:,pl.ds(off,run)]).T.astype(jnp.bfloat16)
        @pl.when(i==nb-1)
        def _():
            def fin(b,_):
                off=pl.multiple_of(b*run,run)
                srow=pl.multiple_of(spos_ref[b]*run,run)
                g=dkT[:,pl.ds(off,run)]*0.125
                dk_ref[pl.ds(srow,run),:]=unrot(g,cos_ref[:,pl.ds(off,run)],sin_ref[:,pl.ds(off,run)]).T.astype(jnp.bfloat16)
                dv_ref[pl.ds(srow,run),:]=(dvT[:,pl.ds(off,run)]*0.5).T.astype(jnp.bfloat16)
                return 0
            lax.fori_loop(0,nb,fin,0)
    full=lambda *s: pl.BlockSpec(s,lambda i,*_:(0,)*len(s))
    o=jax.ShapeDtypeStruct((S,W),jnp.bfloat16)
    return pl.pallas_call(kern,
        out_shape=(o,o,o),
        grid_spec=pltpu.PrefetchScalarGridSpec(num_scalar_prefetch=2,grid=(nb,),
            in_specs=[pl.BlockSpec((W,run),lambda i,*_:(0,i)),full(hl,S,HEAD),full(W,S),full(hl,S,HEAD),
                      pl.BlockSpec((run,W),lambda i,jl,sp:(sp[i],0)),pl.BlockSpec((W,run),lambda i,*_:(0,i)),pl.BlockSpec((hl,1,run),lambda i,*_:(0,0,i)),
                      pl.BlockSpec((1,run),lambda i,*_:(0,i)),full(HEAD//2,S),full(HEAD//2,S)],
            out_specs=[full(S,W)]*3,
            scratch_shapes=[pltpu.VMEM((W,S),jnp.float32)]*2),
        compiler_params=pltpu.CompilerParams(vmem_limit_bytes=48<<20),
        name="attention_backward",
    )(jlo,spos,qT,kn,kT,vn,don,of,lse,lo,cosT,sinT)


def project(n1, w, vf, cos, sin, blk, *, run):
    S=n1.shape[0]; W=vf.shape[1]; hl=W//HEAD; nb=S//run; hh=HEAD//2
    def kern(blk_ref, n_ref, w_ref, vf_ref, c_ref, s_ref, q_o, kT_o, vT_o, kn_o, vn_o):
        t=dot(w_ref[...],n_ref[...],NT)
        c=c_ref[...]; s=s_ref[...]
        def rope(base):
            parts=[]
            for h in range(hl):
                a=t[base+h*HEAD:base+h*HEAD+hh]; b=t[base+h*HEAD+hh:base+(h+1)*HEAD]
                parts += [a*c-b*s, b*c+a*s]
            return jnp.concatenate(parts,axis=0)
        q_o[...]=rope(0).astype(BF)
        k=rope(W)
        kT_o[...]=k.astype(BF)
        v=0.5*t[2*W:]+0.5*vf_ref[...].astype(F32).T
        vT_o[...]=v.astype(BF)
        for h in range(hl):
            kn_o[h]=k[h*HEAD:(h+1)*HEAD].T.astype(BF)
            vn_o[h]=v[h*HEAD:(h+1)*HEAD].T.astype(BF)
    T=jax.ShapeDtypeStruct((W,S),BF); N=jax.ShapeDtypeStruct((hl,S,HEAD),BF)
    tb=pl.BlockSpec((W,run),lambda r,b:(0,b[r])); nbk=pl.BlockSpec((hl,run,HEAD),lambda r,b:(0,b[r],0))
    return pl.pallas_call(kern,out_shape=(T,T,T,N,N),
        grid_spec=pltpu.PrefetchScalarGridSpec(num_scalar_prefetch=1,grid=(nb,),
            in_specs=[pl.BlockSpec((run,D),lambda r,b:(r,0)),pl.BlockSpec((3*W,D),lambda r,b:(0,0)),pl.BlockSpec((run,W),lambda r,b:(r,0)),
                      pl.BlockSpec((hh,run),lambda r,b:(0,b[r])),pl.BlockSpec((hh,run),lambda r,b:(0,b[r]))],
            out_specs=[tb,tb,tb,nbk,nbk]),
        compiler_params=pltpu.CompilerParams(vmem_limit_bytes=48<<20),
        name="project_qkv",
    )(blk,n1,w,vf,cos,sin)


def exchange(v):
    return lax.all_to_all(v, CTX, 0, 0, tiled=True)


def body(tokens_in, value_first, out_grad, gain_attn, w_qkv, w_out, gain_mlp, w_gate_up, w_down, cont_lengths, row_token):
    inputs = tokens_in[0].astype(F32)
    rows = inputs.shape[0]
    nctx = lax.axis_size(CTX)
    nz = lax.axis_size("z")
    me = lax.axis_index(CTX)
    S = rows * nctx
    W = D // nctx
    run = PROMPT // nctx
    nb = S // run
    nprompt = PROMPT // run
    lengths = cont_lengths[0]
    count = jnp.arange(lengths.shape[0], dtype=jnp.int32)
    starts = PROMPT + jnp.sum(jnp.where(count[:, None] < count[None, :], lengths[:, None], 0), axis=0)
    token = jnp.arange(S, dtype=jnp.int32)
    passed = token[None, :] >= starts[:, None]
    opening = jnp.max(jnp.where(passed, starts[:, None], 0), axis=0).astype(jnp.int32)
    position = jnp.where(opening > 0, PROMPT + token - opening, token)
    freq = BASE ** (-(jnp.arange(HEAD // 2, dtype=F32) * 2.0 / HEAD))
    angles = freq[:, None] * position.astype(F32)[None, :]
    cosT = jnp.cos(angles)
    sinT = jnp.sin(angles)
    block = jnp.arange(nb, dtype=jnp.int32)
    jlo = jnp.where(block < nprompt, block, opening[::run] // run).astype(jnp.int32)
    blk = lax.all_gather(row_token[0, ::run], CTX, axis=0, tiled=True) // run
    spos = jnp.sum(jnp.where(blk[None, :] == block[:, None], block[None, :], 0), axis=1).astype(jnp.int32)

    inverse_one = lax.rsqrt(jnp.mean(inputs * inputs, axis=1, keepdims=True) + EPS)
    unit_one = inputs * inverse_one
    gains = lax.all_gather(jnp.stack([gain_attn, gain_mlp]), "z", axis=1, tiled=True).astype(F32)
    gain_one, gain_two = gains[0], gains[1]
    normed_one = (unit_one * gain_one).astype(BF)
    normed_all = lax.all_gather(normed_one, CTX, axis=0, tiled=True)
    w_own = lax.dynamic_index_in_dim(w_qkv.reshape(D // nz, 3, nctx, W), me, 2, keepdims=False).reshape(D // nz, 3 * W)
    w_own = lax.all_gather(w_own, "z", axis=0, tiled=True).T
    vf_all = exchange(value_first[0].reshape(rows, nctx, W).transpose(1, 0, 2)).reshape(S, W)
    qT, kT, vT, kn, vn = project(normed_all, w_own, vf_all, cosT, sinT, blk, run=run)
    opening2 = opening[None, :]
    attn_all, attnT, lse = attn_fwd(qT, kn, vT, opening2, jlo, spos, run=run, nprompt=nprompt, fsz=(8, 4, 2, 1), msz=(4, 2, 1))
    attn_low = exchange(attn_all.reshape(nctx, rows, W)).transpose(1, 0, 2).reshape(rows, D)

    out_whole = lax.all_gather(w_out, "z", axis=0, tiled=True)
    gate_whole = lax.all_gather(w_gate_up, "z", axis=0, tiled=True)
    down_whole = lax.all_gather(w_down, "z", axis=0, tiled=True)
    qkv_whole = lax.all_gather(w_qkv, "z", axis=0, tiled=True)
    middle = inputs + dot(attn_low, out_whole, NN)
    inverse_two = lax.rsqrt(jnp.mean(middle * middle, axis=1, keepdims=True) + EPS)
    unit_two = middle * inverse_two
    normed_two = (unit_two * gain_two).astype(BF)
    gu = dot(normed_two, gate_whole, NN)
    gate_in = gu[:, :FF]
    upward = gu[:, FF:]
    sigmoid_gate = jax.nn.sigmoid(gate_in)
    hidden = (gate_in * sigmoid_gate * upward).astype(BF)
    grad_low = out_grad[0]
    grad_hidden = dot(grad_low, down_whole, NN)
    grad_gate = grad_hidden * upward * sigmoid_gate * (1.0 + gate_in * (1.0 - sigmoid_gate))
    grad_upward = grad_hidden * gate_in * sigmoid_gate
    grad_gate_up = jnp.concatenate([grad_gate, grad_upward], axis=1).astype(BF)
    mixed_out = (middle + dot(hidden, down_whole, NT)).astype(BF)
    grad_normed = dot(grad_gate_up, gate_whole, NT)
    grad_unit_two = grad_normed * gain_two
    gain_two_total = jnp.sum(grad_normed * unit_two, axis=0)
    grad_middle = grad_low.astype(F32) + inverse_two * (
        grad_unit_two - unit_two * jnp.mean(grad_unit_two * unit_two, axis=1, keepdims=True)
    )
    grad_branch = grad_middle.astype(BF)
    grad_attn = dot(grad_branch, out_whole, NT).astype(BF)
    grad_attn_all = exchange(grad_attn.reshape(rows, nctx, W).transpose(1, 0, 2)).reshape(S, W)
    dq, dk, dv = attn_bwd(qT, kn, kT, vn, grad_attn_all, attnT, lse, opening2, jlo, spos, cosT, sinT, run=run, nprompt=nprompt, fsz=(4, 2, 1), msz=(2, 1))
    dqkv_own = jnp.concatenate([dq, dk, dv], axis=1)

    terms = jnp.concatenate([dot(attn_low, grad_branch, TN).astype(BF), dot(normed_two, grad_gate_up, TN).astype(BF), dot(grad_low, hidden, TN).astype(BF)], axis=1)
    received = exchange(terms.reshape(nctx, D // nctx, terms.shape[1]))
    share = jnp.sum(received.astype(F32), axis=0).astype(BF)
    share = lax.psum_scatter(share, "z", scatter_dimension=0, tiled=True).astype(F32)

    qkv_term = dot(normed_all, dqkv_own, TN).astype(BF)
    qkv_term = qkv_term.reshape(nctx, nz, D // (nctx * nz), 3 * W).transpose(1, 0, 2, 3)
    qkv_term = lax.psum_scatter(qkv_term, "z", scatter_dimension=0, tiled=True)[0]
    qkv_share = exchange(qkv_term).reshape(nctx, D // (nctx * nz), 3, W).transpose(1, 2, 0, 3).reshape(D // (nctx * nz), 3 * D).astype(F32)

    dqkv = exchange(dqkv_own.reshape(nctx, rows, 3 * W)).reshape(nctx, rows, 3, W).transpose(1, 2, 0, 3).reshape(rows, 3 * D)
    first_value_grad = dqkv[:, 2 * D :].astype(F32)
    grad_normed = dot(dqkv, qkv_whole, NT)
    grad_unit = grad_normed * gain_one
    gain_one_total = jnp.sum(grad_normed * unit_one, axis=0)
    input_grad = grad_middle + inverse_one * (
        grad_unit - unit_one * jnp.mean(grad_unit * unit_one, axis=1, keepdims=True)
    )
    gain_share = lax.psum_scatter(jnp.stack([gain_one_total, gain_two_total], axis=1), ("chip", "core", "z"), scatter_dimension=0, tiled=True)
    return (
        mixed_out[None],
        input_grad[None],
        first_value_grad[None],
        gain_share[:, 0],
        qkv_share,
        share[:, :D],
        gain_share[:, 1],
        share[:, D : D + 2 * FF],
        share[:, D + 2 * FF :],
    )


def solution(mesh):
    ctx, fsdp = mesh.devices.shape
    split = Mesh(mesh.devices.reshape(ctx // 2, 2, fsdp), ("chip", "core", "z"))
    rows3 = P("z", CTX, None)
    weight = P("z", None)
    every = ("chip", "core", "z")
    return jax.shard_map(
        body,
        mesh=split,
        in_specs=(rows3, rows3, rows3, P("z"), weight, weight, P("z"), weight, weight, weight, P("z", CTX)),
        out_specs=(rows3, rows3, rows3, P(every), P(every, None), P(every, None), P(every), P(every, None), P(every, None)),
        check_vma=False,
    )
```

```python
import jax
import jax.numpy as jnp
from jax import lax
from jax.experimental import pallas as pl
from jax.experimental.pallas import tpu as pltpu
from jax.sharding import Mesh, PartitionSpec as P

D = 1024
HEADS = 16
HEAD = 64
FF = 2816
PROMPT = 2048
EPS = 1e-05
BASE = 10000.0
LOG2E = 1.4426950408889634
NEG = -1e30
C2 = 0.125 * LOG2E
CTX = ("chip", "core")
BF = jnp.bfloat16
F32 = jnp.float32


def dot(a,b,dims): return lax.dot_general(a,b,(dims,((),())),preferred_element_type=jnp.float32)
NN=((1,),(0,)); NT=((1,),(1,)); TN=((0,),(0,))

def chunked(lo_, hi_, sizes, fn, c):
    for n in sizes:
        cnt=(hi_-lo_)//n
        c=lax.fori_loop(0,cnt,lambda t,c,n=n,lo_=lo_: fn(lo_+t*n,c,n),c)
        lo_=lo_+cnt*n
    return c

def attn_fwd(qT,kn,vT,lo,jlo,spos, *, run, nprompt, fsz=(4,2,1), msz=(2,1)):
    W,S=qT.shape; hl=W//HEAD; nb=S//run
    def kern(jlo_ref, spos_ref, q_ref,k_ref,v_ref,lo_ref,o_ref,of_ref,lse_ref):
        i=pl.program_id(0)
        qs=[q_ref[h*HEAD:(h+1)*HEAD,:] for h in range(hl)]
        def tile(j, carry, n, masked):
            kb=n*run
            off=pl.multiple_of(j*run,run)
            out=[]
            if masked:
                ct=j*run+lax.broadcasted_iota(jnp.int32,(kb,run),0)
                rt=i*run+lax.broadcasted_iota(jnp.int32,(kb,run),1)
                vis=(ct<=rt)&(ct>=lo_ref[...])
            for h in range(hl):
                m,l,acc=carry[h]
                s=dot(k_ref[h,pl.ds(off,kb),:],qs[h],NN)
                if masked: s=jnp.where(vis,s,NEG)
                mn=jnp.maximum(m,jnp.max(s,axis=0,keepdims=True)*C2)
                p=jnp.exp2(s*C2-mn)
                a=jnp.exp2(m-mn)
                l=l*a+jnp.sum(p,axis=0,keepdims=True)
                acc=acc*a+dot(v_ref[h*HEAD:(h+1)*HEAD,pl.ds(off,kb)],p.astype(jnp.bfloat16),NN)
                out.append((mn,l,acc))
            return tuple(out)
        init=tuple((jnp.full((1,run),NEG,jnp.float32),jnp.zeros((1,run),jnp.float32),jnp.zeros((HEAD,run),jnp.float32)) for _ in range(hl))
        c=chunked(0,jnp.minimum(i,nprompt),fsz,lambda j,c,n:tile(j,c,n,False),init)
        c=chunked(jlo_ref[i],i+1,msz,lambda j,c,n:tile(j,c,n,True),c)
        outs=[]
        for h in range(hl):
            m,l,acc=c[h]
            o=acc/l
            of_ref[h*HEAD:(h+1)*HEAD,:]=o
            lse_ref[h,:,:]=m+jnp.log2(l)
            outs.append(o)
        o=jnp.concatenate(outs,axis=0) if hl>1 else outs[0]
        o_ref[...]=o.T.astype(jnp.bfloat16)
    full=lambda *s: pl.BlockSpec(s,lambda i,*_:(0,)*len(s))
    return pl.pallas_call(kern,
        out_shape=(jax.ShapeDtypeStruct((S,W),jnp.bfloat16),jax.ShapeDtypeStruct((W,S),jnp.float32),jax.ShapeDtypeStruct((hl,1,S),jnp.float32)),
        grid_spec=pltpu.PrefetchScalarGridSpec(num_scalar_prefetch=2,grid=(nb,),
            in_specs=[pl.BlockSpec((W,run),lambda i,*_:(0,i)),full(hl,S,HEAD),full(W,S),pl.BlockSpec((1,run),lambda i,*_:(0,i))],
            out_specs=[pl.BlockSpec((run,W),lambda i,jl,sp:(sp[i],0)),pl.BlockSpec((W,run),lambda i,*_:(0,i)),pl.BlockSpec((hl,1,run),lambda i,*_:(0,0,i))]),
        compiler_params=pltpu.CompilerParams(vmem_limit_bytes=48<<20),
        cost_estimate=pl.CostEstimate(flops=14 * S * S * W, bytes_accessed=12 * S * W, transcendentals=S * S // 2),
        name="attention_forward",
    )(jlo,spos,qT,kn,vT,lo)

def attn_bwd(qT,kn,kT,vn,don,of,lse,lo,jlo,spos,cosT,sinT, *, run, nprompt, fsz=(2,1), msz=(1,)):
    W,S=qT.shape; hl=W//HEAD; nb=S//run; hh=HEAD//2
    def unrot(g,cos,sin):
        parts=[]
        for h in range(hl):
            a=g[h*HEAD:h*HEAD+hh]; b=g[h*HEAD+hh:(h+1)*HEAD]
            parts += [a*cos+b*sin, b*cos-a*sin]
        return jnp.concatenate(parts,axis=0)
    def kern(jlo_ref, spos_ref, q_ref,k_ref,kT_ref,v_ref,do_ref,of_ref,lse_ref,lo_ref,cos_ref,sin_ref,g_ref,dkT,dvT):
        i=pl.program_id(0)
        @pl.when(i==0)
        def _():
            dkT[...]=jnp.zeros_like(dkT); dvT[...]=jnp.zeros_like(dvT)
        doT=do_ref[...].T
        dof=doT.astype(jnp.float32)
        qs=[q_ref[h*HEAD:(h+1)*HEAD,:] for h in range(hl)]
        dos=[doT[h*HEAD:(h+1)*HEAD,:] for h in range(hl)]
        dl=[jnp.sum(dof[h*HEAD:(h+1)*HEAD]*of_ref[h*HEAD:(h+1)*HEAD,:],axis=0,keepdims=True) for h in range(hl)]
        ls=[lse_ref[h,:,:] for h in range(hl)]
        def tile(j, carry, n, masked):
            kb=n*run
            off=pl.multiple_of(j*run,run)
            if masked:
                ct=j*run+lax.broadcasted_iota(jnp.int32,(kb,run),0)
                rt=i*run+lax.broadcasted_iota(jnp.int32,(kb,run),1)
                vis=(ct<=rt)&(ct>=lo_ref[...])
            out=[]
            for h in range(hl):
                hs=slice(h*HEAD,(h+1)*HEAD)
                s=dot(k_ref[h,pl.ds(off,kb),:],qs[h],NN)
                p=jnp.exp2(s*C2-ls[h])
                if masked: p=jnp.where(vis,p,0.0)
                dp=dot(v_ref[h,pl.ds(off,kb),:],dos[h],NN)
                ds=(p*(dp-dl[h])).astype(jnp.bfloat16)
                dvT[hs,pl.ds(off,kb)]+=dot(dos[h],p.astype(jnp.bfloat16),NT)
                dkT[hs,pl.ds(off,kb)]+=dot(qs[h],ds,NT)
                out.append(carry[h]+dot(kT_ref[hs,pl.ds(off,kb)],ds,NN))
            return tuple(out)
        c=tuple(jnp.zeros((HEAD,run),jnp.float32) for _ in range(hl))
        c=chunked(0,jnp.minimum(i,nprompt),fsz,lambda j,c,n:tile(j,c,n,False),c)
        c=chunked(jlo_ref[i],i+1,msz,lambda j,c,n:tile(j,c,n,True),c)
        dq=jnp.concatenate(c,axis=0)*0.125
        off=pl.multiple_of(i*run,run)
        srow=pl.multiple_of(spos_ref[i]*run,run)
        g_ref[pl.ds(srow,run),:W]=unrot(dq,cos_ref[:,pl.ds(off,run)],sin_ref[:,pl.ds(off,run)]).T.astype(jnp.bfloat16)
        @pl.when(i==nb-1)
        def _():
            def fin(b,_):
                off=pl.multiple_of(b*run,run)
                srow=pl.multiple_of(spos_ref[b]*run,run)
                g=dkT[:,pl.ds(off,run)]*0.125
                g_ref[pl.ds(srow,run),W:2*W]=unrot(g,cos_ref[:,pl.ds(off,run)],sin_ref[:,pl.ds(off,run)]).T.astype(jnp.bfloat16)
                g_ref[pl.ds(srow,run),2*W:]=(dvT[:,pl.ds(off,run)]*0.5).T.astype(jnp.bfloat16)
                return 0
            lax.fori_loop(0,nb,fin,0)
    full=lambda *s: pl.BlockSpec(s,lambda i,*_:(0,)*len(s))
    return pl.pallas_call(kern,
        out_shape=jax.ShapeDtypeStruct((S,3*W),jnp.bfloat16),
        grid_spec=pltpu.PrefetchScalarGridSpec(num_scalar_prefetch=2,grid=(nb,),
            in_specs=[pl.BlockSpec((W,run),lambda i,*_:(0,i)),full(hl,S,HEAD),full(W,S),full(hl,S,HEAD),
                      pl.BlockSpec((run,W),lambda i,jl,sp:(sp[i],0)),pl.BlockSpec((W,run),lambda i,*_:(0,i)),pl.BlockSpec((hl,1,run),lambda i,*_:(0,0,i)),
                      pl.BlockSpec((1,run),lambda i,*_:(0,i)),full(HEAD//2,S),full(HEAD//2,S)],
            out_specs=full(S,3*W),
            scratch_shapes=[pltpu.VMEM((W,S),jnp.float32)]*2),
        compiler_params=pltpu.CompilerParams(vmem_limit_bytes=48<<20),
        cost_estimate=pl.CostEstimate(flops=16 * S * S * W, bytes_accessed=24 * S * W, transcendentals=S * S // 2),
        name="attention_backward",
    )(jlo,spos,qT,kn,kT,vn,don,of,lse,lo,cosT,sinT)


def cost(flops, nbytes, trans=0):
    return pl.CostEstimate(flops=int(flops), bytes_accessed=int(nbytes), transcendentals=int(trans))


def whole(*shape):
    return pl.BlockSpec(shape, lambda *_: (0,) * len(shape))


ANY = pl.BlockSpec(memory_space=pl.ANY)


def params():
    return pltpu.CompilerParams(vmem_limit_bytes=56 << 20)


def project(x, gain, w, vf, cos, sin, blk, *, run):
    S = x.shape[0]
    W = vf.shape[2]
    hl = W // HEAD
    nb = S // run
    per = nb // vf.shape[0]
    hh = HEAD // 2

    def kern(blk_ref, x_ref, g_ref, w_ref, vf_ref, c_ref, s_ref, n_o, q_o, kT_o, vT_o, kn_o, vn_o):
        xf = x_ref[...].astype(F32)
        inv = lax.rsqrt(jnp.mean(xf * xf, axis=1, keepdims=True) + EPS)
        n1 = (xf * inv * g_ref[...]).astype(BF)
        n_o[...] = n1
        t = dot(w_ref[...], n1, NT)
        c = c_ref[...]
        s = s_ref[...]

        def rope(base):
            parts = []
            for h in range(hl):
                a = t[base + h * HEAD : base + h * HEAD + hh]
                b = t[base + h * HEAD + hh : base + (h + 1) * HEAD]
                parts += [a * c - b * s, b * c + a * s]
            return jnp.concatenate(parts, axis=0)

        q_o[...] = rope(0).astype(BF)
        k = rope(W)
        kT_o[...] = k.astype(BF)
        v = 0.5 * t[2 * W :] + 0.5 * vf_ref[0].astype(F32).T
        vT_o[...] = v.astype(BF)
        for h in range(hl):
            kn_o[h] = k[h * HEAD : (h + 1) * HEAD].T.astype(BF)
            vn_o[h] = v[h * HEAD : (h + 1) * HEAD].T.astype(BF)

    T = jax.ShapeDtypeStruct((W, S), BF)
    N = jax.ShapeDtypeStruct((hl, S, HEAD), BF)
    tb = pl.BlockSpec((W, run), lambda r, b: (0, b[r]))
    nbk = pl.BlockSpec((hl, run, HEAD), lambda r, b: (0, b[r], 0))
    rb = pl.BlockSpec((hh, run), lambda r, b: (0, b[r]))
    return pl.pallas_call(
        kern,
        out_shape=(jax.ShapeDtypeStruct((S, D), BF), T, T, T, N, N),
        grid_spec=pltpu.PrefetchScalarGridSpec(
            num_scalar_prefetch=1,
            grid=(nb,),
            in_specs=[pl.BlockSpec((run, D), lambda r, b: (r, 0)), whole(1, D), whole(3 * W, D), pl.BlockSpec((1, run, W), lambda r, b: (r // per, r % per, 0)), rb, rb],
            out_specs=[pl.BlockSpec((run, D), lambda r, b: (r, 0)), tb, tb, tb, nbk, nbk],
        ),
        compiler_params=params(),
        cost_estimate=cost(6 * S * D * W, 4 * S * D + 12 * S * W),
        name="project_qkv",
    )(blk, x, gain, w, vf, cos, sin)


def load_pieces(pieces, refs, pos_ref, dst, sems):
    copies = []
    for ref, row, rows, col, place, sem in pieces:
        at = pl.multiple_of(pos_ref[place], rows)
        copies.append(
            pltpu.make_async_copy(
                refs[ref].at[pl.ds(row, rows), pl.ds(col, dst.shape[1])], dst.at[pl.ds(at, rows), :], sems.at[sem]
            )
        )
    return copies


def feed_forward(attn3, x, og, gain, pos, arrays, out_pieces, gate_pieces, down_pieces, keep):
    n, rows, W = attn3.shape
    FC = 256
    steps = FF // FC
    nsem = len(out_pieces) + len(gate_pieces) + len(down_pieces)
    na = len(arrays)
    last = pos.shape[0]
    H = D // 2

    def kern(pos_ref, a_ref, x_ref, og_ref, g_ref, *rest):
        refs = rest[:na]
        mixed_o, r_o, near_o, far_o, dy_o, da_o, wr_o = rest[na : na + 7]
        wo, wg, wd, y1, u2, n2, al, acc_m, acc_n, sems = rest[na + 7 :]
        f = pl.program_id(0)

        def sides(ref, place):
            for out, c in ((near_o, pos_ref[last - 2]), (far_o, 1 - pos_ref[last - 2])):
                for e in range(D // 256):
                    out[:, place + e * 128 : place + (e + 1) * 128] = ref[:, pl.ds(pl.multiple_of((2 * e + c) * 128, 128), 128)]

        @pl.when(f == 0)
        def _():
            first = load_pieces(out_pieces, refs, pos_ref, wo, sems)
            second = load_pieces(gate_pieces, refs, pos_ref, wg, sems)
            third = load_pieces(down_pieces, refs, pos_ref, wd, sems)
            for cp in first + second + third:
                cp.start()
            for i in range(n):
                al[:, i * W : (i + 1) * W] = a_ref[i]
            sides(og_ref, 2 * H)
            sides(al, H)
            for cp in first:
                cp.wait()
            y = x_ref[...].astype(F32) + dot(al[...], wo[...], NN)
            y1[...] = y
            inv = lax.rsqrt(jnp.mean(y * y, axis=1, keepdims=True) + EPS)
            xh = y * inv
            u2[...] = xh
            n2[...] = (xh * g_ref[...]).astype(BF)
            sides(n2, 0)
            acc_m[...] = jnp.zeros_like(acc_m)
            acc_n[...] = jnp.zeros_like(acc_n)
            for cp in second + third:
                cp.wait()
            wr_o[...] = wg[pl.ds(pl.multiple_of(pos_ref[last - 1], keep), keep), :]

        c0 = pl.multiple_of(f * FC, FC)
        c1 = pl.multiple_of(FF + f * FC, FC)
        a = n2[...]
        g = dot(a, wg[:, pl.ds(c0, FC)], NN)
        u = dot(a, wg[:, pl.ds(c1, FC)], NN)
        dh = dot(og_ref[...], wd[:, pl.ds(c0, FC)], NN)
        sg = jax.nn.sigmoid(g)
        silu = g * sg
        hid = (silu * u).astype(BF)
        dg = (dh * u * sg * (1.0 + g * (1.0 - sg))).astype(BF)
        du = (dh * silu).astype(BF)
        r_o[:, :FC] = dg
        r_o[:, FC : 2 * FC] = du
        r_o[:, 2 * FC :] = hid
        acc_m[...] += dot(hid, wd[:, pl.ds(c0, FC)], NT)
        acc_n[...] += dot(dg, wg[:, pl.ds(c0, FC)], NT) + dot(du, wg[:, pl.ds(c1, FC)], NT)

        @pl.when(f == steps - 1)
        def _():
            y = y1[...]
            mixed_o[...] = (y + acc_m[...]).astype(BF)
            inv = lax.rsqrt(jnp.mean(y * y, axis=1, keepdims=True) + EPS)
            xh = u2[...]
            t = acc_n[...] * g_ref[...]
            dy = og_ref[...].astype(F32) + inv * (t - xh * jnp.mean(t * xh, axis=1, keepdims=True))
            dy_o[...] = dy
            low = dy.astype(BF)
            near_o[:, 3 * H :] = low
            far_o[:, 3 * H :] = low
            da = dot(low, wo[...], NT).astype(BF)
            for i in range(n):
                da_o[i] = da[:, i * W : (i + 1) * W]

    side = jax.ShapeDtypeStruct((rows, 5 * H), BF)
    return pl.pallas_call(
        kern,
        out_shape=(
            jax.ShapeDtypeStruct((rows, D), BF),
            jax.ShapeDtypeStruct((rows, 3 * FF), BF),
            side,
            side,
            jax.ShapeDtypeStruct((rows, D), F32),
            jax.ShapeDtypeStruct((n, rows, W), BF),
            jax.ShapeDtypeStruct((keep, 2 * FF), BF),
        ),
        grid_spec=pltpu.PrefetchScalarGridSpec(
            num_scalar_prefetch=1,
            grid=(steps,),
            in_specs=[whole(n, rows, W), whole(rows, D), whole(rows, D), whole(1, D)] + [ANY] * na,
            out_specs=[
                whole(rows, D),
                pl.BlockSpec((rows, 3 * FC), lambda f, *_: (0, f)),
                whole(rows, 5 * H),
                whole(rows, 5 * H),
                whole(rows, D),
                whole(n, rows, W),
                whole(keep, 2 * FF),
            ],
            scratch_shapes=[
                pltpu.VMEM((D, D), BF),
                pltpu.VMEM((D, 2 * FF), BF),
                pltpu.VMEM((D, FF), BF),
                pltpu.VMEM((rows, D), F32),
                pltpu.VMEM((rows, D), F32),
                pltpu.VMEM((rows, D), BF),
                pltpu.VMEM((rows, D), BF),
                pltpu.VMEM((rows, D), F32),
                pltpu.VMEM((rows, D), F32),
                pltpu.SemaphoreType.DMA((nsem,)),
            ],
        ),
        compiler_params=params(),
        cost_estimate=cost(4 * rows * D * (2 * D + 6 * FF), 2 * D * (D + 3 * FF) + 2 * rows * (10 * D + 3 * FF)),
        name="feed_forward",
    )(pos, attn3, x, og, gain, *arrays)


def tail(dqkv3, x, dy1, gain, pos, arrays, pieces, keep):
    n, rows, W3 = dqkv3.shape
    W = W3 // 3
    na = len(arrays)
    group = max(1, len(pieces) // 4)

    def kern(pos_ref, d_ref, x_ref, dy_ref, g_ref, *rest):
        refs = rest[:na]
        ig_o, fv_o, wr_o = rest[na : na + 3]
        w, dn, sems = rest[na + 3 :]
        copies = load_pieces(pieces, refs, pos_ref, w, sems)
        for cp in copies:
            cp.start()
        if n > 1:
            d = jnp.concatenate([d_ref[i, :, p * W : (p + 1) * W] for p in range(3) for i in range(n)], axis=1)
        else:
            d = d_ref[0]
        fv_o[...] = d[:, 2 * D :].astype(F32)
        for g in range(len(pieces) // group):
            for cp in copies[g * group : (g + 1) * group]:
                cp.wait()
            size = D // (len(pieces) // group)
            first = pl.multiple_of(pos_ref[pieces[g * group][4]] // size * size, size)
            dn[:, pl.ds(first, size)] = dot(d, w[pl.ds(first, size), :], NT)
        wr_o[...] = w[pl.ds(pl.multiple_of(pos_ref[pos.shape[0] - 1], keep), keep), :]
        xf = x_ref[...].astype(F32)
        inv = lax.rsqrt(jnp.mean(xf * xf, axis=1, keepdims=True) + EPS)
        xh = xf * inv
        t = dn[...] * g_ref[...]
        ig_o[...] = dy_ref[...] + inv * (t - xh * jnp.mean(t * xh, axis=1, keepdims=True))

    o = jax.ShapeDtypeStruct((rows, D), F32)
    return pl.pallas_call(
        kern,
        out_shape=(o, o, jax.ShapeDtypeStruct((keep, 3 * D), BF)),
        grid_spec=pltpu.PrefetchScalarGridSpec(
            num_scalar_prefetch=1,
            grid=(1,),
            in_specs=[whole(n, rows, W3), whole(rows, D), whole(rows, D), whole(1, D)] + [ANY] * na,
            out_specs=[whole(rows, D), whole(rows, D), whole(keep, 3 * D)],
            scratch_shapes=[pltpu.VMEM((D, 3 * D), BF), pltpu.VMEM((rows, D), F32), pltpu.SemaphoreType.DMA((len(pieces),))],
        ),
        compiler_params=params(),
        cost_estimate=cost(6 * rows * D * D, 6 * D * D + rows * D * 20),
        name="input_gradient",
    )(pos, dqkv3, x, dy1, gain, *arrays)


def weight_terms(near, far, r_near, r_far, order, order_down):
    rows = near.shape[0]
    H = D // 2
    FC = 256
    steps = FF // FC
    nb = order.shape[0]
    own = H // nb
    n = 4

    def kern(o_ref, od_ref, na, fa, nd, fd, ra, rb, *rest):
        outs = rest[:n]
        downs, lt0, lt = rest[n:]
        f = pl.program_id(0)

        @pl.when(f == 0)
        def _():
            for i, side in ((0, na), (1, fa)):
                for p in range(3):
                    lt0[p, :, i * rows : (i + 1) * rows] = side[:, p * H : (p + 1) * H].T
            for p in range(3):
                table = od_ref if p == 2 else o_ref
                for b in range(nb):
                    lt[p, b * own : (b + 1) * own, :] = lt0[p, pl.ds(pl.multiple_of(table[b] * own, own), own), :]

        @pl.when(f < steps)
        def _():
            t = dot(lt[0, :, :rows], ra[:, : 2 * FC], NN) + dot(lt[0, :, rows:], rb[:, : 2 * FC], NN)
            d = dot(lt[2, :, :rows], ra[:, 2 * FC :], NN) + dot(lt[2, :, rows:], rb[:, 2 * FC :], NN)
            for e in range(n):
                outs[e][...] = t[e * H // n : (e + 1) * H // n].astype(BF)
                downs[e] = d[e * H // n : (e + 1) * H // n].astype(BF)

        @pl.when(f >= steps)
        def _():
            t = dot(lt[1, :, :rows], nd[...], NN) + dot(lt[1, :, rows:], fd[...], NN)
            for e in range(n):
                outs[e][...] = t[e * H // n : (e + 1) * H // n].astype(BF)

    more = D // (2 * FC)
    dy = pl.BlockSpec((rows, H), lambda f, *_: (0, 3 + jnp.maximum(f - steps, 0)))
    rb = pl.BlockSpec((rows, 3 * FC), lambda f, *_: (0, jnp.minimum(f, steps - 1)))
    ob = pl.BlockSpec((H // n, 2 * FC), lambda f, *_: (0, f))
    db = pl.BlockSpec((n, H // n, FC), lambda f, *_: (0, 0, jnp.minimum(f, steps - 1)))
    outs = pl.pallas_call(
        kern,
        out_shape=tuple([jax.ShapeDtypeStruct((H // n, 2 * FF + D), BF)] * n + [jax.ShapeDtypeStruct((n, H // n, FF), BF)]),
        grid_spec=pltpu.PrefetchScalarGridSpec(
            num_scalar_prefetch=2,
            grid=(steps + more,),
            in_specs=[whole(rows, 3 * H)] * 2 + [dy] * 2 + [rb] * 2,
            out_specs=[ob] * n + [db],
            scratch_shapes=[pltpu.VMEM((3, H, 2 * rows), BF)] * 2,
        ),
        compiler_params=params(),
        cost_estimate=cost(4 * rows * H * (3 * FF + D), 2 * (2 * rows + H) * (3 * FF + D) + 12 * rows * H),
        name="weight_terms",
    )(order, order_down, near, far, near, far, r_near, r_far)
    return outs[:n], outs[n]


def exchange(v):
    return lax.all_to_all(v, CTX, 0, 0, tiled=True)


def swapped(v, axes, size, mask):
    return lax.ppermute(v, axes, [(i, i ^ mask) for i in range(size)])


def gathered(v, axes, size, index):
    parts = [v] + [swapped(v, axes, size, s) for s in range(1, size)]
    return jnp.stack([lax.select_n(index ^ a, *parts) for a in range(size)])


def half_rows(w, core):
    half = w.shape[0] // 2
    return lax.dynamic_slice_in_dim(w, core * half, half, 0)


def body(tokens_in, value_first, out_grad, gain_attn, w_qkv, w_out, gain_mlp, w_gate_up, w_down, cont_lengths, row_token):
    x = tokens_in[0]
    og = out_grad[0]
    rows = x.shape[0]
    nchip = lax.axis_size("chip")
    nctx = lax.axis_size(CTX)
    nz = lax.axis_size("z")
    me = lax.axis_index(CTX)
    chip = lax.axis_index("chip")
    core = lax.axis_index("core")
    z = lax.axis_index("z")
    fast = nctx == 8 and nz == 4
    S = rows * nctx
    W = D // nctx
    run = PROMPT // nctx
    nb = S // run
    nprompt = PROMPT // run
    shard = D // nz
    own = D // (nctx * nz)
    at = (me * nz + z) * own
    keep = own if fast else 16

    x_all = lax.all_gather(x, CTX, axis=0, tiled=True)
    w_own = lax.dynamic_index_in_dim(w_qkv.reshape(shard, 3, nctx, W), me, 2, keepdims=False).reshape(shard, 3 * W)
    gains = jnp.stack([gain_attn, gain_mlp])
    runs = (row_token[0, ::run] // run).astype(BF)
    runs = jnp.pad(runs[None], ((0, 15), (0, W - runs.shape[0])))
    vf = jnp.concatenate([value_first[0].reshape(rows, nctx, W).transpose(1, 0, 2), jnp.broadcast_to(runs, (nctx, 16, W))], axis=1)
    vf = exchange(vf)
    if fast:
        pay = jnp.concatenate([w_own, jnp.pad(gains, ((0, 14), (0, 3 * W - shard)))], axis=0)
        pay = gathered(pay, "z", nz, z)
    else:
        w_own = lax.all_gather(w_own, "z", axis=0, tiled=True).T
        gains = lax.all_gather(gains, "z", axis=1, tiled=True).astype(F32)
        gain_one, gain_two = gains[0:1], gains[1:2]
        blk = vf[:, rows, : nb // nctx].astype(jnp.int32).reshape(nb)

    lengths = cont_lengths[0]
    count = jnp.arange(lengths.shape[0], dtype=jnp.int32)
    starts = PROMPT + jnp.sum(jnp.where(count[:, None] < count[None, :], lengths[:, None], 0), axis=0)
    token = jnp.arange(S, dtype=jnp.int32)
    passed = token[None, :] >= starts[:, None]
    opening = jnp.max(jnp.where(passed, starts[:, None], 0), axis=0).astype(jnp.int32)
    position = jnp.where(opening > 0, PROMPT + token - opening, token)
    freq = BASE ** (-(jnp.arange(HEAD // 2, dtype=F32) * 2.0 / HEAD))
    angles = freq[:, None] * position.astype(F32)[None, :]
    cosT = jnp.cos(angles)
    sinT = jnp.sin(angles)
    block = jnp.arange(nb, dtype=jnp.int32)
    jlo = jnp.where(block < nprompt, block, opening[::run] // run).astype(jnp.int32)
    opening = opening[None, :]

    if fast:
        piece = shard // nctx
        mine = jnp.concatenate([lax.dynamic_slice_in_dim(w, me * piece, piece, 0) for w in (w_out, w_gate_up)], axis=1)
        near = jnp.concatenate([swapped(mine, "z", nz, d) for d in range(1, nz)], axis=0)
        down = half_rows(w_down, core)
        qkv = half_rows(w_qkv, core)
        x_all, near, vf, pay, down, qkv = lax.optimization_barrier((x_all, near, vf, pay, down, qkv))
        w_own = pay[:, :shard].reshape(D, 3 * W).T
        gains = pay[:, shard : shard + 2, :shard].transpose(1, 0, 2).reshape(2, D).astype(F32)
        gain_one, gain_two = gains[0:1], gains[1:2]
        blk = vf[:, rows, : nb // nctx].astype(jnp.int32).reshape(nb)
        planes = [near] + [swapped(near, "chip", nchip, e) for e in range(1, nchip)]
        down = lax.all_gather(down, "z", axis=0, tiled=True)
        pos = [z * shard]
        out_pieces, gate_pieces = [[(i, 0, shard, 0, 0, i)] for i in range(2)]
        sem = 2
        for f in range(2):
            for e in range(nchip):
                for d in range(1, nz):
                    pos.append((z ^ d) * shard + ((chip ^ e) * 2 + (core ^ f)) * piece)
                    ref = 2 + f * nchip + e
                    out_pieces.append((ref, (d - 1) * piece, piece, 0, len(pos) - 1, sem))
                    gate_pieces.append((ref, (d - 1) * piece, piece, D, len(pos) - 1, sem + 1))
                    sem += 2
        down_pieces = []
        half = shard // 2
        for k in range(nz):
            for f in range(2):
                pos.append(k * shard + (core ^ f) * half)
                down_pieces.append((2 + 2 * nchip + f, k * half, half, 0, len(pos) - 1, sem))
                sem += 1
        qkv_pieces = []
        for d in range(nz):
            for f in range(2):
                pos.append((z ^ d) * shard + (core ^ f) * half)
                qkv_pieces.append((f, d * half, half, 0, len(pos) - 1, len(qkv_pieces)))
        pos = jnp.stack(pos + [core, at]).astype(jnp.int32)
    else:
        arrays = [lax.all_gather(w, "z", axis=0, tiled=True) for w in (w_out, w_gate_up, w_down)]
        qkv_arrays = [lax.all_gather(w_qkv, "z", axis=0, tiled=True)]
        pos = jnp.zeros((3,), jnp.int32)
        out_pieces, gate_pieces, down_pieces = [[(i, 0, D, 0, 0, i)] for i in range(3)]
        qkv_pieces = [(0, 0, D, 0, 0, 0)]

    spos = jnp.sum(jnp.where(blk[None, :] == block[:, None], block[None, :], 0), axis=1).astype(jnp.int32)
    normed_all, qT, kT, vT, kn, vn = project(x_all, gain_one, w_own, vf, cosT, sinT, blk, run=run)
    attn_all, attnT, lse = attn_fwd(qT, kn, vT, opening, jlo, spos, run=run, nprompt=nprompt, fsz=(8, 4, 2, 1), msz=(4, 2, 1))
    if fast:
        attn_all, qkv, down, *planes = lax.optimization_barrier((attn_all, qkv, down, *planes))
        arrays = [w_out, w_gate_up] + planes + [swapped(p, "core", 2, 1) for p in planes] + [down, swapped(down, "core", 2, 1)]
        qkv = [qkv] + [swapped(qkv, "z", nz, d) for d in range(1, nz)]
    attn3 = exchange(attn_all.reshape(nctx, rows, W))
    if not fast:
        attn3 = attn3.transpose(1, 0, 2).reshape(1, rows, D)
    mixed_out, right, side_near, side_far, dy1, dattn3, gate_rows = feed_forward(
        attn3, x, og, gain_two, pos, arrays, out_pieces, gate_pieces, down_pieces, keep
    )
    if not fast:
        dattn3 = dattn3.reshape(rows, nctx, W).transpose(1, 0, 2)
    dattn_all = exchange(dattn3).reshape(S, W)

    def columns(v, chunks):
        return v[:, : 2 * FF].reshape(v.shape[0], chunks, 2, FF // chunks).transpose(0, 2, 1, 3).reshape(v.shape[0], 2 * FF)

    if fast:
        come_right = swapped(right, "core", 2, 1)
        come_side = swapped(side_far, "core", 2, 1)
        order = jnp.stack([(chip ^ e) * nz + (z ^ d) for e in range(nchip) for d in range(nz)]).astype(jnp.int32)
        order_down = jnp.stack([(chip ^ e) * nz + k for k in range(nz) for e in range(nchip)]).astype(jnp.int32)
        terms, downs = weight_terms(side_near, come_side, right, come_right, order, order_down)
        dattn_all, terms, downs, *qkv = lax.optimization_barrier((dattn_all, terms, downs, *qkv))
        qkv = jnp.concatenate(qkv, axis=0)
        qkv_arrays = [qkv, swapped(qkv, "core", 2, 1)]
        terms = [terms[0]] + [swapped(terms[e], "chip", nchip, e) for e in range(1, nchip)]
        downs = lax.all_to_all(downs, "z", 0, 0, tiled=True)
    else:
        chunks = right.reshape(rows, FF // 256, 3, 256)
        dgu = chunks[:, :, :2].transpose(0, 2, 1, 3).reshape(rows, 2 * FF)
        hidden = chunks[:, :, 2].reshape(rows, FF)
        dy1_low = side_near[:, 3 * D // 2 :]
        attn_low = attn3[0]
        normed_two = jnp.stack([side_near[:, : D // 2].reshape(rows, D // 256, 128), side_far[:, : D // 2].reshape(rows, D // 256, 128)], axis=2).reshape(rows, D)
        terms = jnp.concatenate([dot(attn_low, dy1_low, TN), dot(normed_two, dgu, TN), dot(og, hidden, TN)], axis=1).astype(BF)
        share = lax.psum_scatter(terms, CTX, scatter_dimension=0, tiled=True)
        share = lax.psum_scatter(share, "z", scatter_dimension=0, tiled=True).astype(F32)
        out_share, gate_share, down_share = share[:, :D], share[:, D : D + 2 * FF], share[:, D + 2 * FF :]

    dqkv_own = attn_bwd(
        qT, kn, kT, vn, dattn_all, attnT, lse, opening, jlo, spos, cosT, sinT, run=run, nprompt=nprompt, fsz=(4, 2, 1), msz=(2, 1)
    )
    if fast:
        dqkv_own, terms, downs = lax.optimization_barrier((dqkv_own, terms, downs))

        def block_sum(parts, i):
            return sum(v[i * own : (i + 1) * own].astype(F32) for v in parts)

        share = block_sum(terms, 0) + sum(swapped(block_sum(terms, d).astype(BF), "z", nz, d).astype(F32) for d in range(1, nz))
        downs = [downs[k] for k in range(nz)]
        down_share = block_sum(downs, 0) + sum(
            swapped(block_sum(downs, e).astype(BF), "chip", nchip, e).astype(F32) for e in range(1, nchip)
        )
        gate_share = columns(share, FF // 256)
        out_share = share[:, 2 * FF :]
    dqkv3 = exchange(dqkv_own.reshape(nctx, rows, 3 * W))
    if not fast:
        dqkv3 = dqkv3.reshape(nctx, rows, 3, W).transpose(1, 2, 0, 3).reshape(1, rows, 3 * D)

    term = dot(normed_all, dqkv_own, TN).astype(BF).reshape(nctx, nz, own, 3 * W)
    if fast:

        def slot(d):
            return lax.dynamic_index_in_dim(term, z ^ d, 1, keepdims=False)

        term = slot(0).astype(F32) + sum(swapped(slot(d), "z", nz, d).astype(F32) for d in range(1, nz))
        term = term.astype(BF)
    else:
        term = lax.psum_scatter(term.transpose(1, 0, 2, 3), "z", scatter_dimension=0, tiled=True)[0]
    dqkv3, term = lax.optimization_barrier((dqkv3, term))
    qkv_share = exchange(term).reshape(nctx, own, 3, W).transpose(1, 2, 0, 3).reshape(own, 3 * D).astype(F32)

    input_grad, first_value_grad, qkv_rows = tail(dqkv3, x, dy1, gain_one, pos, qkv_arrays, qkv_pieces, keep)

    gain_own = lax.dynamic_slice_in_dim(gains, at, own, 1)
    if not fast:
        qkv_rows = lax.dynamic_slice_in_dim(qkv_arrays[0], at, own, 0)
        gate_rows = lax.dynamic_slice_in_dim(arrays[1], at, own, 0)
    gain_one_share = jnp.sum(qkv_rows.astype(F32) * qkv_share, axis=1) / gain_own[0]
    gain_two_share = jnp.sum(gate_rows.astype(F32) * gate_share, axis=1) / gain_own[1]
    return (
        mixed_out[None],
        input_grad[None],
        first_value_grad[None],
        gain_one_share,
        qkv_share,
        out_share,
        gain_two_share,
        gate_share,
        down_share,
    )


def solution(mesh):
    ctx, fsdp = mesh.devices.shape
    split = Mesh(mesh.devices.reshape(ctx // 2, 2, fsdp), ("chip", "core", "z"))
    rows3 = P("z", CTX, None)
    weight = P("z", None)
    every = ("chip", "core", "z")
    return jax.shard_map(
        body,
        mesh=split,
        in_specs=(rows3, rows3, rows3, P("z"), weight, weight, P("z"), weight, weight, weight, P("z", CTX)),
        out_specs=(rows3, rows3, rows3, P(every), P(every, None), P(every, None), P(every), P(every, None), P(every, None)),
        check_vma=False,
    )
```

```python
import jax
import jax.numpy as jnp
from jax import lax
from jax.experimental import pallas as pl
from jax.experimental.pallas import tpu as pltpu
from jax.sharding import Mesh, PartitionSpec as P

D = 1024
HEADS = 16
HEAD = 64
FF = 2816
PROMPT = 2048
EPS = 1e-05
BASE = 10000.0
LOG2E = 1.4426950408889634
NEG = -1e30
C2 = 0.125 * LOG2E
CTX = ("chip", "core")
BF = jnp.bfloat16
F32 = jnp.float32


def dot(a, b, dims):
    return lax.dot_general(a, b, (dims, ((), ())), preferred_element_type=F32)


NN = ((1,), (0,))
NT = ((1,), (1,))
TN = ((0,), (0,))


def chunked(first, stop, sizes, fn, c):
    for n in sizes:
        count = (stop - first) // n
        c = lax.fori_loop(0, count, lambda t, c, n=n, first=first: fn(first + t * n, c, n), c)
        first = first + count * n
    return c


def visible(i, j, rows, run, lo):
    key = j * run + lax.broadcasted_iota(jnp.int32, (rows, run), 0)
    query = i * run + lax.broadcasted_iota(jnp.int32, (rows, run), 1)
    return (key <= query) & (key >= lo)


def attn_fwd(qT, kn, vT, lo, jlo, opos, *, run, nprompt, base, count):
    W, S = qT.shape
    hl = W // HEAD
    keys = S if base + count > nprompt else nprompt * run
    full_sizes, own_sizes = (8, 4, 2, 1), (4, 2, 1)

    def kern(jlo_ref, opos_ref, q_ref, k_ref, v_ref, lo_ref, o_ref, of_ref, lse_ref, s_scr):
        i = pl.program_id(0) + base
        qs = [q_ref[h * HEAD : (h + 1) * HEAD, :] for h in range(hl)]
        full = jnp.minimum(i, nprompt)
        own = jlo_ref[i]
        total = full + (i + 1 - own)

        def fold(f, s):
            return f(s.reshape(s.shape[0] // 8, 8, run), axis=0)

        def score(t, tops, n, shift, masked):
            tops = list(tops)
            for u in range(n):
                j = t + u + shift
                at = pl.multiple_of(j * run, run)
                row = pl.multiple_of((t + u) * run, run)
                if masked:
                    vis = visible(i, j, run, run, lo_ref[...])
                for h in range(hl):
                    s = dot(k_ref[h, pl.ds(at, run), :], qs[h], NN)
                    if masked:
                        s = jnp.where(vis, s, NEG)
                    s_scr[h, pl.ds(row, run), :] = s
                    tops[h] = jnp.maximum(tops[h], fold(jnp.max, s))
            return tuple(tops)

        tops = tuple(jnp.full((8, run), NEG, F32) for _ in range(hl))
        tops = chunked(0, full, full_sizes, lambda t, c, n: score(t, c, n, 0, False), tops)
        tops = chunked(full, total, own_sizes, lambda t, c, n: score(t, c, n, own - full, True), tops)
        m = [jnp.max(tops[h], axis=0, keepdims=True) * C2 for h in range(hl)]

        def weigh(t, c, n, shift):
            c = list(c)
            for u in range(n):
                at = pl.multiple_of((t + u + shift) * run, run)
                row = pl.multiple_of((t + u) * run, run)
                for h in range(hl):
                    l, acc = c[h]
                    p = jnp.exp2(s_scr[h, pl.ds(row, run), :] * C2 - m[h])
                    l = l + fold(jnp.sum, p)
                    acc = acc + dot(v_ref[h * HEAD : (h + 1) * HEAD, pl.ds(at, run)], p.astype(BF), NN)
                    c[h] = (l, acc)
            return tuple(c)

        c = tuple((jnp.zeros((8, run), F32), jnp.zeros((HEAD, run), F32)) for _ in range(hl))
        c = chunked(0, full, full_sizes, lambda t, c, n: weigh(t, c, n, 0), c)
        c = chunked(full, total, own_sizes, lambda t, c, n: weigh(t, c, n, own - full), c)
        outs = []
        for h in range(hl):
            l8, acc = c[h]
            l = jnp.sum(l8, axis=0, keepdims=True)
            o = acc / l
            of_ref[h * HEAD : (h + 1) * HEAD, :] = o
            lse_ref[h, :, :] = m[h] + jnp.log2(l)
            outs.append(o)
        o = jnp.concatenate(outs, axis=0) if hl > 1 else outs[0]
        o_ref[...] = o.T.astype(BF)

    rows = count * run
    return pl.pallas_call(
        kern,
        out_shape=(jax.ShapeDtypeStruct((rows, W), BF), jax.ShapeDtypeStruct((W, rows), F32), jax.ShapeDtypeStruct((hl, 1, rows), F32)),
        grid_spec=pltpu.PrefetchScalarGridSpec(
            num_scalar_prefetch=2,
            grid=(count,),
            in_specs=[
                pl.BlockSpec((W, run), lambda i, *_: (0, i + base)),
                pl.BlockSpec((hl, keys, HEAD), lambda i, *_: (0, 0, 0)),
                pl.BlockSpec((W, keys), lambda i, *_: (0, 0)),
                pl.BlockSpec((1, run), lambda i, *_: (0, i + base)),
            ],
            out_specs=[
                pl.BlockSpec((run, W), lambda i, jl, op: (op[i + base], 0)),
                pl.BlockSpec((W, run), lambda i, *_: (0, i)),
                pl.BlockSpec((hl, 1, run), lambda i, *_: (0, 0, i)),
            ],
            scratch_shapes=[pltpu.VMEM((hl, keys, run), F32)],
        ),
        compiler_params=params(),
        cost_estimate=cost(20 * rows * keys * W // 2, 12 * S * W, rows * keys // 2),
        name="attention_forward",
    )(jlo, opos, qT, kn, vT, lo)


def attn_bwd(qT, kn, kT, vn, don, of, lse, lo, jlo, spos, opos, cosT, sinT, sums, *, run, nprompt, base, count):
    W, S = qT.shape
    hl = W // HEAD
    hh = HEAD // 2
    keys = S if base + count > nprompt else nprompt * run
    later = base > 0
    P_ = nprompt * run
    full_sizes, own_sizes = (4, 2, 1), (2, 1)

    def unrotate(g, cos, sin):
        parts = []
        for h in range(hl):
            a = g[h * HEAD : h * HEAD + hh]
            b = g[h * HEAD + hh : (h + 1) * HEAD]
            parts += [a * cos + b * sin, b * cos - a * sin]
        return jnp.concatenate(parts, axis=0)

    def kern(jlo_ref, spos_ref, opos_ref, q_ref, k_ref, kT_ref, v_ref, do_ref, of_ref, lse_ref, lo_ref, cos_ref, sin_ref, *rest):
        if sums is not None:
            sk_ref, sv_ref = rest[:2]
            rest = rest[2:]
        if later:
            g_ref, ok_ref, ov_ref, dkT, dvT = rest
        else:
            g_ref, dkT, dvT = rest
        i = pl.program_id(0) + base

        @pl.when(pl.program_id(0) == 0)
        def _():
            if sums is not None:
                dkT[...] = sk_ref[...]
                dvT[...] = sv_ref[...]
            else:
                dkT[...] = jnp.zeros_like(dkT)
                dvT[...] = jnp.zeros_like(dvT)

        doT = do_ref[...].T
        dof = doT.astype(F32)
        qs = [q_ref[h * HEAD : (h + 1) * HEAD, :] for h in range(hl)]
        dos = [doT[h * HEAD : (h + 1) * HEAD, :] for h in range(hl)]
        delta = [
            jnp.sum(dof[h * HEAD : (h + 1) * HEAD] * of_ref[h * HEAD : (h + 1) * HEAD, :], axis=0, keepdims=True) for h in range(hl)
        ]
        ls = [lse_ref[h, :, :] for h in range(hl)]

        def tile(j, carry, n, masked):
            kb = n * run
            at = pl.multiple_of(j * run, run)
            if masked:
                vis = visible(i, j, kb, run, lo_ref[...])
            out = []
            for h in range(hl):
                hs = slice(h * HEAD, (h + 1) * HEAD)
                s = dot(k_ref[h, pl.ds(at, kb), :], qs[h], NN)
                p = jnp.exp2(s * C2 - ls[h])
                if masked:
                    p = jnp.where(vis, p, 0.0)
                dp = dot(v_ref[h, pl.ds(at, kb), :], dos[h], NN)
                ds = (p * (dp - delta[h])).astype(BF)
                dvT[hs, pl.ds(at, kb)] += dot(dos[h], p.astype(BF), NT)
                dkT[hs, pl.ds(at, kb)] += dot(qs[h], ds, NT)
                out.append(carry[h] + dot(kT_ref[hs, pl.ds(at, kb)], ds, NN))
            return tuple(out)

        c = tuple(jnp.zeros((HEAD, run), F32) for _ in range(hl))
        c = chunked(0, jnp.minimum(i, nprompt), full_sizes, lambda j, c, n: tile(j, c, n, False), c)
        c = chunked(jlo_ref[i], i + 1, own_sizes, lambda j, c, n: tile(j, c, n, True), c)
        dq = (jnp.concatenate(c, axis=0) if hl > 1 else c[0]) * 0.125

        def turned(g, b):
            at = pl.multiple_of(b * run, run)
            return unrotate(g, cos_ref[:, pl.ds(at, run)], sin_ref[:, pl.ds(at, run)]).T.astype(BF)

        row = pl.multiple_of(opos_ref[i] * run, run)
        g_ref[pl.ds(row, run), :W] = turned(dq, i)

        @pl.when(pl.program_id(0) == count - 1)
        def _():
            def finish(b, _):
                at = pl.multiple_of(b * run, run)
                row = pl.multiple_of(opos_ref[b] * run, run)
                g_ref[pl.ds(row, run), W : 2 * W] = turned(dkT[:, pl.ds(at, run)] * 0.125, b)
                g_ref[pl.ds(row, run), 2 * W :] = (dvT[:, pl.ds(at, run)] * 0.5).T.astype(BF)
                return 0

            lax.fori_loop(base, base + count, finish, 0)
            if later:
                ok_ref[...] = dkT[:, :P_]
                ov_ref[...] = dvT[:, :P_]

    full = lambda *s: pl.BlockSpec(s, lambda i, *_: (0,) * len(s))
    rows = count * run
    sum_shape = jax.ShapeDtypeStruct((W, P_), F32)
    return pl.pallas_call(
        kern,
        out_shape=(jax.ShapeDtypeStruct((rows, 3 * W), BF),) + ((sum_shape, sum_shape) if later else ()),
        grid_spec=pltpu.PrefetchScalarGridSpec(
            num_scalar_prefetch=3,
            grid=(count,),
            in_specs=[
                pl.BlockSpec((W, run), lambda i, *_: (0, i + base)),
                full(hl, keys, HEAD),
                full(W, keys),
                full(hl, keys, HEAD),
                pl.BlockSpec((run, W), lambda i, jl, sp, op: (sp[i + base], 0)),
                pl.BlockSpec((W, run), lambda i, *_: (0, i)),
                pl.BlockSpec((hl, 1, run), lambda i, *_: (0, 0, i)),
                pl.BlockSpec((1, run), lambda i, *_: (0, i + base)),
                full(hh, keys),
                full(hh, keys),
            ]
            + ([full(W, P_)] * 2 if sums is not None else []),
            out_specs=[full(rows, 3 * W)] + ([full(W, P_)] * 2 if later else []),
            scratch_shapes=[pltpu.VMEM((W, keys), F32)] * 2,
        ),
        compiler_params=params(),
        cost_estimate=cost(32 * rows * keys * W // 2, 24 * S * W, rows * keys // 2),
        name="attention_backward",
    )(jlo, spos, opos, qT, kn, kT, vn, don, of, lse, lo, cosT, sinT, *(sums or ()))


def cost(flops, nbytes, trans=0):
    return pl.CostEstimate(flops=int(flops), bytes_accessed=int(nbytes), transcendentals=int(trans))


def whole(*shape):
    return pl.BlockSpec(shape, lambda *_: (0,) * len(shape))


ANY = pl.BlockSpec(memory_space=pl.ANY)


def params():
    return pltpu.CompilerParams(vmem_limit_bytes=56 << 20)


def project(x, gain, w, vf, cos, sin, blk, *, run):
    S = x.shape[0]
    W = vf.shape[2]
    hl = W // HEAD
    nb = S // run
    per = nb // vf.shape[0]
    hh = HEAD // 2

    def kern(blk_ref, x_ref, g_ref, w_ref, vf_ref, c_ref, s_ref, n_o, q_o, kT_o, vT_o, kn_o, vn_o):
        xf = x_ref[...].astype(F32)
        inv = lax.rsqrt(jnp.mean(xf * xf, axis=1, keepdims=True) + EPS)
        n1 = (xf * inv * g_ref[...]).astype(BF)
        n_o[...] = n1
        t = dot(w_ref[...], n1, NT)
        c = c_ref[...]
        s = s_ref[...]

        def rope(base):
            parts = []
            for h in range(hl):
                a = t[base + h * HEAD : base + h * HEAD + hh]
                b = t[base + h * HEAD + hh : base + (h + 1) * HEAD]
                parts += [a * c - b * s, b * c + a * s]
            return jnp.concatenate(parts, axis=0)

        q_o[...] = rope(0).astype(BF)
        k = rope(W)
        kT_o[...] = k.astype(BF)
        v = 0.5 * t[2 * W :] + 0.5 * vf_ref[0].astype(F32).T
        vT_o[...] = v.astype(BF)
        for h in range(hl):
            kn_o[h] = k[h * HEAD : (h + 1) * HEAD].T.astype(BF)
            vn_o[h] = v[h * HEAD : (h + 1) * HEAD].T.astype(BF)

    T = jax.ShapeDtypeStruct((W, S), BF)
    N = jax.ShapeDtypeStruct((hl, S, HEAD), BF)
    tb = pl.BlockSpec((W, run), lambda r, b: (0, b[r]))
    nbk = pl.BlockSpec((hl, run, HEAD), lambda r, b: (0, b[r], 0))
    rb = pl.BlockSpec((hh, run), lambda r, b: (0, b[r]))
    return pl.pallas_call(
        kern,
        out_shape=(jax.ShapeDtypeStruct((S, D), BF), T, T, T, N, N),
        grid_spec=pltpu.PrefetchScalarGridSpec(
            num_scalar_prefetch=1,
            grid=(nb,),
            in_specs=[pl.BlockSpec((run, D), lambda r, b: (r, 0)), whole(1, D), whole(3 * W, D), pl.BlockSpec((1, run, W), lambda r, b: (r // per, r % per, 0)), rb, rb],
            out_specs=[pl.BlockSpec((run, D), lambda r, b: (r, 0)), tb, tb, tb, nbk, nbk],
        ),
        compiler_params=params(),
        cost_estimate=cost(6 * S * D * W, 4 * S * D + 12 * S * W),
        name="project_qkv",
    )(blk, x, gain, w, vf, cos, sin)


def load_pieces(pieces, refs, pos_ref, dst, sems):
    copies = []
    for ref, row, rows, col, place, sem in pieces:
        at = pl.multiple_of(pos_ref[place], rows)
        copies.append(
            pltpu.make_async_copy(
                refs[ref].at[pl.ds(row, rows), pl.ds(col, dst.shape[1])], dst.at[pl.ds(at, rows), :], sems.at[sem]
            )
        )
    return copies


CUT = 1536
HALF = D // 2


def column_pieces(pieces, first, width):
    return [(ref, row, size, col + first, place, sem) for ref, row, size, col, place, sem in pieces]


def feed_forward(start, carried, attn3, x, og, gain, pos, arrays, out_pieces, gate_pieces, down_pieces, keep):
    n, rows, W = attn3.shape
    lo, hi = (0, CUT) if start else (CUT, FF)
    width = hi - lo
    FC = width // 2
    nsem = len(out_pieces) + 2 * len(gate_pieces) + len(down_pieces)
    na = len(arrays)
    last = pos.shape[0]
    ncarry = len(carried)

    def kern(pos_ref, a_ref, x_ref, og_ref, g_ref, *rest):
        refs = rest[:na]
        rest = rest[na:]
        cin, rest = rest[:ncarry], rest[ncarry:]
        if start:
            r_o, near_o, far_o, wr_o, y_o, n2_o, m_o, acc_o = rest[:8]
            wo, wg, wu, wd, al, sems = rest[8:]
        else:
            mixed_o, r_o, low_o, dy_o, da_o, wr_o = rest[:6]
            wo, wg, wu, wd, acc_m, acc_n, sems = rest[6:]
        f = pl.program_id(0)

        def sides(ref, place):
            for out, c in ((near_o, pos_ref[last - 2]), (far_o, 1 - pos_ref[last - 2])):
                for e in range(D // 256):
                    out[:, place + e * 128 : place + (e + 1) * 128] = ref[:, pl.ds(pl.multiple_of((2 * e + c) * 128, 128), 128)]

        @pl.when(f == 0)
        def _():
            ng = len(gate_pieces)
            first = load_pieces(out_pieces, refs, pos_ref, wo, sems)
            second = load_pieces(column_pieces(gate_pieces, lo, 0), refs, pos_ref, wg, sems)
            second += load_pieces([(r, a, b, c + FF + lo, p, s + nsem - ng) for r, a, b, c, p, s in renumber(gate_pieces)], refs, pos_ref, wu, sems)
            third = load_pieces(column_pieces(down_pieces, lo, 0), refs, pos_ref, wd, sems)
            for cp in (first + second + third) if start else (second + third + first):
                cp.start()
            if start:
                for i in range(n):
                    al[:, i * W : (i + 1) * W] = a_ref[i]
                sides(og_ref, 2 * HALF)
                sides(al, HALF)
                for cp in first:
                    cp.wait()
                y = x_ref[...].astype(F32) + dot(al[...], wo[...], NN)
                y_o[...] = y
                inv = lax.rsqrt(jnp.mean(y * y, axis=1, keepdims=True) + EPS)
                n2_o[...] = (y * inv * g_ref[...]).astype(BF)
                sides(n2_o, 0)
                m_o[...] = y
                acc_o[...] = jnp.zeros_like(acc_o)
            else:
                acc_m[...] = cin[2][...]
                acc_n[...] = cin[3][...]
            for cp in second + third:
                cp.wait()
            if not start:
                for cp in first:
                    cp.wait()

        n2 = n2_o if start else cin[1]
        am = m_o if start else acc_m
        an = acc_o if start else acc_n
        c0 = pl.multiple_of(f * FC, 128)
        a = n2[...]
        g = dot(a, wg[:, pl.ds(c0, FC)], NN)
        u = dot(a, wu[:, pl.ds(c0, FC)], NN)
        dh = dot(og_ref[...], wd[:, pl.ds(c0, FC)], NN)
        sg = jax.nn.sigmoid(g)
        silu = g * sg
        hid = (silu * u).astype(BF)
        dg = (dh * u * sg * (1.0 + g * (1.0 - sg))).astype(BF)
        du = (dh * silu).astype(BF)
        r_o[:, :FC] = dg
        r_o[:, FC : 2 * FC] = du
        r_o[:, 2 * FC :] = hid
        am[...] += dot(hid, wd[:, pl.ds(c0, FC)], NT)
        an[...] += dot(dg, wg[:, pl.ds(c0, FC)], NT) + dot(du, wu[:, pl.ds(c0, FC)], NT)

        @pl.when(f == 1)
        def _():
            at = pl.multiple_of(pos_ref[last - 1], keep)
            wr_o[:, :width] = wg[pl.ds(at, keep), :]
            wr_o[:, width:] = wu[pl.ds(at, keep), :]
            if not start:
                mixed_o[...] = am[...].astype(BF)
                y = cin[0][...]
                inv = lax.rsqrt(jnp.mean(y * y, axis=1, keepdims=True) + EPS)
                xh = y * inv
                t = an[...] * g_ref[...]
                dy = og_ref[...].astype(F32) + inv * (t - xh * jnp.mean(t * xh, axis=1, keepdims=True))
                dy_o[...] = dy
                low = dy.astype(BF)
                low_o[...] = low
                da = dot(low, wo[...], NT).astype(BF)
                for i in range(n):
                    da_o[i] = da[:, i * W : (i + 1) * W]

    wide = jax.ShapeDtypeStruct((rows, D), F32)
    side = jax.ShapeDtypeStruct((rows, 3 * HALF), BF)
    low = jax.ShapeDtypeStruct((rows, D), BF)
    right = jax.ShapeDtypeStruct((rows, 3 * width), BF)
    own_rows = jax.ShapeDtypeStruct((keep, 2 * width), BF)
    rspec = pl.BlockSpec((rows, 3 * FC), lambda f, *_: (0, f))
    full = whole(rows, D)
    if start:
        outs = (right, side, side, own_rows, wide, low, wide, wide)
        specs = [rspec, whole(rows, 3 * HALF), whole(rows, 3 * HALF), whole(keep, 2 * width), full, full, full, full]
        extra = [pltpu.VMEM((rows, D), BF)]
    else:
        outs = (low, right, low, wide, jax.ShapeDtypeStruct((n, rows, W), BF), own_rows)
        specs = [full, rspec, full, full, whole(n, rows, W), whole(keep, 2 * width)]
        extra = [pltpu.VMEM((rows, D), F32)] * 2
    return pl.pallas_call(
        kern,
        out_shape=outs,
        grid_spec=pltpu.PrefetchScalarGridSpec(
            num_scalar_prefetch=1,
            grid=(2,),
            in_specs=[whole(n, rows, W), full, full, whole(1, D)] + [ANY] * na + [full] * ncarry,
            out_specs=specs,
            scratch_shapes=[
                pltpu.VMEM((D, D), BF),
                pltpu.VMEM((D, width), BF),
                pltpu.VMEM((D, width), BF),
                pltpu.VMEM((D, width), BF),
                *extra,
                pltpu.SemaphoreType.DMA((nsem,)),
            ],
        ),
        compiler_params=params(),
        cost_estimate=cost(4 * rows * D * (D + 6 * width), 2 * D * (D + 3 * width) + 2 * rows * (14 * D + 3 * width)),
        name="feed_forward_start" if start else "feed_forward_end",
    )(pos, attn3, x, og, gain, *arrays, *carried)


def renumber(pieces):
    return [(r, a, b, c, p, i) for i, (r, a, b, c, p, _) in enumerate(pieces)]


def tail(dqkv3, x, dy1, gain, pos, arrays, pieces, keep):
    n, rows, W3 = dqkv3.shape
    W = W3 // 3
    na = len(arrays)
    group = max(1, len(pieces) // 4)

    def kern(pos_ref, d_ref, x_ref, dy_ref, g_ref, *rest):
        refs = rest[:na]
        ig_o, fv_o, wr_o = rest[na : na + 3]
        w, dn, sems = rest[na + 3 :]
        copies = load_pieces(pieces, refs, pos_ref, w, sems)
        for cp in copies:
            cp.start()
        if n > 1:
            d = jnp.concatenate([d_ref[i, :, p * W : (p + 1) * W] for p in range(3) for i in range(n)], axis=1)
        else:
            d = d_ref[0]
        fv_o[...] = d[:, 2 * D :].astype(F32)
        for g in range(len(pieces) // group):
            for cp in copies[g * group : (g + 1) * group]:
                cp.wait()
            size = D // (len(pieces) // group)
            first = pl.multiple_of(pos_ref[pieces[g * group][4]] // size * size, size)
            dn[:, pl.ds(first, size)] = dot(d, w[pl.ds(first, size), :], NT)
        wr_o[...] = w[pl.ds(pl.multiple_of(pos_ref[pos.shape[0] - 1], keep), keep), :]
        xf = x_ref[...].astype(F32)
        inv = lax.rsqrt(jnp.mean(xf * xf, axis=1, keepdims=True) + EPS)
        xh = xf * inv
        t = dn[...] * g_ref[...]
        ig_o[...] = dy_ref[...] + inv * (t - xh * jnp.mean(t * xh, axis=1, keepdims=True))

    o = jax.ShapeDtypeStruct((rows, D), F32)
    return pl.pallas_call(
        kern,
        out_shape=(o, o, jax.ShapeDtypeStruct((keep, 3 * D), BF)),
        grid_spec=pltpu.PrefetchScalarGridSpec(
            num_scalar_prefetch=1,
            grid=(1,),
            in_specs=[whole(n, rows, W3), whole(rows, D), whole(rows, D), whole(1, D)] + [ANY] * na,
            out_specs=[whole(rows, D), whole(rows, D), whole(keep, 3 * D)],
            scratch_shapes=[pltpu.VMEM((D, 3 * D), BF), pltpu.VMEM((rows, D), F32), pltpu.SemaphoreType.DMA((len(pieces),))],
        ),
        compiler_params=params(),
        cost_estimate=cost(6 * rows * D * D, 6 * D * D + rows * D * 20),
        name="input_gradient",
    )(pos, dqkv3, x, dy1, gain, *arrays)


def weight_terms(near, far, r_near, r_far, orders, low, low_far):
    rows = near.shape[0]
    width = r_near.shape[1] // 3
    FC = width // 2
    nb = orders.shape[1]
    own = HALF // nb
    n = 4
    more = low is not None
    cols = 2 * width + (D if more else 0)

    def kern(o_ref, na, fa, ra, rb, *rest):
        if more:
            nd, fd = rest[:2]
            rest = rest[2:]
        t_o, d_o, lt0, lt = rest
        f = pl.program_id(0)

        @pl.when(f == 0)
        def _():
            for i, side in ((0, na), (1, fa)):
                for p in range(3):
                    lt0[p, :, i * rows : (i + 1) * rows] = side[:, p * HALF : (p + 1) * HALF].T
            for p in range(3):
                for b in range(nb):
                    at = o_ref[1 if p == 2 else 0, b]
                    lt[p, b * own : (b + 1) * own, :] = lt0[p, pl.ds(pl.multiple_of(at * own, own), own), :]

        def put(p, a, b, out, place, size):
            t = dot(lt[p, :, :rows], a, NN) + dot(lt[p, :, rows:], b, NN)
            for e in range(n):
                out[e, :, pl.ds(place, size)] = t[e * HALF // n : (e + 1) * HALF // n].astype(BF)

        put(0, ra[:, : 2 * FC], rb[:, : 2 * FC], t_o, pl.multiple_of(2 * FC * f, 128), 2 * FC)
        put(2, ra[:, 2 * FC :], rb[:, 2 * FC :], d_o, pl.multiple_of(FC * f, 128), FC)
        if more:

            @pl.when(f == 1)
            def _():
                put(1, nd[...], fd[...], t_o, 2 * width, D)

    rb = pl.BlockSpec((rows, 3 * FC), lambda f, *_: (0, f))
    return pl.pallas_call(
        kern,
        out_shape=(jax.ShapeDtypeStruct((n, HALF // n, cols), BF), jax.ShapeDtypeStruct((n, HALF // n, width), BF)),
        grid_spec=pltpu.PrefetchScalarGridSpec(
            num_scalar_prefetch=1,
            grid=(2,),
            in_specs=[whole(rows, 3 * HALF)] * 2 + [rb] * 2 + ([whole(rows, D)] * 2 if more else []),
            out_specs=[whole(n, HALF // n, cols), whole(n, HALF // n, width)],
            scratch_shapes=[pltpu.VMEM((3, HALF, 2 * rows), BF)] * 2,
        ),
        compiler_params=params(),
        cost_estimate=cost(4 * rows * HALF * (cols + width), 2 * (2 * rows + HALF) * (cols + width) + 12 * rows * HALF),
        name="weight_terms",
    )(orders, near, far, r_near, r_far, *((low, low_far) if more else ()))


def exchange(v):
    return lax.all_to_all(v, CTX, 0, 0, tiled=True)


def swapped(v, axes, size, mask):
    return lax.ppermute(v, axes, [(i, i ^ mask) for i in range(size)])


def gathered(v, axes, size, index):
    parts = [v] + [swapped(v, axes, size, s) for s in range(1, size)]
    return jnp.stack([lax.select_n(index ^ a, *parts) for a in range(size)])


def half_rows(w, core):
    half = w.shape[0] // 2
    return lax.dynamic_slice_in_dim(w, core * half, half, 0)


def body(tokens_in, value_first, out_grad, gain_attn, w_qkv, w_out, gain_mlp, w_gate_up, w_down, cont_lengths, row_token):
    x = tokens_in[0]
    og = out_grad[0]
    rows = x.shape[0]
    nchip = lax.axis_size("chip")
    nctx = lax.axis_size(CTX)
    nz = lax.axis_size("z")
    me = lax.axis_index(CTX)
    chip = lax.axis_index("chip")
    core = lax.axis_index("core")
    z = lax.axis_index("z")
    fast = nctx == 8 and nz == 4
    S = rows * nctx
    W = D // nctx
    run = PROMPT // nctx
    nb = S // run
    nprompt = PROMPT // run
    shard = D // nz
    own = D // (nctx * nz)
    at = (me * nz + z) * own
    keep = own if fast else 16

    x_all = lax.all_gather(x, CTX, axis=0, tiled=True)
    w_own = lax.dynamic_index_in_dim(w_qkv.reshape(shard, 3, nctx, W), me, 2, keepdims=False).reshape(shard, 3 * W)
    gains = jnp.stack([gain_attn, gain_mlp])
    runs = (row_token[0, ::run] // run).astype(BF)
    runs = jnp.pad(runs[None], ((0, 15), (0, W - runs.shape[0])))
    vf = jnp.concatenate([value_first[0].reshape(rows, nctx, W).transpose(1, 0, 2), jnp.broadcast_to(runs, (nctx, 16, W))], axis=1)
    vf = exchange(vf)
    if fast:
        pay = jnp.concatenate([w_own, jnp.pad(gains, ((0, 14), (0, 3 * W - shard)))], axis=0)
        pay = gathered(pay, "z", nz, z)
    else:
        w_own = lax.all_gather(w_own, "z", axis=0, tiled=True).T
        gains = lax.all_gather(gains, "z", axis=1, tiled=True).astype(F32)
        gain_one, gain_two = gains[0:1], gains[1:2]
        blk = vf[:, rows, : nb // nctx].astype(jnp.int32).reshape(nb)

    lengths = cont_lengths[0]
    count = jnp.arange(lengths.shape[0], dtype=jnp.int32)
    starts = PROMPT + jnp.sum(jnp.where(count[:, None] < count[None, :], lengths[:, None], 0), axis=0)
    token = jnp.arange(S, dtype=jnp.int32)
    passed = token[None, :] >= starts[:, None]
    opening = jnp.max(jnp.where(passed, starts[:, None], 0), axis=0).astype(jnp.int32)
    position = jnp.where(opening > 0, PROMPT + token - opening, token)
    freq = BASE ** (-(jnp.arange(HEAD // 2, dtype=F32) * 2.0 / HEAD))
    angles = freq[:, None] * position.astype(F32)[None, :]
    cosT = jnp.cos(angles)
    sinT = jnp.sin(angles)
    block = jnp.arange(nb, dtype=jnp.int32)
    jlo = jnp.where(block < nprompt, block, opening[::run] // run).astype(jnp.int32)
    opening = opening[None, :]

    if fast:
        piece = shard // nctx
        mine = jnp.concatenate([lax.dynamic_slice_in_dim(w, me * piece, piece, 0) for w in (w_out, w_gate_up)], axis=1)
        near = jnp.concatenate([swapped(mine, "z", nz, d) for d in range(1, nz)], axis=0)
        down = half_rows(w_down, core)
        qkv = half_rows(w_qkv, core)
        x_all, near, vf, pay, down, qkv = lax.optimization_barrier((x_all, near, vf, pay, down, qkv))
        w_own = pay[:, :shard].reshape(D, 3 * W).T
        gains = pay[:, shard : shard + 2, :shard].transpose(1, 0, 2).reshape(2, D).astype(F32)
        gain_one, gain_two = gains[0:1], gains[1:2]
        blk = vf[:, rows, : nb // nctx].astype(jnp.int32).reshape(nb)
        planes = [near] + [swapped(near, "chip", nchip, e) for e in range(1, nchip)]
        down = lax.all_gather(down, "z", axis=0, tiled=True)
        pos = [z * shard]
        out_pieces, gate_pieces = [[(i, 0, shard, 0, 0, i)] for i in range(2)]
        sem = 2
        for f in range(2):
            for e in range(nchip):
                for d in range(1, nz):
                    pos.append((z ^ d) * shard + ((chip ^ e) * 2 + (core ^ f)) * piece)
                    ref = 2 + f * nchip + e
                    out_pieces.append((ref, (d - 1) * piece, piece, 0, len(pos) - 1, sem))
                    gate_pieces.append((ref, (d - 1) * piece, piece, D, len(pos) - 1, sem + 1))
                    sem += 2
        down_pieces = []
        half = shard // 2
        for k in range(nz):
            for f in range(2):
                pos.append(k * shard + (core ^ f) * half)
                down_pieces.append((2 + 2 * nchip + f, k * half, half, 0, len(pos) - 1, sem))
                sem += 1
        qkv_pieces = []
        for d in range(nz):
            for f in range(2):
                pos.append(d * shard + (core ^ f) * half)
                qkv_pieces.append((f, d * half, half, 0, len(pos) - 1, len(qkv_pieces)))
        pos = jnp.stack(pos + [core, at]).astype(jnp.int32)
    else:
        arrays = [lax.all_gather(w, "z", axis=0, tiled=True) for w in (w_out, w_gate_up, w_down)]
        qkv_arrays = [lax.all_gather(w_qkv, "z", axis=0, tiled=True)]
        pos = jnp.zeros((3,), jnp.int32)
        out_pieces, gate_pieces, down_pieces = [[(i, 0, D, 0, 0, i)] for i in range(3)]
        qkv_pieces = [(0, 0, D, 0, 0, 0)]

    spos = jnp.sum(jnp.where(blk[None, :] == block[:, None], block[None, :], 0), axis=1).astype(jnp.int32)
    normed_all, qT, kT, vT, kn, vn = project(x_all, gain_one, w_own, vf, cosT, sinT, blk, run=run)
    everything = {"run": run, "nprompt": nprompt, "base": 0, "count": nb}
    attn_all, attnT, lse = attn_fwd(qT, kn, vT, opening, jlo, spos, **everything)
    if fast:
        attn_all, qkv, down, *planes = lax.optimization_barrier((attn_all, qkv, down, *planes))
        qkv = lax.all_gather(qkv, "z", axis=0, tiled=True)
        arrays = [w_out, w_gate_up] + planes + [swapped(p, "core", 2, 1) for p in planes] + [down, swapped(down, "core", 2, 1)]
    attn3 = exchange(attn_all.reshape(nctx, rows, W))
    if not fast:
        attn3 = attn3.transpose(1, 0, 2).reshape(1, rows, D)
    pieces = (out_pieces, gate_pieces, down_pieces)
    right_a, side_near, side_far, rows_a, *carried = feed_forward(True, (), attn3, x, og, gain_two, pos, arrays, *pieces, keep)
    if fast:
        come_right_a = swapped(right_a, "core", 2, 1)
        come_side = swapped(side_far, "core", 2, 1)
    mixed_out, right_b, dy1_low, dy1, dattn3, rows_b = feed_forward(False, carried, attn3, x, og, gain_two, pos, arrays, *pieces, keep)
    if fast:
        dattn3, right_b, dy1_low, qkv, come_right_a, come_side = lax.optimization_barrier(
            (dattn3, right_b, dy1_low, qkv, come_right_a, come_side)
        )
    else:
        dattn3 = dattn3.reshape(rows, nctx, W).transpose(1, 0, 2)
    dattn_all = exchange(dattn3).reshape(S, W)
    wa, wb = CUT, FF - CUT

    def halves_of(v):
        a = v[:, : 2 * wa].reshape(v.shape[0], 2, 2, wa // 2)
        b = v[:, 2 * wa : 2 * FF].reshape(v.shape[0], 2, 2, wb // 2)
        return jnp.concatenate([v_.reshape(v.shape[0], -1) for i in range(2) for v_ in (a[:, :, i], b[:, :, i])], axis=1)

    if fast:
        come_right_b = swapped(right_b, "core", 2, 1)
        come_low = swapped(dy1_low, "core", 2, 1)
        by_chip = [(chip ^ e) * nz + k for e in range(nchip) for k in range(nz)]
        by_all = [k + 0 * chip for k in range(nchip * nz)]
        by_fsdp = [(chip ^ e) * nz + k for k in range(nz) for e in range(nchip)]
        orders_a = jnp.stack([jnp.stack(by_chip), jnp.stack(by_fsdp)]).astype(jnp.int32)
        orders_b = jnp.stack([jnp.stack(by_all), jnp.stack(by_fsdp)]).astype(jnp.int32)
        terms_a, downs_a = weight_terms(side_near, come_side, right_a, come_right_a, orders_a, None, None)
        terms_b, downs_b = weight_terms(side_near, come_side, right_b, come_right_b, orders_b, dy1_low, come_low)
        dattn_all, terms_b, downs_b = lax.optimization_barrier((dattn_all, terms_b, downs_b))
        qkv_arrays = [qkv, swapped(qkv, "core", 2, 1)]
        terms_a = [terms_a[0]] + [swapped(terms_a[e], "chip", nchip, e) for e in range(1, nchip)]
        terms_b = lax.all_to_all(terms_b, "chip", 0, 0, tiled=True)
        downs = [lax.psum_scatter(v, "z", scatter_dimension=0, tiled=True)[0] for v in (downs_a, downs_b)]
    else:
        chunk = lambda v, w: v.reshape(rows, 2, 3, w // 2)
        ra, rb = chunk(right_a, wa), chunk(right_b, wb)
        part = lambda i: jnp.concatenate([ra[:, :, i].reshape(rows, wa), rb[:, :, i].reshape(rows, wb)], axis=1)
        normed_two = jnp.stack([side_near[:, :HALF].reshape(rows, D // 256, 128), side_far[:, :HALF].reshape(rows, D // 256, 128)], axis=2).reshape(rows, D)
        terms = jnp.concatenate(
            [dot(attn3[0], dy1_low, TN), dot(normed_two, part(0), TN), dot(normed_two, part(1), TN), dot(og, part(2), TN)], axis=1
        ).astype(BF)
        share = lax.psum_scatter(terms, CTX, scatter_dimension=0, tiled=True)
        share = lax.psum_scatter(share, "z", scatter_dimension=0, tiled=True).astype(F32)
        out_share, gate_share, down_share = share[:, :D], share[:, D : D + 2 * FF], share[:, D + 2 * FF :]

    (dqkv_own,) = attn_bwd(qT, kn, kT, vn, dattn_all, attnT, lse, opening, jlo, spos, spos, cosT, sinT, None, **everything)
    if fast:
        dqkv_own, terms_a, terms_b, downs = lax.optimization_barrier((dqkv_own, terms_a, terms_b, downs))

        share = jnp.concatenate(
            [sum(v.astype(F32) for v in terms_a).astype(BF), sum(terms_b[k].astype(F32) for k in range(nchip)).astype(BF)], axis=1
        )
        share = lax.psum_scatter(share, "z", scatter_dimension=0, tiled=True).astype(F32)
        downs = jnp.concatenate(downs, axis=1).reshape(nchip, own, FF)
        down_share = downs[0].astype(F32) + sum(swapped(downs[e], "chip", nchip, e).astype(F32) for e in range(1, nchip))
        gate_share = halves_of(share)
        out_share = share[:, 2 * FF :]
    dqkv3 = exchange(dqkv_own.reshape(nctx, rows, 3 * W))
    if not fast:
        dqkv3 = dqkv3.reshape(nctx, rows, 3, W).transpose(1, 2, 0, 3).reshape(1, rows, 3 * D)

    term = dot(normed_all, dqkv_own, TN).astype(BF).reshape(nctx, nz, own, 3 * W)
    if fast:

        def slot(d):
            return lax.dynamic_index_in_dim(term, z ^ d, 1, keepdims=False)

        term = slot(0).astype(F32) + sum(swapped(slot(d), "z", nz, d).astype(F32) for d in range(1, nz))
        term = term.astype(BF)
    else:
        term = lax.psum_scatter(term.transpose(1, 0, 2, 3), "z", scatter_dimension=0, tiled=True)[0]
    dqkv3, term = lax.optimization_barrier((dqkv3, term))
    qkv_share = exchange(term).reshape(nctx, own, 3, W).transpose(1, 2, 0, 3).reshape(own, 3 * D).astype(F32)

    input_grad, first_value_grad, qkv_rows = tail(dqkv3, x, dy1, gain_one, pos, qkv_arrays, qkv_pieces, keep)

    gain_own = lax.dynamic_slice_in_dim(gains, at, own, 1)
    if fast:
        _, rows_a, rows_b = lax.optimization_barrier((dqkv3, rows_a, rows_b))
        gate_rows = jnp.concatenate([rows_a[:, :wa], rows_b[:, :wb], rows_a[:, wa:], rows_b[:, wb:]], axis=1)
    else:
        qkv_rows = lax.dynamic_slice_in_dim(qkv_arrays[0], at, own, 0)
        gate_rows = lax.dynamic_slice_in_dim(arrays[1], at, own, 0)
    gain_one_share = jnp.sum(qkv_rows.astype(F32) * qkv_share, axis=1) / gain_own[0]
    gain_two_share = jnp.sum(gate_rows.astype(F32) * gate_share, axis=1) / gain_own[1]
    return (
        mixed_out[None],
        input_grad[None],
        first_value_grad[None],
        gain_one_share,
        qkv_share,
        out_share,
        gain_two_share,
        gate_share,
        down_share,
    )


def solution(mesh):
    ctx, fsdp = mesh.devices.shape
    split = Mesh(mesh.devices.reshape(ctx // 2, 2, fsdp), ("chip", "core", "z"))
    rows3 = P("z", CTX, None)
    weight = P("z", None)
    every = ("chip", "core", "z")
    return jax.shard_map(
        body,
        mesh=split,
        in_specs=(rows3, rows3, rows3, P("z"), weight, weight, P("z"), weight, weight, weight, P("z", CTX)),
        out_specs=(rows3, rows3, rows3, P(every), P(every, None), P(every, None), P(every), P(every, None), P(every, None)),
        check_vma=False,
    )
```

```python
import jax
import jax.numpy as jnp
from jax import lax
from jax.experimental import pallas as pl
from jax.experimental.pallas import tpu as pltpu
from jax.sharding import Mesh, PartitionSpec as P

D = 1024
HEADS = 16
HEAD = 64
FF = 2816
PROMPT = 2048
EPS = 1e-05
BASE = 10000.0
LOG2E = 1.4426950408889634
NEG = -1e30
C2 = 0.125 * LOG2E
CTX = ("chip", "core")
BF = jnp.bfloat16
F32 = jnp.float32


def dot(a, b, dims):
    return lax.dot_general(a, b, (dims, ((), ())), preferred_element_type=F32)


NN = ((1,), (0,))
NT = ((1,), (1,))
TN = ((0,), (0,))


def chunked(first, stop, sizes, fn, c):
    for n in sizes:
        count = (stop - first) // n
        c = lax.fori_loop(0, count, lambda t, c, n=n, first=first: fn(first + t * n, c, n), c)
        first = first + count * n
    return c


def visible(i, j, rows, run, lo):
    key = j * run + lax.broadcasted_iota(jnp.int32, (rows, run), 0)
    query = i * run + lax.broadcasted_iota(jnp.int32, (rows, run), 1)
    return (key <= query) & (key >= lo)


def attn_fwd(qT, kn, vT, lo, jlo, opos, *, run, nprompt, base, count):
    W, S = qT.shape
    hl = W // HEAD
    keys = S if base + count > nprompt else nprompt * run
    full_sizes, own_sizes = (8, 4, 2, 1), (4, 2, 1)

    def kern(jlo_ref, opos_ref, q_ref, k_ref, v_ref, lo_ref, o_ref, of_ref, lse_ref, s_scr):
        i = pl.program_id(0) + base
        qs = [q_ref[h * HEAD : (h + 1) * HEAD, :] for h in range(hl)]
        full = jnp.minimum(i, nprompt)
        own = jlo_ref[i]
        total = full + (i + 1 - own)

        def fold(f, s):
            return f(s.reshape(s.shape[0] // 8, 8, run), axis=0)

        def score(t, tops, n, shift, masked):
            tops = list(tops)
            for u in range(n):
                j = t + u + shift
                at = pl.multiple_of(j * run, run)
                row = pl.multiple_of((t + u) * run, run)
                if masked:
                    vis = visible(i, j, run, run, lo_ref[...])
                for h in range(hl):
                    s = dot(k_ref[h, pl.ds(at, run), :], qs[h], NN)
                    if masked:
                        s = jnp.where(vis, s, NEG)
                    s_scr[h, pl.ds(row, run), :] = s
                    tops[h] = jnp.maximum(tops[h], fold(jnp.max, s))
            return tuple(tops)

        tops = tuple(jnp.full((8, run), NEG, F32) for _ in range(hl))
        tops = chunked(0, full, full_sizes, lambda t, c, n: score(t, c, n, 0, False), tops)
        tops = chunked(full, total, own_sizes, lambda t, c, n: score(t, c, n, own - full, True), tops)
        m = [jnp.max(tops[h], axis=0, keepdims=True) * C2 for h in range(hl)]

        def weigh(t, c, n, shift):
            c = list(c)
            for u in range(n):
                at = pl.multiple_of((t + u + shift) * run, run)
                row = pl.multiple_of((t + u) * run, run)
                for h in range(hl):
                    l, acc = c[h]
                    p = jnp.exp2(s_scr[h, pl.ds(row, run), :] * C2 - m[h])
                    l = l + fold(jnp.sum, p)
                    acc = acc + dot(v_ref[h * HEAD : (h + 1) * HEAD, pl.ds(at, run)], p.astype(BF), NN)
                    c[h] = (l, acc)
            return tuple(c)

        c = tuple((jnp.zeros((8, run), F32), jnp.zeros((HEAD, run), F32)) for _ in range(hl))
        c = chunked(0, full, full_sizes, lambda t, c, n: weigh(t, c, n, 0), c)
        c = chunked(full, total, own_sizes, lambda t, c, n: weigh(t, c, n, own - full), c)
        outs = []
        for h in range(hl):
            l8, acc = c[h]
            l = jnp.sum(l8, axis=0, keepdims=True)
            o = acc / l
            of_ref[h * HEAD : (h + 1) * HEAD, :] = o
            lse_ref[h, :, :] = m[h] + jnp.log2(l)
            outs.append(o)
        o = jnp.concatenate(outs, axis=0) if hl > 1 else outs[0]
        o_ref[...] = o.T.astype(BF)

    rows = count * run
    return pl.pallas_call(
        kern,
        out_shape=(jax.ShapeDtypeStruct((rows, W), BF), jax.ShapeDtypeStruct((W, rows), F32), jax.ShapeDtypeStruct((hl, 1, rows), F32)),
        grid_spec=pltpu.PrefetchScalarGridSpec(
            num_scalar_prefetch=2,
            grid=(count,),
            in_specs=[
                pl.BlockSpec((W, run), lambda i, *_: (0, i + base)),
                pl.BlockSpec((hl, keys, HEAD), lambda i, *_: (0, 0, 0)),
                pl.BlockSpec((W, keys), lambda i, *_: (0, 0)),
                pl.BlockSpec((1, run), lambda i, *_: (0, i + base)),
            ],
            out_specs=[
                pl.BlockSpec((run, W), lambda i, jl, op: (op[i + base], 0)),
                pl.BlockSpec((W, run), lambda i, *_: (0, i)),
                pl.BlockSpec((hl, 1, run), lambda i, *_: (0, 0, i)),
            ],
            scratch_shapes=[pltpu.VMEM((hl, keys, run), F32)],
        ),
        compiler_params=params(),
        cost_estimate=cost(20 * rows * keys * W // 2, 12 * S * W, rows * keys // 2),
        name="attention_forward",
    )(jlo, opos, qT, kn, vT, lo)


def attn_bwd(qT, kn, kT, vn, don, of, lse, lo, jlo, spos, opos, cosT, sinT, sums, *, run, nprompt, base, count):
    W, S = qT.shape
    hl = W // HEAD
    hh = HEAD // 2
    keys = S if base + count > nprompt else nprompt * run
    later = base > 0
    P_ = nprompt * run
    full_sizes, own_sizes = (4, 2, 1), (2, 1)

    def unrotate(g, cos, sin):
        parts = []
        for h in range(hl):
            a = g[h * HEAD : h * HEAD + hh]
            b = g[h * HEAD + hh : (h + 1) * HEAD]
            parts += [a * cos + b * sin, b * cos - a * sin]
        return jnp.concatenate(parts, axis=0)

    def kern(jlo_ref, spos_ref, opos_ref, q_ref, k_ref, kT_ref, v_ref, do_ref, of_ref, lse_ref, lo_ref, cos_ref, sin_ref, *rest):
        if sums is not None:
            sk_ref, sv_ref = rest[:2]
            rest = rest[2:]
        if later:
            g_ref, ok_ref, ov_ref, dkT, dvT = rest
        else:
            g_ref, dkT, dvT = rest
        i = pl.program_id(0) + base

        @pl.when(pl.program_id(0) == 0)
        def _():
            if sums is not None:
                dkT[...] = sk_ref[...]
                dvT[...] = sv_ref[...]
            else:
                dkT[...] = jnp.zeros_like(dkT)
                dvT[...] = jnp.zeros_like(dvT)

        doT = do_ref[...].T
        dof = doT.astype(F32)
        qs = [q_ref[h * HEAD : (h + 1) * HEAD, :] for h in range(hl)]
        dos = [doT[h * HEAD : (h + 1) * HEAD, :] for h in range(hl)]
        delta = [
            jnp.sum(dof[h * HEAD : (h + 1) * HEAD] * of_ref[h * HEAD : (h + 1) * HEAD, :], axis=0, keepdims=True) for h in range(hl)
        ]
        ls = [lse_ref[h, :, :] for h in range(hl)]

        def tile(j, carry, n, masked):
            kb = n * run
            at = pl.multiple_of(j * run, run)
            if masked:
                vis = visible(i, j, kb, run, lo_ref[...])
            out = []
            for h in range(hl):
                hs = slice(h * HEAD, (h + 1) * HEAD)
                s = dot(k_ref[h, pl.ds(at, kb), :], qs[h], NN)
                p = jnp.exp2(s * C2 - ls[h])
                if masked:
                    p = jnp.where(vis, p, 0.0)
                dp = dot(v_ref[h, pl.ds(at, kb), :], dos[h], NN)
                ds = (p * (dp - delta[h])).astype(BF)
                dvT[hs, pl.ds(at, kb)] += dot(dos[h], p.astype(BF), NT)
                dkT[hs, pl.ds(at, kb)] += dot(qs[h], ds, NT)
                out.append(carry[h] + dot(kT_ref[hs, pl.ds(at, kb)], ds, NN))
            return tuple(out)

        c = tuple(jnp.zeros((HEAD, run), F32) for _ in range(hl))
        c = chunked(0, jnp.minimum(i, nprompt), full_sizes, lambda j, c, n: tile(j, c, n, False), c)
        c = chunked(jlo_ref[i], i + 1, own_sizes, lambda j, c, n: tile(j, c, n, True), c)
        dq = (jnp.concatenate(c, axis=0) if hl > 1 else c[0]) * 0.125

        def turned(g, b):
            at = pl.multiple_of(b * run, run)
            return unrotate(g, cos_ref[:, pl.ds(at, run)], sin_ref[:, pl.ds(at, run)]).T.astype(BF)

        row = pl.multiple_of(opos_ref[i] * run, run)
        g_ref[pl.ds(row, run), :W] = turned(dq, i)

        @pl.when(pl.program_id(0) == count - 1)
        def _():
            def finish(b, _):
                at = pl.multiple_of(b * run, run)
                row = pl.multiple_of(opos_ref[b] * run, run)
                g_ref[pl.ds(row, run), W : 2 * W] = turned(dkT[:, pl.ds(at, run)] * 0.125, b)
                g_ref[pl.ds(row, run), 2 * W :] = (dvT[:, pl.ds(at, run)] * 0.5).T.astype(BF)
                return 0

            lax.fori_loop(base, base + count, finish, 0)
            if later:
                ok_ref[...] = dkT[:, :P_]
                ov_ref[...] = dvT[:, :P_]

    full = lambda *s: pl.BlockSpec(s, lambda i, *_: (0,) * len(s))
    rows = count * run
    sum_shape = jax.ShapeDtypeStruct((W, P_), F32)
    return pl.pallas_call(
        kern,
        out_shape=(jax.ShapeDtypeStruct((rows, 3 * W), BF),) + ((sum_shape, sum_shape) if later else ()),
        grid_spec=pltpu.PrefetchScalarGridSpec(
            num_scalar_prefetch=3,
            grid=(count,),
            in_specs=[
                pl.BlockSpec((W, run), lambda i, *_: (0, i + base)),
                full(hl, keys, HEAD),
                full(W, keys),
                full(hl, keys, HEAD),
                pl.BlockSpec((run, W), lambda i, jl, sp, op: (sp[i + base], 0)),
                pl.BlockSpec((W, run), lambda i, *_: (0, i)),
                pl.BlockSpec((hl, 1, run), lambda i, *_: (0, 0, i)),
                pl.BlockSpec((1, run), lambda i, *_: (0, i + base)),
                full(hh, keys),
                full(hh, keys),
            ]
            + ([full(W, P_)] * 2 if sums is not None else []),
            out_specs=[full(rows, 3 * W)] + ([full(W, P_)] * 2 if later else []),
            scratch_shapes=[pltpu.VMEM((W, keys), F32)] * 2,
        ),
        compiler_params=params(),
        cost_estimate=cost(32 * rows * keys * W // 2, 24 * S * W, rows * keys // 2),
        name="attention_backward",
    )(jlo, spos, opos, qT, kn, kT, vn, don, of, lse, lo, cosT, sinT, *(sums or ()))


def cost(flops, nbytes, trans=0):
    return pl.CostEstimate(flops=int(flops), bytes_accessed=int(nbytes), transcendentals=int(trans))


def whole(*shape):
    return pl.BlockSpec(shape, lambda *_: (0,) * len(shape))


ANY = pl.BlockSpec(memory_space=pl.ANY)


def params():
    return pltpu.CompilerParams(vmem_limit_bytes=56 << 20)


def project(x, gain, w, vf, cos, sin, blk, *, run):
    S = x.shape[0]
    W = vf.shape[2]
    hl = W // HEAD
    nb = S // run
    per = nb // vf.shape[0]
    hh = HEAD // 2

    def kern(blk_ref, x_ref, g_ref, w_ref, vf_ref, c_ref, s_ref, n_o, q_o, kT_o, vT_o, kn_o, vn_o):
        xf = x_ref[...].astype(F32)
        inv = lax.rsqrt(jnp.mean(xf * xf, axis=1, keepdims=True) + EPS)
        n1 = (xf * inv * g_ref[...]).astype(BF)
        n_o[...] = n1
        t = dot(w_ref[...], n1, NT)
        c = c_ref[...]
        s = s_ref[...]

        def rope(base):
            parts = []
            for h in range(hl):
                a = t[base + h * HEAD : base + h * HEAD + hh]
                b = t[base + h * HEAD + hh : base + (h + 1) * HEAD]
                parts += [a * c - b * s, b * c + a * s]
            return jnp.concatenate(parts, axis=0)

        q_o[...] = rope(0).astype(BF)
        k = rope(W)
        kT_o[...] = k.astype(BF)
        v = 0.5 * t[2 * W :] + 0.5 * vf_ref[0].astype(F32).T
        vT_o[...] = v.astype(BF)
        for h in range(hl):
            kn_o[h] = k[h * HEAD : (h + 1) * HEAD].T.astype(BF)
            vn_o[h] = v[h * HEAD : (h + 1) * HEAD].T.astype(BF)

    T = jax.ShapeDtypeStruct((W, S), BF)
    N = jax.ShapeDtypeStruct((hl, S, HEAD), BF)
    tb = pl.BlockSpec((W, run), lambda r, b: (0, b[r]))
    nbk = pl.BlockSpec((hl, run, HEAD), lambda r, b: (0, b[r], 0))
    rb = pl.BlockSpec((hh, run), lambda r, b: (0, b[r]))
    return pl.pallas_call(
        kern,
        out_shape=(jax.ShapeDtypeStruct((S, D), BF), T, T, T, N, N),
        grid_spec=pltpu.PrefetchScalarGridSpec(
            num_scalar_prefetch=1,
            grid=(nb,),
            in_specs=[pl.BlockSpec((run, D), lambda r, b: (r, 0)), whole(1, D), whole(3 * W, D), pl.BlockSpec((1, run, W), lambda r, b: (r // per, r % per, 0)), rb, rb],
            out_specs=[pl.BlockSpec((run, D), lambda r, b: (r, 0)), tb, tb, tb, nbk, nbk],
        ),
        compiler_params=params(),
        cost_estimate=cost(6 * S * D * W, 4 * S * D + 12 * S * W),
        name="project_qkv",
    )(blk, x, gain, w, vf, cos, sin)


def load_pieces(pieces, refs, pos_ref, dst, sems):
    copies = []
    for ref, row, rows, col, place, sem in pieces:
        at = pl.multiple_of(pos_ref[place], rows)
        copies.append(
            pltpu.make_async_copy(
                refs[ref].at[pl.ds(row, rows), pl.ds(col, dst.shape[1])], dst.at[pl.ds(at, rows), :], sems.at[sem]
            )
        )
    return copies


CUT = 1536
HALF = D // 2


def column_pieces(pieces, first, width):
    return [(ref, row, size, col + first, place, sem) for ref, row, size, col, place, sem in pieces]


def feed_forward(start, carried, attn3, x, og, gain, pos, arrays, out_pieces, gate_pieces, down_pieces, keep):
    n, rows, W = attn3.shape
    lo, hi = (0, CUT) if start else (CUT, FF)
    width = hi - lo
    FC = width // 2
    nsem = len(out_pieces) + 2 * len(gate_pieces) + len(down_pieces)
    na = len(arrays)
    last = pos.shape[0]
    ncarry = len(carried)

    def kern(pos_ref, a_ref, x_ref, og_ref, g_ref, *rest):
        refs = rest[:na]
        rest = rest[na:]
        cin, rest = rest[:ncarry], rest[ncarry:]
        if start:
            r_o, near_o, far_o, wr_o, y_o, n2_o, m_o, acc_o = rest[:8]
            wo, wg, wu, wd, al, sems = rest[8:]
        else:
            mixed_o, r_o, low_o, dy_o, da_o, wr_o = rest[:6]
            wo, wg, wu, wd, acc_m, acc_n, sems = rest[6:]
        f = pl.program_id(0)

        def sides(ref, place):
            for out, c in ((near_o, pos_ref[last - 2]), (far_o, 1 - pos_ref[last - 2])):
                for e in range(D // 256):
                    out[:, place + e * 128 : place + (e + 1) * 128] = ref[:, pl.ds(pl.multiple_of((2 * e + c) * 128, 128), 128)]

        @pl.when(f == 0)
        def _():
            ng = len(gate_pieces)
            first = load_pieces(out_pieces, refs, pos_ref, wo, sems)
            second = load_pieces(column_pieces(gate_pieces, lo, 0), refs, pos_ref, wg, sems)
            second += load_pieces([(r, a, b, c + FF + lo, p, s + nsem - ng) for r, a, b, c, p, s in renumber(gate_pieces)], refs, pos_ref, wu, sems)
            third = load_pieces(column_pieces(down_pieces, lo, 0), refs, pos_ref, wd, sems)
            for cp in (first + second + third) if start else (second + third + first):
                cp.start()
            if start:
                for i in range(n):
                    al[:, i * W : (i + 1) * W] = a_ref[i]
                sides(og_ref, 2 * HALF)
                sides(al, HALF)
                for cp in first:
                    cp.wait()
                y = x_ref[...].astype(F32) + dot(al[...], wo[...], NN)
                y_o[...] = y
                inv = lax.rsqrt(jnp.mean(y * y, axis=1, keepdims=True) + EPS)
                n2_o[...] = (y * inv * g_ref[...]).astype(BF)
                sides(n2_o, 0)
                m_o[...] = y
                acc_o[...] = jnp.zeros_like(acc_o)
            else:
                acc_m[...] = cin[2][...]
                acc_n[...] = cin[3][...]
            for cp in second + third:
                cp.wait()
            if not start:
                for cp in first:
                    cp.wait()

        n2 = n2_o if start else cin[1]
        am = m_o if start else acc_m
        an = acc_o if start else acc_n
        c0 = pl.multiple_of(f * FC, 128)
        a = n2[...]
        g = dot(a, wg[:, pl.ds(c0, FC)], NN)
        u = dot(a, wu[:, pl.ds(c0, FC)], NN)
        dh = dot(og_ref[...], wd[:, pl.ds(c0, FC)], NN)
        sg = jax.nn.sigmoid(g)
        silu = g * sg
        hid = (silu * u).astype(BF)
        dg = (dh * u * sg * (1.0 + g * (1.0 - sg))).astype(BF)
        du = (dh * silu).astype(BF)
        r_o[:, :FC] = dg
        r_o[:, FC : 2 * FC] = du
        r_o[:, 2 * FC :] = hid
        am[...] += dot(hid, wd[:, pl.ds(c0, FC)], NT)
        an[...] += dot(dg, wg[:, pl.ds(c0, FC)], NT) + dot(du, wu[:, pl.ds(c0, FC)], NT)

        @pl.when(f == 1)
        def _():
            at = pl.multiple_of(pos_ref[last - 1], keep)
            wr_o[:, :width] = wg[pl.ds(at, keep), :]
            wr_o[:, width:] = wu[pl.ds(at, keep), :]
            if not start:
                mixed_o[...] = am[...].astype(BF)
                y = cin[0][...]
                inv = lax.rsqrt(jnp.mean(y * y, axis=1, keepdims=True) + EPS)
                xh = y * inv
                t = an[...] * g_ref[...]
                dy = og_ref[...].astype(F32) + inv * (t - xh * jnp.mean(t * xh, axis=1, keepdims=True))
                dy_o[...] = dy
                low = dy.astype(BF)
                low_o[...] = low
                da = dot(low, wo[...], NT).astype(BF)
                for i in range(n):
                    da_o[i] = da[:, i * W : (i + 1) * W]

    wide = jax.ShapeDtypeStruct((rows, D), F32)
    side = jax.ShapeDtypeStruct((rows, 3 * HALF), BF)
    low = jax.ShapeDtypeStruct((rows, D), BF)
    right = jax.ShapeDtypeStruct((rows, 3 * width), BF)
    own_rows = jax.ShapeDtypeStruct((keep, 2 * width), BF)
    rspec = pl.BlockSpec((rows, 3 * FC), lambda f, *_: (0, f))
    full = whole(rows, D)
    if start:
        outs = (right, side, side, own_rows, wide, low, wide, wide)
        specs = [rspec, whole(rows, 3 * HALF), whole(rows, 3 * HALF), whole(keep, 2 * width), full, full, full, full]
        extra = [pltpu.VMEM((rows, D), BF)]
    else:
        outs = (low, right, low, wide, jax.ShapeDtypeStruct((n, rows, W), BF), own_rows)
        specs = [full, rspec, full, full, whole(n, rows, W), whole(keep, 2 * width)]
        extra = [pltpu.VMEM((rows, D), F32)] * 2
    return pl.pallas_call(
        kern,
        out_shape=outs,
        grid_spec=pltpu.PrefetchScalarGridSpec(
            num_scalar_prefetch=1,
            grid=(2,),
            in_specs=[whole(n, rows, W), full, full, whole(1, D)] + [ANY] * na + [full] * ncarry,
            out_specs=specs,
            scratch_shapes=[
                pltpu.VMEM((D, D), BF),
                pltpu.VMEM((D, width), BF),
                pltpu.VMEM((D, width), BF),
                pltpu.VMEM((D, width), BF),
                *extra,
                pltpu.SemaphoreType.DMA((nsem,)),
            ],
        ),
        compiler_params=params(),
        cost_estimate=cost(4 * rows * D * (D + 6 * width), 2 * D * (D + 3 * width) + 2 * rows * (14 * D + 3 * width)),
        name="feed_forward_start" if start else "feed_forward_end",
    )(pos, attn3, x, og, gain, *arrays, *carried)


def renumber(pieces):
    return [(r, a, b, c, p, i) for i, (r, a, b, c, p, _) in enumerate(pieces)]


def tail(dqkv3, x, dy1, gain, pos, arrays, pieces, keep):
    n, rows, W3 = dqkv3.shape
    W = W3 // 3
    na = len(arrays)
    group = max(1, len(pieces) // 4)

    def kern(pos_ref, d_ref, x_ref, dy_ref, g_ref, *rest):
        refs = rest[:na]
        ig_o, fv_o, wr_o = rest[na : na + 3]
        w, dn, sems = rest[na + 3 :]
        copies = load_pieces(pieces, refs, pos_ref, w, sems)
        for cp in copies:
            cp.start()
        if n > 1:
            d = jnp.concatenate([d_ref[i, :, p * W : (p + 1) * W] for p in range(3) for i in range(n)], axis=1)
        else:
            d = d_ref[0]
        fv_o[...] = d[:, 2 * D :].astype(F32)
        for cp in copies:
            cp.wait()
        t = dot(d, w[...], NT)
        wr_o[...] = w[pl.ds(pl.multiple_of(pos_ref[pos.shape[0] - 1], keep), keep), :]
        xf = x_ref[...].astype(F32)
        inv = lax.rsqrt(jnp.mean(xf * xf, axis=1, keepdims=True) + EPS)
        xh = xf * inv
        t = t * g_ref[...]
        ig_o[...] = dy_ref[...] + inv * (t - xh * jnp.mean(t * xh, axis=1, keepdims=True))

    o = jax.ShapeDtypeStruct((rows, D), F32)
    return pl.pallas_call(
        kern,
        out_shape=(o, o, jax.ShapeDtypeStruct((keep, 3 * D), BF)),
        grid_spec=pltpu.PrefetchScalarGridSpec(
            num_scalar_prefetch=1,
            grid=(1,),
            in_specs=[whole(n, rows, W3), whole(rows, D), whole(rows, D), whole(1, D)] + [ANY] * na,
            out_specs=[whole(rows, D), whole(rows, D), whole(keep, 3 * D)],
            scratch_shapes=[pltpu.VMEM((D, 3 * D), BF), pltpu.VMEM((rows, D), F32), pltpu.SemaphoreType.DMA((len(pieces),))],
        ),
        compiler_params=params(),
        cost_estimate=cost(6 * rows * D * D, 6 * D * D + rows * D * 20),
        name="input_gradient",
    )(pos, dqkv3, x, dy1, gain, *arrays)


def weight_terms(near, far, r_near, r_far, orders, low, low_far):
    rows = near.shape[0]
    width = r_near.shape[1] // 3
    FC = width // 2
    nb = orders.shape[1]
    own = HALF // nb
    n = 4
    more = low is not None
    cols = width + (D if more else 0)

    def kern(o_ref, na, fa, ra, rb, *rest):
        if more:
            nd, fd = rest[:2]
            rest = rest[2:]
        t_o, d_o, lt0, lt = rest
        f = pl.program_id(0)

        @pl.when(f == 0)
        def _():
            for i, side in ((0, na), (1, fa)):
                for p in range(3):
                    lt0[p, :, i * rows : (i + 1) * rows] = side[:, p * HALF : (p + 1) * HALF].T
            for p in range(3):
                for b in range(nb):
                    at = o_ref[min(p, 1), b]
                    lt[p, b * own : (b + 1) * own, :] = lt0[p, pl.ds(pl.multiple_of(at * own, own), own), :]

        def put(p, a, b, out, place, size):
            t = dot(lt[p, :, :rows], a, NN) + dot(lt[p, :, rows:], b, NN)
            for e in range(n):
                out[e, :, pl.ds(place, size)] = t[e * HALF // n : (e + 1) * HALF // n].astype(BF)

        put(0, ra[:, : 2 * FC], rb[:, : 2 * FC], t_o, pl.multiple_of(2 * FC * f, 128), 2 * FC)
        put(2, ra[:, 2 * FC :], rb[:, 2 * FC :], d_o, pl.multiple_of(FC * f, 128), FC)
        if more:

            @pl.when(f == 1)
            def _():
                put(1, nd[...], fd[...], d_o, width, D)

    rb = pl.BlockSpec((rows, 3 * FC), lambda f, *_: (0, f))
    return pl.pallas_call(
        kern,
        out_shape=(jax.ShapeDtypeStruct((n, HALF // n, 2 * width), BF), jax.ShapeDtypeStruct((n, HALF // n, cols), BF)),
        grid_spec=pltpu.PrefetchScalarGridSpec(
            num_scalar_prefetch=1,
            grid=(2,),
            in_specs=[whole(rows, 3 * HALF)] * 2 + [rb] * 2 + ([whole(rows, D)] * 2 if more else []),
            out_specs=[whole(n, HALF // n, 2 * width), whole(n, HALF // n, cols)],
            scratch_shapes=[pltpu.VMEM((3, HALF, 2 * rows), BF)] * 2,
        ),
        compiler_params=params(),
        cost_estimate=cost(4 * rows * HALF * (cols + 2 * width), 2 * (2 * rows + HALF) * (cols + 2 * width) + 12 * rows * HALF),
        name="weight_terms",
    )(orders, near, far, r_near, r_far, *((low, low_far) if more else ()))


def exchange(v):
    return lax.all_to_all(v, CTX, 0, 0, tiled=True)


def swapped(v, axes, size, mask):
    return lax.ppermute(v, axes, [(i, i ^ mask) for i in range(size)])


def gathered(v, axes, size, index):
    parts = [v] + [swapped(v, axes, size, s) for s in range(1, size)]
    return jnp.stack([lax.select_n(index ^ a, *parts) for a in range(size)])


def half_rows(w, core):
    half = w.shape[0] // 2
    return lax.dynamic_slice_in_dim(w, core * half, half, 0)


def body(tokens_in, value_first, out_grad, gain_attn, w_qkv, w_out, gain_mlp, w_gate_up, w_down, cont_lengths, row_token):
    x = tokens_in[0]
    og = out_grad[0]
    rows = x.shape[0]
    nchip = lax.axis_size("chip")
    nctx = lax.axis_size(CTX)
    nz = lax.axis_size("z")
    me = lax.axis_index(CTX)
    chip = lax.axis_index("chip")
    core = lax.axis_index("core")
    z = lax.axis_index("z")
    fast = nctx == 8 and nz == 4
    S = rows * nctx
    W = D // nctx
    run = PROMPT // nctx
    nb = S // run
    nprompt = PROMPT // run
    shard = D // nz
    own = D // (nctx * nz)
    at = (me * nz + z) * own
    keep = own if fast else 16

    x_all = lax.all_gather(x, CTX, axis=0, tiled=True)
    w_own = lax.dynamic_index_in_dim(w_qkv.reshape(shard, 3, nctx, W), me, 2, keepdims=False).reshape(shard, 3 * W)
    gains = jnp.stack([gain_attn, gain_mlp])
    runs = (row_token[0, ::run] // run).astype(BF)
    runs = jnp.pad(runs[None], ((0, 15), (0, W - runs.shape[0])))
    vf = jnp.concatenate([value_first[0].reshape(rows, nctx, W).transpose(1, 0, 2), jnp.broadcast_to(runs, (nctx, 16, W))], axis=1)
    vf = exchange(vf)
    if fast:
        pay = jnp.concatenate([w_own, jnp.pad(gains, ((0, 14), (0, 3 * W - shard)))], axis=0)
        pay = gathered(pay, "z", nz, z)
    else:
        w_own = lax.all_gather(w_own, "z", axis=0, tiled=True).T
        gains = lax.all_gather(gains, "z", axis=1, tiled=True).astype(F32)
        gain_one, gain_two = gains[0:1], gains[1:2]
        blk = vf[:, rows, : nb // nctx].astype(jnp.int32).reshape(nb)

    lengths = cont_lengths[0]
    count = jnp.arange(lengths.shape[0], dtype=jnp.int32)
    starts = PROMPT + jnp.sum(jnp.where(count[:, None] < count[None, :], lengths[:, None], 0), axis=0)
    token = jnp.arange(S, dtype=jnp.int32)
    passed = token[None, :] >= starts[:, None]
    opening = jnp.max(jnp.where(passed, starts[:, None], 0), axis=0).astype(jnp.int32)
    position = jnp.where(opening > 0, PROMPT + token - opening, token)
    freq = BASE ** (-(jnp.arange(HEAD // 2, dtype=F32) * 2.0 / HEAD))
    angles = freq[:, None] * position.astype(F32)[None, :]
    cosT = jnp.cos(angles)
    sinT = jnp.sin(angles)
    block = jnp.arange(nb, dtype=jnp.int32)
    jlo = jnp.where(block < nprompt, block, opening[::run] // run).astype(jnp.int32)
    opening = opening[None, :]

    if fast:
        w_own = pay[:, :shard].reshape(D, 3 * W).T
        gains = pay[:, shard : shard + 2, :shard].transpose(1, 0, 2).reshape(2, D).astype(F32)
        gain_one, gain_two = gains[0:1], gains[1:2]
        blk = vf[:, rows, : nb // nctx].astype(jnp.int32).reshape(nb)
    spos = jnp.sum(jnp.where(blk[None, :] == block[:, None], block[None, :], 0), axis=1).astype(jnp.int32)

    if fast:
        piece = shard // nctx
        mine = jnp.concatenate([lax.dynamic_slice_in_dim(w, me * piece, piece, 0) for w in (w_out, w_gate_up)], axis=1)
        near = jnp.concatenate([swapped(mine, "z", nz, d) for d in range(1, nz)], axis=0)
        down = half_rows(w_down, core)
        qkv = half_rows(w_qkv, core)
        x_all, near, vf, w_own, gains, gain_one, blk, spos, cosT, sinT, jlo, down, qkv = lax.optimization_barrier(
            (x_all, near, vf, w_own, gains, gain_one, blk, spos, cosT, sinT, jlo, down, qkv)
        )
        planes = [near] + [swapped(near, "chip", nchip, e) for e in range(1, nchip)]
        down = lax.all_gather(down, "z", axis=0, tiled=True)
        pos = [z * shard]
        out_pieces, gate_pieces = [[(i, 0, shard, 0, 0, i)] for i in range(2)]
        sem = 2
        for f in range(2):
            for e in range(nchip):
                for d in range(1, nz):
                    pos.append((z ^ d) * shard + ((chip ^ e) * 2 + (core ^ f)) * piece)
                    ref = 2 + f * nchip + e
                    out_pieces.append((ref, (d - 1) * piece, piece, 0, len(pos) - 1, sem))
                    gate_pieces.append((ref, (d - 1) * piece, piece, D, len(pos) - 1, sem + 1))
                    sem += 2
        down_pieces = []
        half = shard // 2
        for k in range(nz):
            for f in range(2):
                pos.append(k * shard + (core ^ f) * half)
                down_pieces.append((2 + 2 * nchip + f, k * half, half, 0, len(pos) - 1, sem))
                sem += 1
        qkv_pieces = []
        for d in range(nz):
            for f in range(2):
                pos.append(d * shard + (core ^ f) * half)
                qkv_pieces.append((f, d * half, half, 0, len(pos) - 1, len(qkv_pieces)))
        pos = jnp.stack(pos + [core, at]).astype(jnp.int32)
    else:
        arrays = [lax.all_gather(w, "z", axis=0, tiled=True) for w in (w_out, w_gate_up, w_down)]
        qkv_arrays = [lax.all_gather(w_qkv, "z", axis=0, tiled=True)]
        pos = jnp.zeros((3,), jnp.int32)
        out_pieces, gate_pieces, down_pieces = [[(i, 0, D, 0, 0, i)] for i in range(3)]
        qkv_pieces = [(0, 0, D, 0, 0, 0)]

    normed_all, qT, kT, vT, kn, vn = project(x_all, gain_one, w_own, vf, cosT, sinT, blk, run=run)
    everything = {"run": run, "nprompt": nprompt, "base": 0, "count": nb}
    attn_all, attnT, lse = attn_fwd(qT, kn, vT, opening, jlo, spos, **everything)
    if fast:
        attn_all, qkv, down, *planes = lax.optimization_barrier((attn_all, qkv, down, *planes))
        qkv = lax.all_gather(qkv, "z", axis=0, tiled=True)
        arrays = [w_out, w_gate_up] + planes + [swapped(p, "core", 2, 1) for p in planes] + [down, swapped(down, "core", 2, 1)]
    attn3 = exchange(attn_all.reshape(nctx, rows, W))
    if not fast:
        attn3 = attn3.transpose(1, 0, 2).reshape(1, rows, D)
    pieces = (out_pieces, gate_pieces, down_pieces)
    right_a, side_near, side_far, rows_a, *carried = feed_forward(True, (), attn3, x, og, gain_two, pos, arrays, *pieces, keep)
    if fast:
        come_right_a = swapped(right_a, "core", 2, 1)
        come_side = swapped(side_far, "core", 2, 1)
    mixed_out, right_b, dy1_low, dy1, dattn3, rows_b = feed_forward(False, carried, attn3, x, og, gain_two, pos, arrays, *pieces, keep)
    if fast:
        dattn3, right_b, dy1_low, qkv, come_right_a, come_side = lax.optimization_barrier(
            (dattn3, right_b, dy1_low, qkv, come_right_a, come_side)
        )
    else:
        dattn3 = dattn3.reshape(rows, nctx, W).transpose(1, 0, 2)
    dattn_all = exchange(dattn3).reshape(S, W)
    wa, wb = CUT, FF - CUT

    def halves_of(v):
        a = v[:, : 2 * wa].reshape(v.shape[0], 2, 2, wa // 2)
        b = v[:, 2 * wa : 2 * FF].reshape(v.shape[0], 2, 2, wb // 2)
        return jnp.concatenate([v_.reshape(v.shape[0], -1) for i in range(2) for v_ in (a[:, :, i], b[:, :, i])], axis=1)

    if fast:
        come_right_b = swapped(right_b, "core", 2, 1)
        come_low = swapped(dy1_low, "core", 2, 1)
        by_chip = [(chip ^ e) * nz + k for e in range(nchip) for k in range(nz)]
        by_all = [k + 0 * chip for k in range(nchip * nz)]
        by_fsdp = [(chip ^ e) * nz + k for k in range(nz) for e in range(nchip)]
        orders_a = jnp.stack([jnp.stack(by_chip), jnp.stack(by_fsdp)]).astype(jnp.int32)
        orders_b = jnp.stack([jnp.stack(by_all), jnp.stack(by_fsdp)]).astype(jnp.int32)
        terms_a, downs_a = weight_terms(side_near, come_side, right_a, come_right_a, orders_a, None, None)
        terms_b, downs_b = weight_terms(side_near, come_side, right_b, come_right_b, orders_b, dy1_low, come_low)
        dattn_all, terms_b, downs_b = lax.optimization_barrier((dattn_all, terms_b, downs_b))
        qkv_arrays = [qkv, swapped(qkv, "core", 2, 1)]
        terms_a = [terms_a[0]] + [swapped(terms_a[e], "chip", nchip, e) for e in range(1, nchip)]
        terms_b = lax.all_to_all(terms_b, "chip", 0, 0, tiled=True)
        downs = [lax.psum_scatter(v, "z", scatter_dimension=0, tiled=True)[0] for v in (downs_a, downs_b)]
    else:
        chunk = lambda v, w: v.reshape(rows, 2, 3, w // 2)
        ra, rb = chunk(right_a, wa), chunk(right_b, wb)
        part = lambda i: jnp.concatenate([ra[:, :, i].reshape(rows, wa), rb[:, :, i].reshape(rows, wb)], axis=1)
        normed_two = jnp.stack([side_near[:, :HALF].reshape(rows, D // 256, 128), side_far[:, :HALF].reshape(rows, D // 256, 128)], axis=2).reshape(rows, D)
        terms = jnp.concatenate(
            [dot(attn3[0], dy1_low, TN), dot(normed_two, part(0), TN), dot(normed_two, part(1), TN), dot(og, part(2), TN)], axis=1
        ).astype(BF)
        share = lax.psum_scatter(terms, CTX, scatter_dimension=0, tiled=True)
        share = lax.psum_scatter(share, "z", scatter_dimension=0, tiled=True).astype(F32)
        out_share, gate_share, down_share = share[:, :D], share[:, D : D + 2 * FF], share[:, D + 2 * FF :]

    (dqkv_own,) = attn_bwd(qT, kn, kT, vn, dattn_all, attnT, lse, opening, jlo, spos, spos, cosT, sinT, None, **everything)
    if fast:
        dqkv_own, terms_a, terms_b, downs = lax.optimization_barrier((dqkv_own, terms_a, terms_b, downs))

        share = jnp.concatenate(
            [sum(v.astype(F32) for v in terms_a).astype(BF), sum(terms_b[k].astype(F32) for k in range(nchip)).astype(BF)], axis=1
        )
        dqkv_term, share = lax.optimization_barrier((dqkv_own, share))
        share = lax.psum_scatter(share, "z", scatter_dimension=0, tiled=True)
    dqkv3 = exchange(dqkv_own.reshape(nctx, rows, 3 * W))
    if fast:
        dqkv3, downs = lax.optimization_barrier((dqkv3, downs))
        downs = jnp.concatenate(downs, axis=1).reshape(nchip, own, FF + D)
        down_share = downs[0].astype(F32) + sum(swapped(downs[e], "chip", nchip, e).astype(F32) for e in range(1, nchip))
        out_share, down_share = down_share[:, FF:], down_share[:, :FF]
    if not fast:
        dqkv3 = dqkv3.reshape(nctx, rows, 3, W).transpose(1, 2, 0, 3).reshape(1, rows, 3 * D)

    term = dot(normed_all, dqkv_term if fast else dqkv_own, TN).astype(BF).reshape(nctx, nz, own, 3 * W)
    if fast:

        def slot(d):
            return lax.dynamic_index_in_dim(term, z ^ d, 1, keepdims=False)

        terms = [slot(0)] + [swapped(slot(d), "z", nz, d) for d in range(1, nz)]
    else:
        term = lax.psum_scatter(term.transpose(1, 0, 2, 3), "z", scatter_dimension=0, tiled=True)[0]
    input_grad, first_value_grad, qkv_rows = tail(dqkv3, x, dy1, gain_one, pos, qkv_arrays, qkv_pieces, keep)
    if fast:
        input_grad, share, *terms = lax.optimization_barrier((input_grad, share, *terms))
        term = sum(t.astype(F32) for t in terms).astype(BF)
        share = share.astype(F32)
        gate_share = halves_of(share)
    qkv_share = exchange(term).reshape(nctx, own, 3, W).transpose(1, 2, 0, 3).reshape(own, 3 * D).astype(F32)

    gain_own = lax.dynamic_slice_in_dim(gains, at, own, 1)
    if fast:
        _, rows_a, rows_b = lax.optimization_barrier((dqkv3, rows_a, rows_b))
        gate_rows = jnp.concatenate([rows_a[:, :wa], rows_b[:, :wb], rows_a[:, wa:], rows_b[:, wb:]], axis=1)
    else:
        qkv_rows = lax.dynamic_slice_in_dim(qkv_arrays[0], at, own, 0)
        gate_rows = lax.dynamic_slice_in_dim(arrays[1], at, own, 0)
    gain_one_share = jnp.sum(qkv_rows.astype(F32) * qkv_share, axis=1) / gain_own[0]
    gain_two_share = jnp.sum(gate_rows.astype(F32) * gate_share, axis=1) / gain_own[1]
    return (
        mixed_out[None],
        input_grad[None],
        first_value_grad[None],
        gain_one_share,
        qkv_share,
        out_share,
        gain_two_share,
        gate_share,
        down_share,
    )


def solution(mesh):
    ctx, fsdp = mesh.devices.shape
    split = Mesh(mesh.devices.reshape(ctx // 2, 2, fsdp), ("chip", "core", "z"))
    rows3 = P("z", CTX, None)
    weight = P("z", None)
    every = ("chip", "core", "z")
    return jax.shard_map(
        body,
        mesh=split,
        in_specs=(rows3, rows3, rows3, P("z"), weight, weight, P("z"), weight, weight, weight, P("z", CTX)),
        out_specs=(rows3, rows3, rows3, P(every), P(every, None), P(every, None), P(every), P(every, None), P(every, None)),
        check_vma=False,
    )
```

```python
import jax
import jax.numpy as jnp
from jax import lax
from jax.experimental import pallas as pl
from jax.experimental.pallas import tpu as pltpu
from jax.sharding import Mesh, PartitionSpec as P

D = 1024
HEADS = 16
HEAD = 64
FF = 2816
PROMPT = 2048
EPS = 1e-05
BASE = 10000.0
LOG2E = 1.4426950408889634
NEG = -1e30
C2 = 0.125 * LOG2E
CTX = ("chip", "core")
BF = jnp.bfloat16
F32 = jnp.float32


def dot(a, b, dims):
    return lax.dot_general(a, b, (dims, ((), ())), preferred_element_type=F32)


NN = ((1,), (0,))
NT = ((1,), (1,))
TN = ((0,), (0,))


def chunked(first, stop, sizes, fn, c):
    for n in sizes:
        count = (stop - first) // n
        c = lax.fori_loop(0, count, lambda t, c, n=n, first=first: fn(first + t * n, c, n), c)
        first = first + count * n
    return c


def visible(i, j, rows, run, lo):
    key = j * run + lax.broadcasted_iota(jnp.int32, (rows, run), 0)
    query = i * run + lax.broadcasted_iota(jnp.int32, (rows, run), 1)
    return (key <= query) & (key >= lo)


def attn_fwd(qT, kn, vT, lo, jlo, opos, *, run, nprompt, base, count):
    W, S = qT.shape
    hl = W // HEAD
    keys = S if base + count > nprompt else nprompt * run
    full_sizes, own_sizes = (8, 4, 2, 1), (4, 2, 1)

    def kern(jlo_ref, opos_ref, q_ref, k_ref, v_ref, lo_ref, o_ref, of_ref, lse_ref, s_scr):
        i = pl.program_id(0) + base
        qs = [q_ref[h * HEAD : (h + 1) * HEAD, :] for h in range(hl)]
        full = jnp.minimum(i, nprompt)
        own = jlo_ref[i]
        total = full + (i + 1 - own)

        def fold(f, s):
            return f(s.reshape(s.shape[0] // 8, 8, run), axis=0)

        def score(t, tops, n, shift, masked):
            tops = list(tops)
            for u in range(n):
                j = t + u + shift
                at = pl.multiple_of(j * run, run)
                row = pl.multiple_of((t + u) * run, run)
                if masked:
                    vis = visible(i, j, run, run, lo_ref[...])
                for h in range(hl):
                    s = dot(k_ref[h, pl.ds(at, run), :], qs[h], NN)
                    if masked:
                        s = jnp.where(vis, s, NEG)
                    s_scr[h, pl.ds(row, run), :] = s
                    tops[h] = jnp.maximum(tops[h], fold(jnp.max, s))
            return tuple(tops)

        tops = tuple(jnp.full((8, run), NEG, F32) for _ in range(hl))
        tops = chunked(0, full, full_sizes, lambda t, c, n: score(t, c, n, 0, False), tops)
        tops = chunked(full, total, own_sizes, lambda t, c, n: score(t, c, n, own - full, True), tops)
        m = [jnp.max(tops[h], axis=0, keepdims=True) * C2 for h in range(hl)]

        def weigh(t, c, n, shift):
            c = list(c)
            for u in range(n):
                at = pl.multiple_of((t + u + shift) * run, run)
                row = pl.multiple_of((t + u) * run, run)
                for h in range(hl):
                    l, acc = c[h]
                    p = jnp.exp2(s_scr[h, pl.ds(row, run), :] * C2 - m[h])
                    l = l + fold(jnp.sum, p)
                    acc = acc + dot(v_ref[h * HEAD : (h + 1) * HEAD, pl.ds(at, run)], p.astype(BF), NN)
                    c[h] = (l, acc)
            return tuple(c)

        c = tuple((jnp.zeros((8, run), F32), jnp.zeros((HEAD, run), F32)) for _ in range(hl))
        c = chunked(0, full, full_sizes, lambda t, c, n: weigh(t, c, n, 0), c)
        c = chunked(full, total, own_sizes, lambda t, c, n: weigh(t, c, n, own - full), c)
        outs = []
        for h in range(hl):
            l8, acc = c[h]
            l = jnp.sum(l8, axis=0, keepdims=True)
            o = acc / l
            of_ref[h * HEAD : (h + 1) * HEAD, :] = o
            lse_ref[h, :, :] = m[h] + jnp.log2(l)
            outs.append(o)
        o = jnp.concatenate(outs, axis=0) if hl > 1 else outs[0]
        o_ref[...] = o.T.astype(BF)

    rows = count * run
    return pl.pallas_call(
        kern,
        out_shape=(jax.ShapeDtypeStruct((rows, W), BF), jax.ShapeDtypeStruct((W, rows), F32), jax.ShapeDtypeStruct((hl, 1, rows), F32)),
        grid_spec=pltpu.PrefetchScalarGridSpec(
            num_scalar_prefetch=2,
            grid=(count,),
            in_specs=[
                pl.BlockSpec((W, run), lambda i, *_: (0, i + base)),
                pl.BlockSpec((hl, keys, HEAD), lambda i, *_: (0, 0, 0)),
                pl.BlockSpec((W, keys), lambda i, *_: (0, 0)),
                pl.BlockSpec((1, run), lambda i, *_: (0, i + base)),
            ],
            out_specs=[
                pl.BlockSpec((run, W), lambda i, jl, op: (op[i + base], 0)),
                pl.BlockSpec((W, run), lambda i, *_: (0, i)),
                pl.BlockSpec((hl, 1, run), lambda i, *_: (0, 0, i)),
            ],
            scratch_shapes=[pltpu.VMEM((hl, keys, run), F32)],
        ),
        compiler_params=params(),
        cost_estimate=cost(20 * rows * keys * W // 2, 12 * S * W, rows * keys // 2),
        name="attention_forward",
    )(jlo, opos, qT, kn, vT, lo)


def attn_bwd(qT, kn, kT, vn, don, of, lse, lo, jlo, spos, opos, cosT, sinT, sums, *, run, nprompt, base, count):
    W, S = qT.shape
    hl = W // HEAD
    hh = HEAD // 2
    keys = S if base + count > nprompt else nprompt * run
    later = base > 0
    P_ = nprompt * run
    full_sizes, own_sizes = (4, 2, 1), (2, 1)

    def unrotate(g, cos, sin):
        parts = []
        for h in range(hl):
            a = g[h * HEAD : h * HEAD + hh]
            b = g[h * HEAD + hh : (h + 1) * HEAD]
            parts += [a * cos + b * sin, b * cos - a * sin]
        return jnp.concatenate(parts, axis=0)

    def kern(jlo_ref, spos_ref, opos_ref, q_ref, k_ref, kT_ref, v_ref, do_ref, of_ref, lse_ref, lo_ref, cos_ref, sin_ref, *rest):
        if sums is not None:
            sk_ref, sv_ref = rest[:2]
            rest = rest[2:]
        if later:
            g_ref, ok_ref, ov_ref, dkT, dvT = rest
        else:
            g_ref, dkT, dvT = rest
        i = pl.program_id(0) + base

        @pl.when(pl.program_id(0) == 0)
        def _():
            if sums is not None:
                dkT[...] = sk_ref[...]
                dvT[...] = sv_ref[...]
            else:
                dkT[...] = jnp.zeros_like(dkT)
                dvT[...] = jnp.zeros_like(dvT)

        doT = do_ref[...].T
        dof = doT.astype(F32)
        qs = [q_ref[h * HEAD : (h + 1) * HEAD, :] for h in range(hl)]
        dos = [doT[h * HEAD : (h + 1) * HEAD, :] for h in range(hl)]
        delta = [
            jnp.sum(dof[h * HEAD : (h + 1) * HEAD] * of_ref[h * HEAD : (h + 1) * HEAD, :], axis=0, keepdims=True) for h in range(hl)
        ]
        ls = [lse_ref[h, :, :] for h in range(hl)]

        def tile(j, carry, n, masked):
            kb = n * run
            at = pl.multiple_of(j * run, run)
            if masked:
                vis = visible(i, j, kb, run, lo_ref[...])
            out = []
            for h in range(hl):
                hs = slice(h * HEAD, (h + 1) * HEAD)
                s = dot(k_ref[h, pl.ds(at, kb), :], qs[h], NN)
                p = jnp.exp2(s * C2 - ls[h])
                if masked:
                    p = jnp.where(vis, p, 0.0)
                dp = dot(v_ref[h, pl.ds(at, kb), :], dos[h], NN)
                ds = (p * (dp - delta[h])).astype(BF)
                dvT[hs, pl.ds(at, kb)] += dot(dos[h], p.astype(BF), NT)
                dkT[hs, pl.ds(at, kb)] += dot(qs[h], ds, NT)
                out.append(carry[h] + dot(kT_ref[hs, pl.ds(at, kb)], ds, NN))
            return tuple(out)

        c = tuple(jnp.zeros((HEAD, run), F32) for _ in range(hl))
        c = chunked(0, jnp.minimum(i, nprompt), full_sizes, lambda j, c, n: tile(j, c, n, False), c)
        c = chunked(jlo_ref[i], i + 1, own_sizes, lambda j, c, n: tile(j, c, n, True), c)
        dq = (jnp.concatenate(c, axis=0) if hl > 1 else c[0]) * 0.125

        def turned(g, b):
            at = pl.multiple_of(b * run, run)
            return unrotate(g, cos_ref[:, pl.ds(at, run)], sin_ref[:, pl.ds(at, run)]).T.astype(BF)

        row = pl.multiple_of(opos_ref[i] * run, run)
        g_ref[pl.ds(row, run), :W] = turned(dq, i)

        @pl.when(pl.program_id(0) == count - 1)
        def _():
            def finish(b, _):
                at = pl.multiple_of(b * run, run)
                row = pl.multiple_of(opos_ref[b] * run, run)
                g_ref[pl.ds(row, run), W : 2 * W] = turned(dkT[:, pl.ds(at, run)] * 0.125, b)
                g_ref[pl.ds(row, run), 2 * W :] = (dvT[:, pl.ds(at, run)] * 0.5).T.astype(BF)
                return 0

            lax.fori_loop(base, base + count, finish, 0)
            if later:
                ok_ref[...] = dkT[:, :P_]
                ov_ref[...] = dvT[:, :P_]

    full = lambda *s: pl.BlockSpec(s, lambda i, *_: (0,) * len(s))
    rows = count * run
    sum_shape = jax.ShapeDtypeStruct((W, P_), F32)
    return pl.pallas_call(
        kern,
        out_shape=(jax.ShapeDtypeStruct((rows, 3 * W), BF),) + ((sum_shape, sum_shape) if later else ()),
        grid_spec=pltpu.PrefetchScalarGridSpec(
            num_scalar_prefetch=3,
            grid=(count,),
            in_specs=[
                pl.BlockSpec((W, run), lambda i, *_: (0, i + base)),
                full(hl, keys, HEAD),
                full(W, keys),
                full(hl, keys, HEAD),
                pl.BlockSpec((run, W), lambda i, jl, sp, op: (sp[i + base], 0)),
                pl.BlockSpec((W, run), lambda i, *_: (0, i)),
                pl.BlockSpec((hl, 1, run), lambda i, *_: (0, 0, i)),
                pl.BlockSpec((1, run), lambda i, *_: (0, i + base)),
                full(hh, keys),
                full(hh, keys),
            ]
            + ([full(W, P_)] * 2 if sums is not None else []),
            out_specs=[full(rows, 3 * W)] + ([full(W, P_)] * 2 if later else []),
            scratch_shapes=[pltpu.VMEM((W, keys), F32)] * 2,
        ),
        compiler_params=params(),
        cost_estimate=cost(32 * rows * keys * W // 2, 24 * S * W, rows * keys // 2),
        name="attention_backward",
    )(jlo, spos, opos, qT, kn, kT, vn, don, of, lse, lo, cosT, sinT, *(sums or ()))


def cost(flops, nbytes, trans=0):
    return pl.CostEstimate(flops=int(flops), bytes_accessed=int(nbytes), transcendentals=int(trans))


def whole(*shape):
    return pl.BlockSpec(shape, lambda *_: (0,) * len(shape))


ANY = pl.BlockSpec(memory_space=pl.ANY)


def params():
    return pltpu.CompilerParams(vmem_limit_bytes=56 << 20)


def project(x, gain, w, vf, cos, sin, blk, *, run):
    S = x.shape[0]
    W = vf.shape[2]
    hl = W // HEAD
    nb = S // run
    per = nb // vf.shape[0]
    hh = HEAD // 2

    pair = 2

    def kern(blk_ref, x_ref, g_ref, w_ref, vf_ref, c_ref, s_ref, n_o, q_o, kT_o, vT_o, kn_o, vn_o):
        xf = x_ref[...].astype(F32)
        inv = lax.rsqrt(jnp.mean(xf * xf, axis=1, keepdims=True) + EPS)
        n1 = (xf * inv * g_ref[...]).astype(BF)
        n_o[...] = n1
        t = dot(w_ref[...], n1, NT)
        vT = vf_ref[0].astype(F32).T
        for r in range(pair):
            at = pl.ds(pl.multiple_of(blk_ref[pl.program_id(0) * pair + r] * run, run), run)
            rows = slice(r * run, (r + 1) * run)
            c = c_ref[:, at]
            s = s_ref[:, at]

            def rope(base):
                parts = []
                for h in range(hl):
                    a = t[base + h * HEAD : base + h * HEAD + hh, rows]
                    b = t[base + h * HEAD + hh : base + (h + 1) * HEAD, rows]
                    parts += [a * c - b * s, b * c + a * s]
                return jnp.concatenate(parts, axis=0)

            q_o[:, at] = rope(0).astype(BF)
            k = rope(W)
            kT_o[:, at] = k.astype(BF)
            v = 0.5 * t[2 * W :, rows] + 0.5 * vT[:, rows]
            vT_o[:, at] = v.astype(BF)
            for h in range(hl):
                kn_o[h, at, :] = k[h * HEAD : (h + 1) * HEAD].T.astype(BF)
                vn_o[h, at, :] = v[h * HEAD : (h + 1) * HEAD].T.astype(BF)

    T = jax.ShapeDtypeStruct((W, S), BF)
    N = jax.ShapeDtypeStruct((hl, S, HEAD), BF)
    rb = pl.BlockSpec((pair * run, D), lambda r, b: (r, 0))
    half = per // pair
    return pl.pallas_call(
        kern,
        out_shape=(jax.ShapeDtypeStruct((S, D), BF), T, T, T, N, N),
        grid_spec=pltpu.PrefetchScalarGridSpec(
            num_scalar_prefetch=1,
            grid=(nb // pair,),
            in_specs=[rb, whole(1, D), whole(3 * W, D), pl.BlockSpec((1, pair * run, W), lambda r, b: (r // half, r % half, 0)), whole(hh, S), whole(hh, S)],
            out_specs=[rb, whole(W, S), whole(W, S), whole(W, S), whole(hl, S, HEAD), whole(hl, S, HEAD)],
        ),
        compiler_params=params(),
        cost_estimate=cost(6 * S * D * W, 4 * S * D + 12 * S * W),
        name="project_qkv",
    )(blk, x, gain, w, vf, cos, sin)


def load_pieces(pieces, refs, pos_ref, dst, sems):
    copies = []
    for ref, row, rows, col, place, sem in pieces:
        at = pl.multiple_of(pos_ref[place], rows)
        copies.append(
            pltpu.make_async_copy(
                refs[ref].at[pl.ds(row, rows), pl.ds(col, dst.shape[1])], dst.at[pl.ds(at, rows), :], sems.at[sem]
            )
        )
    return copies


CUT = 1536
HALF = D // 2


def column_pieces(pieces, first, width):
    return [(ref, row, size, col + first, place, sem) for ref, row, size, col, place, sem in pieces]


def feed_forward(start, carried, attn3, x, og, gain, pos, arrays, out_pieces, gate_pieces, down_pieces, keep):
    n, rows, W = attn3.shape
    lo, hi = (0, CUT) if start else (CUT, FF)
    width = hi - lo
    FC = width // 2
    nsem = len(out_pieces) + 2 * len(gate_pieces) + len(down_pieces)
    na = len(arrays)
    last = pos.shape[0]
    ncarry = len(carried)

    def kern(pos_ref, a_ref, x_ref, og_ref, g_ref, *rest):
        refs = rest[:na]
        rest = rest[na:]
        cin, rest = rest[:ncarry], rest[ncarry:]
        if start:
            r_o, near_o, far_o, wr_o, y_o, n2_o, m_o, acc_o = rest[:8]
            wo, wg, wu, wd, al, sems = rest[8:]
        else:
            mixed_o, r_o, low_o, dy_o, da_o, wr_o = rest[:6]
            wo, wg, wu, wd, acc_m, acc_n, sems = rest[6:]
        f = pl.program_id(0)

        def sides(ref, place):
            for out, c in ((near_o, pos_ref[last - 2]), (far_o, 1 - pos_ref[last - 2])):
                for e in range(D // 256):
                    out[:, place + e * 128 : place + (e + 1) * 128] = ref[:, pl.ds(pl.multiple_of((2 * e + c) * 128, 128), 128)]

        @pl.when(f == 0)
        def _():
            ng = len(gate_pieces)
            first = load_pieces(out_pieces, refs, pos_ref, wo, sems)
            second = load_pieces(column_pieces(gate_pieces, lo, 0), refs, pos_ref, wg, sems)
            second += load_pieces([(r, a, b, c + FF + lo, p, s + nsem - ng) for r, a, b, c, p, s in renumber(gate_pieces)], refs, pos_ref, wu, sems)
            third = load_pieces(column_pieces(down_pieces, lo, 0), refs, pos_ref, wd, sems)
            for cp in (first + second + third) if start else (second + third + first):
                cp.start()
            if start:
                for i in range(n):
                    al[:, i * W : (i + 1) * W] = a_ref[i]
                sides(og_ref, 2 * HALF)
                sides(al, HALF)
                for cp in first:
                    cp.wait()
                y = x_ref[...].astype(F32) + dot(al[...], wo[...], NN)
                y_o[...] = y
                inv = lax.rsqrt(jnp.mean(y * y, axis=1, keepdims=True) + EPS)
                n2_o[...] = (y * inv * g_ref[...]).astype(BF)
                sides(n2_o, 0)
                m_o[...] = y
                acc_o[...] = jnp.zeros_like(acc_o)
            else:
                acc_m[...] = cin[2][...]
                acc_n[...] = cin[3][...]
            for cp in second + third:
                cp.wait()
            if not start:
                for cp in first:
                    cp.wait()

        n2 = n2_o if start else cin[1]
        am = m_o if start else acc_m
        an = acc_o if start else acc_n
        c0 = pl.multiple_of(f * FC, 128)
        a = n2[...]
        g = dot(a, wg[:, pl.ds(c0, FC)], NN)
        u = dot(a, wu[:, pl.ds(c0, FC)], NN)
        dh = dot(og_ref[...], wd[:, pl.ds(c0, FC)], NN)
        sg = jax.nn.sigmoid(g)
        silu = g * sg
        hid = (silu * u).astype(BF)
        dg = (dh * u * sg * (1.0 + g * (1.0 - sg))).astype(BF)
        du = (dh * silu).astype(BF)
        r_o[:, :FC] = dg
        r_o[:, FC : 2 * FC] = du
        r_o[:, 2 * FC :] = hid
        am[...] += dot(hid, wd[:, pl.ds(c0, FC)], NT)
        an[...] += dot(dg, wg[:, pl.ds(c0, FC)], NT) + dot(du, wu[:, pl.ds(c0, FC)], NT)

        @pl.when(f == 1)
        def _():
            at = pl.multiple_of(pos_ref[last - 1], keep)
            wr_o[:, :width] = wg[pl.ds(at, keep), :]
            wr_o[:, width:] = wu[pl.ds(at, keep), :]
            if not start:
                mixed_o[...] = am[...].astype(BF)
                y = cin[0][...]
                inv = lax.rsqrt(jnp.mean(y * y, axis=1, keepdims=True) + EPS)
                xh = y * inv
                t = an[...] * g_ref[...]
                dy = og_ref[...].astype(F32) + inv * (t - xh * jnp.mean(t * xh, axis=1, keepdims=True))
                dy_o[...] = dy
                low = dy.astype(BF)
                low_o[...] = low
                da = dot(low, wo[...], NT).astype(BF)
                for i in range(n):
                    da_o[i] = da[:, i * W : (i + 1) * W]

    wide = jax.ShapeDtypeStruct((rows, D), F32)
    side = jax.ShapeDtypeStruct((rows, 3 * HALF), BF)
    low = jax.ShapeDtypeStruct((rows, D), BF)
    right = jax.ShapeDtypeStruct((rows, 3 * width), BF)
    own_rows = jax.ShapeDtypeStruct((keep, 2 * width), BF)
    rspec = pl.BlockSpec((rows, 3 * FC), lambda f, *_: (0, f))
    full = whole(rows, D)
    if start:
        outs = (right, side, side, own_rows, wide, low, wide, wide)
        specs = [rspec, whole(rows, 3 * HALF), whole(rows, 3 * HALF), whole(keep, 2 * width), full, full, full, full]
        extra = [pltpu.VMEM((rows, D), BF)]
    else:
        outs = (low, right, low, wide, jax.ShapeDtypeStruct((n, rows, W), BF), own_rows)
        specs = [full, rspec, full, full, whole(n, rows, W), whole(keep, 2 * width)]
        extra = [pltpu.VMEM((rows, D), F32)] * 2
    return pl.pallas_call(
        kern,
        out_shape=outs,
        grid_spec=pltpu.PrefetchScalarGridSpec(
            num_scalar_prefetch=1,
            grid=(2,),
            in_specs=[whole(n, rows, W) if start else ANY, full if start else ANY, full, whole(1, D)] + [ANY] * na + [full] * ncarry,
            out_specs=specs,
            scratch_shapes=[
                pltpu.VMEM((D, D), BF),
                pltpu.VMEM((D, width), BF),
                pltpu.VMEM((D, width), BF),
                pltpu.VMEM((D, width), BF),
                *extra,
                pltpu.SemaphoreType.DMA((nsem,)),
            ],
        ),
        compiler_params=params(),
        cost_estimate=cost(4 * rows * D * (D + 6 * width), 2 * D * (D + 3 * width) + 2 * rows * (14 * D + 3 * width)),
        name="feed_forward_start" if start else "feed_forward_end",
    )(pos, attn3, x, og, gain, *arrays, *carried)


def renumber(pieces):
    return [(r, a, b, c, p, i) for i, (r, a, b, c, p, _) in enumerate(pieces)]


def tail(dqkv3, x, dy1, gain, pos, arrays, pieces, keep):
    n, rows, W3 = dqkv3.shape
    W = W3 // 3
    na = len(arrays)
    group = max(1, len(pieces) // 4)

    def kern(pos_ref, d_ref, x_ref, dy_ref, g_ref, *rest):
        refs = rest[:na]
        ig_o, fv_o, wr_o = rest[na : na + 3]
        w, dn, sems = rest[na + 3 :]
        copies = load_pieces(pieces, refs, pos_ref, w, sems)
        for cp in copies:
            cp.start()
        if n > 1:
            d = jnp.concatenate([d_ref[i, :, p * W : (p + 1) * W] for p in range(3) for i in range(n)], axis=1)
        else:
            d = d_ref[0]
        fv_o[...] = d[:, 2 * D :].astype(F32)
        for cp in copies:
            cp.wait()
        t = dot(d, w[...], NT)
        wr_o[...] = w[pl.ds(pl.multiple_of(pos_ref[pos.shape[0] - 1], keep), keep), :]
        xf = x_ref[...].astype(F32)
        inv = lax.rsqrt(jnp.mean(xf * xf, axis=1, keepdims=True) + EPS)
        xh = xf * inv
        t = t * g_ref[...]
        ig_o[...] = dy_ref[...] + inv * (t - xh * jnp.mean(t * xh, axis=1, keepdims=True))

    o = jax.ShapeDtypeStruct((rows, D), F32)
    return pl.pallas_call(
        kern,
        out_shape=(o, o, jax.ShapeDtypeStruct((keep, 3 * D), BF)),
        grid_spec=pltpu.PrefetchScalarGridSpec(
            num_scalar_prefetch=1,
            grid=(1,),
            in_specs=[whole(n, rows, W3), whole(rows, D), whole(rows, D), whole(1, D)] + [ANY] * na,
            out_specs=[whole(rows, D), whole(rows, D), whole(keep, 3 * D)],
            scratch_shapes=[pltpu.VMEM((D, 3 * D), BF), pltpu.VMEM((rows, D), F32), pltpu.SemaphoreType.DMA((len(pieces),))],
        ),
        compiler_params=params(),
        cost_estimate=cost(6 * rows * D * D, 6 * D * D + rows * D * 20),
        name="input_gradient",
    )(pos, dqkv3, x, dy1, gain, *arrays)


def weight_terms(near, far, r_near, r_far, orders, low, low_far):
    rows = near.shape[0]
    width = r_near.shape[1] // 3
    FC = width // 2
    nb = orders.shape[1]
    own = HALF // nb
    n = 4
    more = low is not None
    cols = width + (D if more else 0)

    def kern(o_ref, na, fa, ra, rb, *rest):
        if more:
            nd, fd = rest[:2]
            rest = rest[2:]
        t_o, d_o, lt0, lt = rest
        f = pl.program_id(0)

        @pl.when(f == 0)
        def _():
            for i, side in ((0, na), (1, fa)):
                for p in range(3):
                    lt0[p, :, i * rows : (i + 1) * rows] = side[:, p * HALF : (p + 1) * HALF].T
            for p in range(3):
                for b in range(nb):
                    at = o_ref[min(p, 1), b]
                    lt[p, b * own : (b + 1) * own, :] = lt0[p, pl.ds(pl.multiple_of(at * own, own), own), :]

        def put(p, a, b, out, place, size):
            t = dot(lt[p, :, :rows], a, NN) + dot(lt[p, :, rows:], b, NN)
            for e in range(n):
                out[e, :, pl.ds(place, size)] = t[e * HALF // n : (e + 1) * HALF // n].astype(BF)

        put(0, ra[:, : 2 * FC], rb[:, : 2 * FC], t_o, pl.multiple_of(2 * FC * f, 128), 2 * FC)
        put(2, ra[:, 2 * FC :], rb[:, 2 * FC :], d_o, pl.multiple_of(FC * f, 128), FC)
        if more:

            @pl.when(f == 1)
            def _():
                put(1, nd[...], fd[...], d_o, width, D)

    rb = pl.BlockSpec((rows, 3 * FC), lambda f, *_: (0, f))
    return pl.pallas_call(
        kern,
        out_shape=(jax.ShapeDtypeStruct((n, HALF // n, 2 * width), BF), jax.ShapeDtypeStruct((n, HALF // n, cols), BF)),
        grid_spec=pltpu.PrefetchScalarGridSpec(
            num_scalar_prefetch=1,
            grid=(2,),
            in_specs=[whole(rows, 3 * HALF)] * 2 + [rb] * 2 + ([whole(rows, D)] * 2 if more else []),
            out_specs=[whole(n, HALF // n, 2 * width), whole(n, HALF // n, cols)],
            scratch_shapes=[pltpu.VMEM((3, HALF, 2 * rows), BF)] * 2,
        ),
        compiler_params=params(),
        cost_estimate=cost(4 * rows * HALF * (cols + 2 * width), 2 * (2 * rows + HALF) * (cols + 2 * width) + 12 * rows * HALF),
        name="weight_terms",
    )(orders, near, far, r_near, r_far, *((low, low_far) if more else ()))


def exchange(v):
    return lax.all_to_all(v, CTX, 0, 0, tiled=True)


def swapped(v, axes, size, mask):
    return lax.ppermute(v, axes, [(i, i ^ mask) for i in range(size)])


def gathered(v, axes, size, index):
    parts = [v] + [swapped(v, axes, size, s) for s in range(1, size)]
    return jnp.stack([lax.select_n(index ^ a, *parts) for a in range(size)])


def half_rows(w, core):
    half = w.shape[0] // 2
    return lax.dynamic_slice_in_dim(w, core * half, half, 0)


def body(tokens_in, value_first, out_grad, gain_attn, w_qkv, w_out, gain_mlp, w_gate_up, w_down, cont_lengths, row_token):
    x = tokens_in[0]
    og = out_grad[0]
    rows = x.shape[0]
    nchip = lax.axis_size("chip")
    nctx = lax.axis_size(CTX)
    nz = lax.axis_size("z")
    me = lax.axis_index(CTX)
    chip = lax.axis_index("chip")
    core = lax.axis_index("core")
    z = lax.axis_index("z")
    fast = nctx == 8 and nz == 4
    S = rows * nctx
    W = D // nctx
    run = PROMPT // nctx
    nb = S // run
    nprompt = PROMPT // run
    shard = D // nz
    own = D // (nctx * nz)
    at = (me * nz + z) * own
    keep = own if fast else 16

    x_all = lax.all_gather(x, CTX, axis=0, tiled=True)
    w_own = lax.dynamic_index_in_dim(w_qkv.reshape(shard, 3, nctx, W), me, 2, keepdims=False).reshape(shard, 3 * W)
    gains = jnp.stack([gain_attn, gain_mlp])
    runs = (row_token[0, ::run] // run).astype(BF)
    runs = jnp.pad(runs[None], ((0, 15), (0, W - runs.shape[0])))
    vf = jnp.concatenate([value_first[0].reshape(rows, nctx, W).transpose(1, 0, 2), jnp.broadcast_to(runs, (nctx, 16, W))], axis=1)
    vf = exchange(vf)
    if fast:
        pay = jnp.concatenate([w_own, jnp.pad(gains, ((0, 14), (0, 3 * W - shard)))], axis=0)
        pay = gathered(pay, "z", nz, z)
    else:
        w_own = lax.all_gather(w_own, "z", axis=0, tiled=True).T
        gains = lax.all_gather(gains, "z", axis=1, tiled=True).astype(F32)
        gain_one, gain_two = gains[0:1], gains[1:2]
        blk = vf[:, rows, : nb // nctx].astype(jnp.int32).reshape(nb)

    lengths = cont_lengths[0]
    count = jnp.arange(lengths.shape[0], dtype=jnp.int32)
    starts = PROMPT + jnp.sum(jnp.where(count[:, None] < count[None, :], lengths[:, None], 0), axis=0)
    token = jnp.arange(S, dtype=jnp.int32)
    passed = token[None, :] >= starts[:, None]
    opening = jnp.max(jnp.where(passed, starts[:, None], 0), axis=0).astype(jnp.int32)
    position = jnp.where(opening > 0, PROMPT + token - opening, token)
    freq = BASE ** (-(jnp.arange(HEAD // 2, dtype=F32) * 2.0 / HEAD))
    angles = freq[:, None] * position.astype(F32)[None, :]
    cosT = jnp.cos(angles)
    sinT = jnp.sin(angles)
    block = jnp.arange(nb, dtype=jnp.int32)
    jlo = jnp.where(block < nprompt, block, opening[::run] // run).astype(jnp.int32)
    opening = opening[None, :]

    if fast:
        w_own = pay[:, :shard].reshape(D, 3 * W).T
        gains = pay[:, shard : shard + 2, :shard].transpose(1, 0, 2).reshape(2, D).astype(F32)
        gain_one, gain_two = gains[0:1], gains[1:2]
        blk = vf[:, rows, : nb // nctx].astype(jnp.int32).reshape(nb)
    spos = jnp.sum(jnp.where(blk[None, :] == block[:, None], block[None, :], 0), axis=1).astype(jnp.int32)

    if fast:
        piece = shard // nctx
        mine = jnp.concatenate([lax.dynamic_slice_in_dim(w, me * piece, piece, 0) for w in (w_out, w_gate_up)], axis=1)
        near = jnp.concatenate([swapped(mine, "z", nz, d) for d in range(1, nz)], axis=0)
        down = half_rows(w_down, core)
        qkv = half_rows(w_qkv, core)
        x_all, near, vf, w_own, gains, gain_one, blk, spos, cosT, sinT, jlo, down, qkv = lax.optimization_barrier(
            (x_all, near, vf, w_own, gains, gain_one, blk, spos, cosT, sinT, jlo, down, qkv)
        )
        planes = [near] + [swapped(near, "chip", nchip, e) for e in range(1, nchip)]
        down = lax.all_gather(down, "z", axis=0, tiled=True)
        pos = [z * shard]
        out_pieces, gate_pieces = [[(i, 0, shard, 0, 0, i)] for i in range(2)]
        sem = 2
        for f in range(2):
            for e in range(nchip):
                for d in range(1, nz):
                    pos.append((z ^ d) * shard + ((chip ^ e) * 2 + (core ^ f)) * piece)
                    ref = 2 + f * nchip + e
                    out_pieces.append((ref, (d - 1) * piece, piece, 0, len(pos) - 1, sem))
                    gate_pieces.append((ref, (d - 1) * piece, piece, D, len(pos) - 1, sem + 1))
                    sem += 2
        down_pieces = []
        half = shard // 2
        for k in range(nz):
            for f in range(2):
                pos.append(k * shard + (core ^ f) * half)
                down_pieces.append((2 + 2 * nchip + f, k * half, half, 0, len(pos) - 1, sem))
                sem += 1
        qkv_pieces = []
        for d in range(nz):
            for f in range(2):
                pos.append(d * shard + (core ^ f) * half)
                qkv_pieces.append((f, d * half, half, 0, len(pos) - 1, len(qkv_pieces)))
        pos = jnp.stack(pos + [core, at]).astype(jnp.int32)
    else:
        arrays = [lax.all_gather(w, "z", axis=0, tiled=True) for w in (w_out, w_gate_up, w_down)]
        qkv_arrays = [lax.all_gather(w_qkv, "z", axis=0, tiled=True)]
        pos = jnp.zeros((3,), jnp.int32)
        out_pieces, gate_pieces, down_pieces = [[(i, 0, D, 0, 0, i)] for i in range(3)]
        qkv_pieces = [(0, 0, D, 0, 0, 0)]

    normed_all, qT, kT, vT, kn, vn = project(x_all, gain_one, w_own, vf, cosT, sinT, blk, run=run)
    everything = {"run": run, "nprompt": nprompt, "base": 0, "count": nb}
    attn_all, attnT, lse = attn_fwd(qT, kn, vT, opening, jlo, spos, **everything)
    if fast:
        attn_all, qkv, down, *planes = lax.optimization_barrier((attn_all, qkv, down, *planes))
        qkv = lax.all_gather(qkv, "z", axis=0, tiled=True)
        arrays = [w_out, w_gate_up] + planes + [swapped(p, "core", 2, 1) for p in planes] + [down, swapped(down, "core", 2, 1)]
    attn3 = exchange(attn_all.reshape(nctx, rows, W))
    if not fast:
        attn3 = attn3.transpose(1, 0, 2).reshape(1, rows, D)
    pieces = (out_pieces, gate_pieces, down_pieces)
    right_a, side_near, side_far, rows_a, *carried = feed_forward(True, (), attn3, x, og, gain_two, pos, arrays, *pieces, keep)
    if fast:
        come_right_a = swapped(right_a, "core", 2, 1)
        come_side = swapped(side_far, "core", 2, 1)
    mixed_out, right_b, dy1_low, dy1, dattn3, rows_b = feed_forward(False, carried, attn3, x, og, gain_two, pos, arrays, *pieces, keep)
    if fast:
        dattn3, right_b, dy1_low, qkv, come_right_a, come_side = lax.optimization_barrier(
            (dattn3, right_b, dy1_low, qkv, come_right_a, come_side)
        )
    else:
        dattn3 = dattn3.reshape(rows, nctx, W).transpose(1, 0, 2)
    dattn_all = exchange(dattn3).reshape(S, W)
    wa, wb = CUT, FF - CUT

    def halves_of(v):
        a = v[:, : 2 * wa].reshape(v.shape[0], 2, 2, wa // 2)
        b = v[:, 2 * wa : 2 * FF].reshape(v.shape[0], 2, 2, wb // 2)
        return jnp.concatenate([v_.reshape(v.shape[0], -1) for i in range(2) for v_ in (a[:, :, i], b[:, :, i])], axis=1)

    if fast:
        come_right_b = swapped(right_b, "core", 2, 1)
        come_low = swapped(dy1_low, "core", 2, 1)
        by_chip = [(chip ^ e) * nz + k for e in range(nchip) for k in range(nz)]
        by_all = [k + 0 * chip for k in range(nchip * nz)]
        by_fsdp = [(chip ^ e) * nz + k for k in range(nz) for e in range(nchip)]
        orders_a = jnp.stack([jnp.stack(by_chip), jnp.stack(by_fsdp)]).astype(jnp.int32)
        orders_b = jnp.stack([jnp.stack(by_all), jnp.stack(by_fsdp)]).astype(jnp.int32)
        terms_a, downs_a = weight_terms(side_near, come_side, right_a, come_right_a, orders_a, None, None)
        terms_b, downs_b = weight_terms(side_near, come_side, right_b, come_right_b, orders_b, dy1_low, come_low)
        dattn_all, terms_b, downs_b = lax.optimization_barrier((dattn_all, terms_b, downs_b))
        qkv_arrays = [qkv, swapped(qkv, "core", 2, 1)]
        terms_a = [terms_a[0]] + [swapped(terms_a[e], "chip", nchip, e) for e in range(1, nchip)]
        terms_b = lax.all_to_all(terms_b, "chip", 0, 0, tiled=True)
        downs = [lax.psum_scatter(v, "z", scatter_dimension=0, tiled=True)[0] for v in (downs_a, downs_b)]
    else:
        chunk = lambda v, w: v.reshape(rows, 2, 3, w // 2)
        ra, rb = chunk(right_a, wa), chunk(right_b, wb)
        part = lambda i: jnp.concatenate([ra[:, :, i].reshape(rows, wa), rb[:, :, i].reshape(rows, wb)], axis=1)
        normed_two = jnp.stack([side_near[:, :HALF].reshape(rows, D // 256, 128), side_far[:, :HALF].reshape(rows, D // 256, 128)], axis=2).reshape(rows, D)
        terms = jnp.concatenate(
            [dot(attn3[0], dy1_low, TN), dot(normed_two, part(0), TN), dot(normed_two, part(1), TN), dot(og, part(2), TN)], axis=1
        ).astype(BF)
        share = lax.psum_scatter(terms, CTX, scatter_dimension=0, tiled=True)
        share = lax.psum_scatter(share, "z", scatter_dimension=0, tiled=True).astype(F32)
        out_share, gate_share, down_share = share[:, :D], share[:, D : D + 2 * FF], share[:, D + 2 * FF :]

    (dqkv_own,) = attn_bwd(qT, kn, kT, vn, dattn_all, attnT, lse, opening, jlo, spos, spos, cosT, sinT, None, **everything)
    if fast:
        dqkv_own, terms_a, terms_b, downs = lax.optimization_barrier((dqkv_own, terms_a, terms_b, downs))

        share = jnp.concatenate(
            [sum(v.astype(F32) for v in terms_a).astype(BF), sum(terms_b[k].astype(F32) for k in range(nchip)).astype(BF)], axis=1
        )
        dqkv_term, share = lax.optimization_barrier((dqkv_own, share))
        share = lax.psum_scatter(share, "z", scatter_dimension=0, tiled=True)
    dqkv3 = exchange(dqkv_own.reshape(nctx, rows, 3 * W))
    if fast:
        dqkv3, downs = lax.optimization_barrier((dqkv3, downs))
        downs = jnp.concatenate(downs, axis=1).reshape(nchip, own, FF + D)
        down_share = downs[0].astype(F32) + sum(swapped(downs[e], "chip", nchip, e).astype(F32) for e in range(1, nchip))
        out_share, down_share = down_share[:, FF:], down_share[:, :FF]
    if not fast:
        dqkv3 = dqkv3.reshape(nctx, rows, 3, W).transpose(1, 2, 0, 3).reshape(1, rows, 3 * D)

    term = dot(normed_all, dqkv_term if fast else dqkv_own, TN).astype(BF).reshape(nctx, nz, own, 3 * W)
    if fast:

        def slot(d):
            return lax.dynamic_index_in_dim(term, z ^ d, 1, keepdims=False)

        terms = [slot(0)] + [swapped(slot(d), "z", nz, d) for d in range(1, nz)]
    else:
        term = lax.psum_scatter(term.transpose(1, 0, 2, 3), "z", scatter_dimension=0, tiled=True)[0]
    input_grad, first_value_grad, qkv_rows = tail(dqkv3, x, dy1, gain_one, pos, qkv_arrays, qkv_pieces, keep)
    if fast:
        input_grad, share, *terms = lax.optimization_barrier((input_grad, share, *terms))
        term = sum(t.astype(F32) for t in terms).astype(BF)
        share = share.astype(F32)
        gate_share = halves_of(share)
    qkv_share = exchange(term).reshape(nctx, own, 3, W).transpose(1, 2, 0, 3).reshape(own, 3 * D).astype(F32)

    gain_own = lax.dynamic_slice_in_dim(gains, at, own, 1)
    if fast:
        _, rows_a, rows_b = lax.optimization_barrier((dqkv3, rows_a, rows_b))
        gate_rows = jnp.concatenate([rows_a[:, :wa], rows_b[:, :wb], rows_a[:, wa:], rows_b[:, wb:]], axis=1)
    else:
        qkv_rows = lax.dynamic_slice_in_dim(qkv_arrays[0], at, own, 0)
        gate_rows = lax.dynamic_slice_in_dim(arrays[1], at, own, 0)
    gain_one_share = jnp.sum(qkv_rows.astype(F32) * qkv_share, axis=1) / gain_own[0]
    gain_two_share = jnp.sum(gate_rows.astype(F32) * gate_share, axis=1) / gain_own[1]
    return (
        mixed_out[None],
        input_grad[None],
        first_value_grad[None],
        gain_one_share,
        qkv_share,
        out_share,
        gain_two_share,
        gate_share,
        down_share,
    )


def solution(mesh):
    ctx, fsdp = mesh.devices.shape
    split = Mesh(mesh.devices.reshape(ctx // 2, 2, fsdp), ("chip", "core", "z"))
    rows3 = P("z", CTX, None)
    weight = P("z", None)
    every = ("chip", "core", "z")
    return jax.shard_map(
        body,
        mesh=split,
        in_specs=(rows3, rows3, rows3, P("z"), weight, weight, P("z"), weight, weight, weight, P("z", CTX)),
        out_specs=(rows3, rows3, rows3, P(every), P(every, None), P(every, None), P(every), P(every, None), P(every, None)),
        check_vma=False,
    )
```

```python
import jax
import jax.numpy as jnp
from jax import lax
from jax.experimental import pallas as pl
from jax.experimental.pallas import tpu as pltpu
from jax.sharding import Mesh, PartitionSpec as P

D = 1024
HEADS = 16
HEAD = 64
FF = 2816
PROMPT = 2048
EPS = 1e-05
BASE = 10000.0
LOG2E = 1.4426950408889634
NEG = -1e30
C2 = 0.125 * LOG2E
CTX = ("chip", "core")
BF = jnp.bfloat16
F32 = jnp.float32


def dot(a, b, dims):
    return lax.dot_general(a, b, (dims, ((), ())), preferred_element_type=F32)


NN = ((1,), (0,))
NT = ((1,), (1,))
TN = ((0,), (0,))


def chunked(first, stop, sizes, fn, c):
    for n in sizes:
        count = (stop - first) // n
        c = lax.fori_loop(0, count, lambda t, c, n=n, first=first: fn(first + t * n, c, n), c)
        first = first + count * n
    return c


def visible(i, j, rows, run, lo):
    key = j * run + lax.broadcasted_iota(jnp.int32, (rows, run), 0)
    query = i * run + lax.broadcasted_iota(jnp.int32, (rows, run), 1)
    return (key <= query) & (key >= lo)


def attn_fwd(qT, kn, vT, lo, jlo, opos, *, run, nprompt, base, count):
    W, S = qT.shape
    hl = W // HEAD
    keys = S if base + count > nprompt else nprompt * run
    full_sizes, own_sizes = (8, 4, 2, 1), (4, 2, 1)

    def kern(jlo_ref, opos_ref, q_ref, k_ref, v_ref, lo_ref, o_ref, of_ref, lse_ref, s_scr):
        i = pl.program_id(0) + base
        qs = [q_ref[h * HEAD : (h + 1) * HEAD, :] for h in range(hl)]
        full = jnp.minimum(i, nprompt)
        own = jlo_ref[i]
        total = full + (i + 1 - own)

        def fold(f, s):
            return f(s.reshape(s.shape[0] // 8, 8, run), axis=0)

        def score(t, tops, n, shift, masked):
            tops = list(tops)
            for u in range(n):
                j = t + u + shift
                at = pl.multiple_of(j * run, run)
                row = pl.multiple_of((t + u) * run, run)
                if masked:
                    vis = visible(i, j, run, run, lo_ref[...])
                for h in range(hl):
                    s = dot(k_ref[h, pl.ds(at, run), :], qs[h], NN)
                    if masked:
                        s = jnp.where(vis, s, NEG)
                    s_scr[h, pl.ds(row, run), :] = s
                    tops[h] = jnp.maximum(tops[h], fold(jnp.max, s))
            return tuple(tops)

        tops = tuple(jnp.full((8, run), NEG, F32) for _ in range(hl))
        tops = chunked(0, full, full_sizes, lambda t, c, n: score(t, c, n, 0, False), tops)
        tops = chunked(full, total, own_sizes, lambda t, c, n: score(t, c, n, own - full, True), tops)
        m = [jnp.max(tops[h], axis=0, keepdims=True) * C2 for h in range(hl)]

        def weigh(t, c, n, shift):
            c = list(c)
            for u in range(n):
                at = pl.multiple_of((t + u + shift) * run, run)
                row = pl.multiple_of((t + u) * run, run)
                for h in range(hl):
                    l, acc = c[h]
                    p = jnp.exp2(s_scr[h, pl.ds(row, run), :] * C2 - m[h])
                    l = l + fold(jnp.sum, p)
                    acc = acc + dot(v_ref[h * HEAD : (h + 1) * HEAD, pl.ds(at, run)], p.astype(BF), NN)
                    c[h] = (l, acc)
            return tuple(c)

        c = tuple((jnp.zeros((8, run), F32), jnp.zeros((HEAD, run), F32)) for _ in range(hl))
        c = chunked(0, full, full_sizes, lambda t, c, n: weigh(t, c, n, 0), c)
        c = chunked(full, total, own_sizes, lambda t, c, n: weigh(t, c, n, own - full), c)
        outs = []
        for h in range(hl):
            l8, acc = c[h]
            l = jnp.sum(l8, axis=0, keepdims=True)
            o = acc / l
            of_ref[h * HEAD : (h + 1) * HEAD, :] = o
            lse_ref[h, :, :] = m[h] + jnp.log2(l)
            outs.append(o)
        o = jnp.concatenate(outs, axis=0) if hl > 1 else outs[0]
        o_ref[...] = o.T.astype(BF)

    rows = count * run
    return pl.pallas_call(
        kern,
        out_shape=(jax.ShapeDtypeStruct((rows, W), BF), jax.ShapeDtypeStruct((W, rows), F32), jax.ShapeDtypeStruct((hl, 1, rows), F32)),
        grid_spec=pltpu.PrefetchScalarGridSpec(
            num_scalar_prefetch=2,
            grid=(count,),
            in_specs=[
                pl.BlockSpec((W, run), lambda i, *_: (0, i + base)),
                pl.BlockSpec((hl, keys, HEAD), lambda i, *_: (0, 0, 0)),
                pl.BlockSpec((W, keys), lambda i, *_: (0, 0)),
                pl.BlockSpec((1, run), lambda i, *_: (0, i + base)),
            ],
            out_specs=[
                pl.BlockSpec((run, W), lambda i, jl, op: (op[i + base], 0)),
                pl.BlockSpec((W, run), lambda i, *_: (0, i)),
                pl.BlockSpec((hl, 1, run), lambda i, *_: (0, 0, i)),
            ],
            scratch_shapes=[pltpu.VMEM((hl, keys, run), F32)],
        ),
        compiler_params=params(),
        cost_estimate=cost(20 * rows * keys * W // 2, 12 * S * W, rows * keys // 2),
        name="attention_forward",
    )(jlo, opos, qT, kn, vT, lo)


def attn_bwd(qT, kn, kT, vn, don, of, lse, lo, jlo, spos, opos, cosT, sinT, sums, *, run, nprompt, base, count):
    W, S = qT.shape
    hl = W // HEAD
    hh = HEAD // 2
    keys = S if base + count > nprompt else nprompt * run
    later = base > 0
    P_ = nprompt * run
    full_sizes, own_sizes = (4, 2, 1), (2, 1)

    def unrotate(g, cos, sin):
        parts = []
        for h in range(hl):
            a = g[h * HEAD : h * HEAD + hh]
            b = g[h * HEAD + hh : (h + 1) * HEAD]
            parts += [a * cos + b * sin, b * cos - a * sin]
        return jnp.concatenate(parts, axis=0)

    def kern(jlo_ref, spos_ref, opos_ref, q_ref, k_ref, kT_ref, v_ref, do_ref, of_ref, lse_ref, lo_ref, cos_ref, sin_ref, *rest):
        if sums is not None:
            sk_ref, sv_ref = rest[:2]
            rest = rest[2:]
        if later:
            g_ref, ok_ref, ov_ref, dkT, dvT = rest
        else:
            g_ref, dkT, dvT = rest
        i = pl.program_id(0) + base

        @pl.when(pl.program_id(0) == 0)
        def _():
            if sums is not None:
                dkT[...] = sk_ref[...]
                dvT[...] = sv_ref[...]
            else:
                dkT[...] = jnp.zeros_like(dkT)
                dvT[...] = jnp.zeros_like(dvT)

        doT = do_ref[...].T
        dof = doT.astype(F32)
        qs = [q_ref[h * HEAD : (h + 1) * HEAD, :] for h in range(hl)]
        dos = [doT[h * HEAD : (h + 1) * HEAD, :] for h in range(hl)]
        delta = [
            jnp.sum(dof[h * HEAD : (h + 1) * HEAD] * of_ref[h * HEAD : (h + 1) * HEAD, :], axis=0, keepdims=True) for h in range(hl)
        ]
        ls = [lse_ref[h, :, :] for h in range(hl)]

        def tile(j, carry, n, masked):
            kb = n * run
            at = pl.multiple_of(j * run, run)
            if masked:
                vis = visible(i, j, kb, run, lo_ref[...])
            out = []
            for h in range(hl):
                hs = slice(h * HEAD, (h + 1) * HEAD)
                s = dot(k_ref[h, pl.ds(at, kb), :], qs[h], NN)
                p = jnp.exp2(s * C2 - ls[h])
                if masked:
                    p = jnp.where(vis, p, 0.0)
                dp = dot(v_ref[h, pl.ds(at, kb), :], dos[h], NN)
                ds = (p * (dp - delta[h])).astype(BF)
                dvT[hs, pl.ds(at, kb)] += dot(dos[h], p.astype(BF), NT)
                dkT[hs, pl.ds(at, kb)] += dot(qs[h], ds, NT)
                out.append(carry[h] + dot(kT_ref[hs, pl.ds(at, kb)], ds, NN))
            return tuple(out)

        c = tuple(jnp.zeros((HEAD, run), F32) for _ in range(hl))
        c = chunked(0, jnp.minimum(i, nprompt), full_sizes, lambda j, c, n: tile(j, c, n, False), c)
        c = chunked(jlo_ref[i], i + 1, own_sizes, lambda j, c, n: tile(j, c, n, True), c)
        dq = (jnp.concatenate(c, axis=0) if hl > 1 else c[0]) * 0.125

        def turned(g, b):
            at = pl.multiple_of(b * run, run)
            return unrotate(g, cos_ref[:, pl.ds(at, run)], sin_ref[:, pl.ds(at, run)]).T.astype(BF)

        row = pl.multiple_of(opos_ref[i] * run, run)
        g_ref[pl.ds(row, run), :W] = turned(dq, i)

        @pl.when(pl.program_id(0) == count - 1)
        def _():
            def finish(b, _):
                at = pl.multiple_of(b * run, run)
                row = pl.multiple_of(opos_ref[b] * run, run)
                g_ref[pl.ds(row, run), W : 2 * W] = turned(dkT[:, pl.ds(at, run)] * 0.125, b)
                g_ref[pl.ds(row, run), 2 * W :] = (dvT[:, pl.ds(at, run)] * 0.5).T.astype(BF)
                return 0

            lax.fori_loop(base, base + count, finish, 0)
            if later:
                ok_ref[...] = dkT[:, :P_]
                ov_ref[...] = dvT[:, :P_]

    full = lambda *s: pl.BlockSpec(s, lambda i, *_: (0,) * len(s))
    rows = count * run
    sum_shape = jax.ShapeDtypeStruct((W, P_), F32)
    return pl.pallas_call(
        kern,
        out_shape=(jax.ShapeDtypeStruct((rows, 3 * W), BF),) + ((sum_shape, sum_shape) if later else ()),
        grid_spec=pltpu.PrefetchScalarGridSpec(
            num_scalar_prefetch=3,
            grid=(count,),
            in_specs=[
                pl.BlockSpec((W, run), lambda i, *_: (0, i + base)),
                full(hl, keys, HEAD),
                full(W, keys),
                full(hl, keys, HEAD),
                pl.BlockSpec((run, W), lambda i, jl, sp, op: (sp[i + base], 0)),
                pl.BlockSpec((W, run), lambda i, *_: (0, i)),
                pl.BlockSpec((hl, 1, run), lambda i, *_: (0, 0, i)),
                pl.BlockSpec((1, run), lambda i, *_: (0, i + base)),
                full(hh, keys),
                full(hh, keys),
            ]
            + ([full(W, P_)] * 2 if sums is not None else []),
            out_specs=[full(rows, 3 * W)] + ([full(W, P_)] * 2 if later else []),
            scratch_shapes=[pltpu.VMEM((W, keys), F32)] * 2,
        ),
        compiler_params=params(),
        cost_estimate=cost(32 * rows * keys * W // 2, 24 * S * W, rows * keys // 2),
        name="attention_backward",
    )(jlo, spos, opos, qT, kn, kT, vn, don, of, lse, lo, cosT, sinT, *(sums or ()))


def cost(flops, nbytes, trans=0):
    return pl.CostEstimate(flops=int(flops), bytes_accessed=int(nbytes), transcendentals=int(trans))


def whole(*shape):
    return pl.BlockSpec(shape, lambda *_: (0,) * len(shape))


ANY = pl.BlockSpec(memory_space=pl.ANY)


def params():
    return pltpu.CompilerParams(vmem_limit_bytes=56 << 20)


def project(x, gain, w, vf, cos, sin, blk, *, run):
    S = x.shape[0]
    W = vf.shape[2]
    hl = W // HEAD
    nb = S // run
    per = nb // vf.shape[0]
    hh = HEAD // 2

    pair = 2

    def kern(blk_ref, x_ref, g_ref, w_ref, vf_ref, c_ref, s_ref, n_o, q_o, kT_o, vT_o, kn_o, vn_o):
        xf = x_ref[...].astype(F32)
        inv = lax.rsqrt(jnp.mean(xf * xf, axis=1, keepdims=True) + EPS)
        n1 = (xf * inv * g_ref[...]).astype(BF)
        n_o[...] = n1
        t = dot(w_ref[...], n1, NT)
        vT = vf_ref[0].astype(F32).T
        for r in range(pair):
            at = pl.ds(pl.multiple_of(blk_ref[pl.program_id(0) * pair + r] * run, run), run)
            rows = slice(r * run, (r + 1) * run)
            c = c_ref[:, at]
            s = s_ref[:, at]

            def rope(base):
                parts = []
                for h in range(hl):
                    a = t[base + h * HEAD : base + h * HEAD + hh, rows]
                    b = t[base + h * HEAD + hh : base + (h + 1) * HEAD, rows]
                    parts += [a * c - b * s, b * c + a * s]
                return jnp.concatenate(parts, axis=0)

            q_o[:, at] = rope(0).astype(BF)
            k = rope(W)
            kT_o[:, at] = k.astype(BF)
            v = 0.5 * t[2 * W :, rows] + 0.5 * vT[:, rows]
            vT_o[:, at] = v.astype(BF)
            for h in range(hl):
                kn_o[h, at, :] = k[h * HEAD : (h + 1) * HEAD].T.astype(BF)
                vn_o[h, at, :] = v[h * HEAD : (h + 1) * HEAD].T.astype(BF)

    T = jax.ShapeDtypeStruct((W, S), BF)
    N = jax.ShapeDtypeStruct((hl, S, HEAD), BF)
    rb = pl.BlockSpec((pair * run, D), lambda r, b: (r, 0))
    half = per // pair
    return pl.pallas_call(
        kern,
        out_shape=(jax.ShapeDtypeStruct((S, D), BF), T, T, T, N, N),
        grid_spec=pltpu.PrefetchScalarGridSpec(
            num_scalar_prefetch=1,
            grid=(nb // pair,),
            in_specs=[rb, whole(1, D), whole(3 * W, D), pl.BlockSpec((1, pair * run, W), lambda r, b: (r // half, r % half, 0)), whole(hh, S), whole(hh, S)],
            out_specs=[rb, whole(W, S), whole(W, S), whole(W, S), whole(hl, S, HEAD), whole(hl, S, HEAD)],
        ),
        compiler_params=params(),
        cost_estimate=cost(6 * S * D * W, 4 * S * D + 12 * S * W),
        name="project_qkv",
    )(blk, x, gain, w, vf, cos, sin)


def load_pieces(pieces, refs, pos_ref, dst, sems):
    copies = []
    for ref, row, rows, col, place, sem in pieces:
        at = pl.multiple_of(pos_ref[place], rows)
        copies.append(
            pltpu.make_async_copy(
                refs[ref].at[pl.ds(row, rows), pl.ds(col, dst.shape[1])], dst.at[pl.ds(at, rows), :], sems.at[sem]
            )
        )
    return copies


CUT = 1536
HALF = D // 2


def column_pieces(pieces, first, width):
    return [(ref, row, size, col + first, place, sem) for ref, row, size, col, place, sem in pieces]


def feed_forward(start, carried, attn3, x, og, gain, pos, arrays, out_pieces, gate_pieces, down_pieces, keep):
    n, rows, W = attn3.shape
    lo, hi = (0, CUT) if start else (CUT, FF)
    width = hi - lo
    FC = width // 2
    nsem = len(out_pieces) + 2 * len(gate_pieces) + len(down_pieces)
    na = len(arrays)
    last = pos.shape[0]
    ncarry = len(carried)

    def kern(pos_ref, a_ref, x_ref, og_ref, g_ref, *rest):
        refs = rest[:na]
        rest = rest[na:]
        cin, rest = rest[:ncarry], rest[ncarry:]
        if start:
            r_o, near_o, far_o, wr_o, y_o, n2_o, m_o, acc_o = rest[:8]
            wo, wg, wu, wd, al, sems = rest[8:]
        else:
            mixed_o, r_o, low_o, dy_o, da_o, wr_o = rest[:6]
            wo, wg, wu, wd, acc_m, acc_n, sems = rest[6:]
        f = pl.program_id(0)

        def sides(ref, place):
            for out, c in ((near_o, pos_ref[last - 2]), (far_o, 1 - pos_ref[last - 2])):
                for e in range(D // 256):
                    out[:, place + e * 128 : place + (e + 1) * 128] = ref[:, pl.ds(pl.multiple_of((2 * e + c) * 128, 128), 128)]

        @pl.when(f == 0)
        def _():
            ng = len(gate_pieces)
            first = load_pieces(out_pieces, refs, pos_ref, wo, sems)
            second = load_pieces(column_pieces(gate_pieces, lo, 0), refs, pos_ref, wg, sems)
            second += load_pieces([(r, a, b, c + FF + lo, p, s + nsem - ng) for r, a, b, c, p, s in renumber(gate_pieces)], refs, pos_ref, wu, sems)
            third = load_pieces(column_pieces(down_pieces, lo, 0), refs, pos_ref, wd, sems)
            for cp in (first + second + third) if start else (second + third + first):
                cp.start()
            if start:
                for i in range(n):
                    al[:, i * W : (i + 1) * W] = a_ref[i]
                sides(og_ref, 2 * HALF)
                sides(al, HALF)
                for cp in first:
                    cp.wait()
                y = x_ref[...].astype(F32) + dot(al[...], wo[...], NN)
                y_o[...] = y
                inv = lax.rsqrt(jnp.mean(y * y, axis=1, keepdims=True) + EPS)
                n2_o[...] = (y * inv * g_ref[...]).astype(BF)
                sides(n2_o, 0)
                m_o[...] = y
                acc_o[...] = jnp.zeros_like(acc_o)
            else:
                acc_m[...] = cin[2][...]
                acc_n[...] = cin[3][...]
            for cp in second + third:
                cp.wait()
            if not start:
                for cp in first:
                    cp.wait()

        n2 = n2_o if start else cin[1]
        am = m_o if start else acc_m
        an = acc_o if start else acc_n
        c0 = pl.multiple_of(f * FC, 128)
        a = n2[...]
        g = dot(a, wg[:, pl.ds(c0, FC)], NN)
        u = dot(a, wu[:, pl.ds(c0, FC)], NN)
        dh = dot(og_ref[...], wd[:, pl.ds(c0, FC)], NN)
        sg = jax.nn.sigmoid(g)
        silu = g * sg
        hid = (silu * u).astype(BF)
        dg = (dh * u * sg * (1.0 + g * (1.0 - sg))).astype(BF)
        du = (dh * silu).astype(BF)
        r_o[:, :FC] = dg
        r_o[:, FC : 2 * FC] = du
        r_o[:, 2 * FC :] = hid
        am[...] += dot(hid, wd[:, pl.ds(c0, FC)], NT)
        an[...] += dot(dg, wg[:, pl.ds(c0, FC)], NT) + dot(du, wu[:, pl.ds(c0, FC)], NT)

        @pl.when(f == 1)
        def _():
            at = pl.multiple_of(pos_ref[last - 1], keep)
            wr_o[:, :width] = wg[pl.ds(at, keep), :]
            wr_o[:, width:] = wu[pl.ds(at, keep), :]
            if not start:
                mixed_o[...] = am[...].astype(BF)
                y = cin[0][...]
                inv = lax.rsqrt(jnp.mean(y * y, axis=1, keepdims=True) + EPS)
                xh = y * inv
                t = an[...] * g_ref[...]
                dy = og_ref[...].astype(F32) + inv * (t - xh * jnp.mean(t * xh, axis=1, keepdims=True))
                dy_o[...] = dy
                low = dy.astype(BF)
                low_o[...] = low
                da = dot(low, wo[...], NT).astype(BF)
                for i in range(n):
                    da_o[i] = da[:, i * W : (i + 1) * W]

    wide = jax.ShapeDtypeStruct((rows, D), F32)
    side = jax.ShapeDtypeStruct((rows, 3 * HALF), BF)
    low = jax.ShapeDtypeStruct((rows, D), BF)
    right = jax.ShapeDtypeStruct((rows, 3 * width), BF)
    own_rows = jax.ShapeDtypeStruct((keep, 2 * width), BF)
    rspec = pl.BlockSpec((rows, 3 * FC), lambda f, *_: (0, f))
    full = whole(rows, D)
    if start:
        outs = (right, side, side, own_rows, wide, low, wide, wide)
        specs = [rspec, whole(rows, 3 * HALF), whole(rows, 3 * HALF), whole(keep, 2 * width), full, full, full, full]
        extra = [pltpu.VMEM((rows, D), BF)]
    else:
        outs = (low, right, low, wide, jax.ShapeDtypeStruct((n, rows, W), BF), own_rows)
        specs = [full, rspec, full, full, whole(n, rows, W), whole(keep, 2 * width)]
        extra = [pltpu.VMEM((rows, D), F32)] * 2
    return pl.pallas_call(
        kern,
        out_shape=outs,
        grid_spec=pltpu.PrefetchScalarGridSpec(
            num_scalar_prefetch=1,
            grid=(2,),
            in_specs=[whole(n, rows, W) if start else ANY, full if start else ANY, full, whole(1, D)] + [ANY] * na + [full] * ncarry,
            out_specs=specs,
            scratch_shapes=[
                pltpu.VMEM((D, D), BF),
                pltpu.VMEM((D, width), BF),
                pltpu.VMEM((D, width), BF),
                pltpu.VMEM((D, width), BF),
                *extra,
                pltpu.SemaphoreType.DMA((nsem,)),
            ],
        ),
        compiler_params=params(),
        cost_estimate=cost(4 * rows * D * (D + 6 * width), 2 * D * (D + 3 * width) + 2 * rows * (14 * D + 3 * width)),
        name="feed_forward_start" if start else "feed_forward_end",
    )(pos, attn3, x, og, gain, *arrays, *carried)


def renumber(pieces):
    return [(r, a, b, c, p, i) for i, (r, a, b, c, p, _) in enumerate(pieces)]


def tail(dqkv3, x, dy1, gain, pos, arrays, pieces, keep):
    n, rows, W3 = dqkv3.shape
    W = W3 // 3
    na = len(arrays)
    group = max(1, len(pieces) // 4)

    def kern(pos_ref, d_ref, x_ref, dy_ref, g_ref, *rest):
        refs = rest[:na]
        ig_o, fv_o, wr_o = rest[na : na + 3]
        w, dn, sems = rest[na + 3 :]
        copies = load_pieces(pieces, refs, pos_ref, w, sems)
        for cp in copies:
            cp.start()
        if n > 1:
            d = jnp.concatenate([d_ref[i, :, p * W : (p + 1) * W] for p in range(3) for i in range(n)], axis=1)
        else:
            d = d_ref[0]
        fv_o[...] = d[:, 2 * D :].astype(F32)
        for cp in copies:
            cp.wait()
        t = dot(d, w[...], NT)
        wr_o[...] = w[pl.ds(pl.multiple_of(pos_ref[pos.shape[0] - 1], keep), keep), :]
        xf = x_ref[...].astype(F32)
        inv = lax.rsqrt(jnp.mean(xf * xf, axis=1, keepdims=True) + EPS)
        xh = xf * inv
        t = t * g_ref[...]
        ig_o[...] = dy_ref[...] + inv * (t - xh * jnp.mean(t * xh, axis=1, keepdims=True))

    o = jax.ShapeDtypeStruct((rows, D), F32)
    return pl.pallas_call(
        kern,
        out_shape=(o, o, jax.ShapeDtypeStruct((keep, 3 * D), BF)),
        grid_spec=pltpu.PrefetchScalarGridSpec(
            num_scalar_prefetch=1,
            grid=(1,),
            in_specs=[whole(n, rows, W3), whole(rows, D), whole(rows, D), whole(1, D)] + [ANY] * na,
            out_specs=[whole(rows, D), whole(rows, D), whole(keep, 3 * D)],
            scratch_shapes=[pltpu.VMEM((D, 3 * D), BF), pltpu.VMEM((rows, D), F32), pltpu.SemaphoreType.DMA((len(pieces),))],
        ),
        compiler_params=params(),
        cost_estimate=cost(6 * rows * D * D, 6 * D * D + rows * D * 20),
        name="input_gradient",
    )(pos, dqkv3, x, dy1, gain, *arrays)


def weight_terms(near, far, r_near, r_far, orders, low, low_far):
    rows = near.shape[0]
    width = r_near.shape[1] // 3
    FC = width // 2
    nb = orders.shape[1]
    own = HALF // nb
    n = 4
    more = low is not None
    cols = width + (D if more else 0)

    def kern(o_ref, na, fa, ra, rb, *rest):
        if more:
            nd, fd = rest[:2]
            rest = rest[2:]
        t_o, d_o, lt0, lt = rest
        f = pl.program_id(0)

        @pl.when(f == 0)
        def _():
            for i, side in ((0, na), (1, fa)):
                for p in (0, 1, 2) if more else (0, 2):
                    lt0[p, :, i * rows : (i + 1) * rows] = side[:, p * HALF : (p + 1) * HALF].T
            for p in (0, 1, 2) if more else (0, 2):
                for b in range(nb):
                    at = o_ref[min(p, 1), b]
                    lt[p, b * own : (b + 1) * own, :] = lt0[p, pl.ds(pl.multiple_of(at * own, own), own), :]

        def put(p, a, b, out, place, size):
            t = dot(lt[p, :, :rows], a, NN) + dot(lt[p, :, rows:], b, NN)
            for e in range(n):
                out[e, :, pl.ds(place, size)] = t[e * HALF // n : (e + 1) * HALF // n].astype(BF)

        put(0, ra[:, : 2 * FC], rb[:, : 2 * FC], t_o, pl.multiple_of(2 * FC * f, 128), 2 * FC)
        put(2, ra[:, 2 * FC :], rb[:, 2 * FC :], d_o, pl.multiple_of(FC * f, 128), FC)
        if more:

            @pl.when(f == 1)
            def _():
                put(1, nd[...], fd[...], d_o, width, D)

    rb = pl.BlockSpec((rows, 3 * FC), lambda f, *_: (0, f))
    return pl.pallas_call(
        kern,
        out_shape=(jax.ShapeDtypeStruct((n, HALF // n, 2 * width), BF), jax.ShapeDtypeStruct((n, HALF // n, cols), BF)),
        grid_spec=pltpu.PrefetchScalarGridSpec(
            num_scalar_prefetch=1,
            grid=(2,),
            in_specs=[whole(rows, 3 * HALF)] * 2 + [rb] * 2 + ([whole(rows, D)] * 2 if more else []),
            out_specs=[whole(n, HALF // n, 2 * width), whole(n, HALF // n, cols)],
            scratch_shapes=[pltpu.VMEM((3, HALF, 2 * rows), BF)] * 2,
        ),
        compiler_params=params(),
        cost_estimate=cost(4 * rows * HALF * (cols + 2 * width), 2 * (2 * rows + HALF) * (cols + 2 * width) + 12 * rows * HALF),
        name="weight_terms",
    )(orders, near, far, r_near, r_far, *((low, low_far) if more else ()))


def exchange(v):
    return lax.all_to_all(v, CTX, 0, 0, tiled=True)


def swapped(v, axes, size, mask):
    return lax.ppermute(v, axes, [(i, i ^ mask) for i in range(size)])


def gathered(v, axes, size, index):
    parts = [v] + [swapped(v, axes, size, s) for s in range(1, size)]
    return jnp.stack([lax.select_n(index ^ a, *parts) for a in range(size)])


def half_rows(w, core):
    half = w.shape[0] // 2
    return lax.dynamic_slice_in_dim(w, core * half, half, 0)


def body(tokens_in, value_first, out_grad, gain_attn, w_qkv, w_out, gain_mlp, w_gate_up, w_down, cont_lengths, row_token):
    x = tokens_in[0]
    og = out_grad[0]
    rows = x.shape[0]
    nchip = lax.axis_size("chip")
    nctx = lax.axis_size(CTX)
    nz = lax.axis_size("z")
    me = lax.axis_index(CTX)
    chip = lax.axis_index("chip")
    core = lax.axis_index("core")
    z = lax.axis_index("z")
    fast = nctx == 8 and nz == 4
    S = rows * nctx
    W = D // nctx
    run = PROMPT // nctx
    nb = S // run
    nprompt = PROMPT // run
    shard = D // nz
    own = D // (nctx * nz)
    at = (me * nz + z) * own
    keep = own if fast else 16

    x_all = lax.all_gather(x, CTX, axis=0, tiled=True)
    w_own = lax.dynamic_index_in_dim(w_qkv.reshape(shard, 3, nctx, W), me, 2, keepdims=False).reshape(shard, 3 * W)
    gains = jnp.stack([gain_attn, gain_mlp])
    runs = (row_token[0, ::run] // run).astype(BF)
    runs = jnp.pad(runs[None], ((0, 15), (0, W - runs.shape[0])))
    vf = jnp.concatenate([value_first[0].reshape(rows, nctx, W).transpose(1, 0, 2), jnp.broadcast_to(runs, (nctx, 16, W))], axis=1)
    vf = exchange(vf)
    if fast:
        pay = jnp.concatenate([w_own, jnp.pad(gains, ((0, 14), (0, 3 * W - shard)))], axis=0)
        pay = gathered(pay, "z", nz, z)
    else:
        w_own = lax.all_gather(w_own, "z", axis=0, tiled=True).T
        gains = lax.all_gather(gains, "z", axis=1, tiled=True).astype(F32)
        gain_one, gain_two = gains[0:1], gains[1:2]
        blk = vf[:, rows, : nb // nctx].astype(jnp.int32).reshape(nb)

    lengths = cont_lengths[0]
    count = jnp.arange(lengths.shape[0], dtype=jnp.int32)
    starts = PROMPT + jnp.sum(jnp.where(count[:, None] < count[None, :], lengths[:, None], 0), axis=0)
    token = jnp.arange(S, dtype=jnp.int32)
    passed = token[None, :] >= starts[:, None]
    opening = jnp.max(jnp.where(passed, starts[:, None], 0), axis=0).astype(jnp.int32)
    position = jnp.where(opening > 0, PROMPT + token - opening, token)
    freq = BASE ** (-(jnp.arange(HEAD // 2, dtype=F32) * 2.0 / HEAD))
    angles = freq[:, None] * position.astype(F32)[None, :]
    cosT = jnp.cos(angles)
    sinT = jnp.sin(angles)
    block = jnp.arange(nb, dtype=jnp.int32)
    jlo = jnp.where(block < nprompt, block, opening[::run] // run).astype(jnp.int32)
    opening = opening[None, :]

    if fast:
        w_own = pay[:, :shard].reshape(D, 3 * W).T
        gains = pay[:, shard : shard + 2, :shard].transpose(1, 0, 2).reshape(2, D).astype(F32)
        gain_one, gain_two = gains[0:1], gains[1:2]
        blk = vf[:, rows, : nb // nctx].astype(jnp.int32).reshape(nb)
    spos = jnp.sum(jnp.where(blk[None, :] == block[:, None], block[None, :], 0), axis=1).astype(jnp.int32)

    if fast:
        piece = shard // nctx
        mine = jnp.concatenate([lax.dynamic_slice_in_dim(w, me * piece, piece, 0) for w in (w_out, w_gate_up)], axis=1)
        near = jnp.concatenate([swapped(mine, "z", nz, d) for d in range(1, nz)], axis=0)
        down = half_rows(w_down, core)
        qkv = half_rows(w_qkv, core)
        x_all, near, vf, w_own, gains, gain_one, blk, spos, cosT, sinT, jlo, down, qkv = lax.optimization_barrier(
            (x_all, near, vf, w_own, gains, gain_one, blk, spos, cosT, sinT, jlo, down, qkv)
        )
        planes = [near] + [swapped(near, "chip", nchip, e) for e in range(1, nchip)]
        down = lax.all_gather(down, "z", axis=0, tiled=True)
        pos = [z * shard]
        out_pieces, gate_pieces = [[(i, 0, shard, 0, 0, i)] for i in range(2)]
        sem = 2
        for f in range(2):
            for e in range(nchip):
                for d in range(1, nz):
                    pos.append((z ^ d) * shard + ((chip ^ e) * 2 + (core ^ f)) * piece)
                    ref = 2 + f * nchip + e
                    out_pieces.append((ref, (d - 1) * piece, piece, 0, len(pos) - 1, sem))
                    gate_pieces.append((ref, (d - 1) * piece, piece, D, len(pos) - 1, sem + 1))
                    sem += 2
        down_pieces = []
        half = shard // 2
        for k in range(nz):
            for f in range(2):
                pos.append(k * shard + (core ^ f) * half)
                down_pieces.append((2 + 2 * nchip + f, k * half, half, 0, len(pos) - 1, sem))
                sem += 1
        qkv_pieces = []
        for d in range(nz):
            for f in range(2):
                pos.append(d * shard + (core ^ f) * half)
                qkv_pieces.append((f, d * half, half, 0, len(pos) - 1, len(qkv_pieces)))
        pos = jnp.stack(pos + [core, at]).astype(jnp.int32)
    else:
        arrays = [lax.all_gather(w, "z", axis=0, tiled=True) for w in (w_out, w_gate_up, w_down)]
        qkv_arrays = [lax.all_gather(w_qkv, "z", axis=0, tiled=True)]
        pos = jnp.zeros((3,), jnp.int32)
        out_pieces, gate_pieces, down_pieces = [[(i, 0, D, 0, 0, i)] for i in range(3)]
        qkv_pieces = [(0, 0, D, 0, 0, 0)]

    normed_all, qT, kT, vT, kn, vn = project(x_all, gain_one, w_own, vf, cosT, sinT, blk, run=run)
    everything = {"run": run, "nprompt": nprompt, "base": 0, "count": nb}
    attn_all, attnT, lse = attn_fwd(qT, kn, vT, opening, jlo, spos, **everything)
    if fast:
        attn_all, qkv, down, *planes = lax.optimization_barrier((attn_all, qkv, down, *planes))
        qkv = lax.all_gather(qkv, "z", axis=0, tiled=True)
        arrays = [w_out, w_gate_up] + planes + [swapped(p, "core", 2, 1) for p in planes] + [down, swapped(down, "core", 2, 1)]
    attn3 = exchange(attn_all.reshape(nctx, rows, W))
    if not fast:
        attn3 = attn3.transpose(1, 0, 2).reshape(1, rows, D)
    pieces = (out_pieces, gate_pieces, down_pieces)
    right_a, side_near, side_far, rows_a, *carried = feed_forward(True, (), attn3, x, og, gain_two, pos, arrays, *pieces, keep)
    if fast:
        come_right_a = swapped(right_a, "core", 2, 1)
        come_side = swapped(side_far, "core", 2, 1)
    mixed_out, right_b, dy1_low, dy1, dattn3, rows_b = feed_forward(False, carried, attn3, x, og, gain_two, pos, arrays, *pieces, keep)
    if fast:
        dattn3, right_b, dy1_low, qkv, come_right_a, come_side = lax.optimization_barrier(
            (dattn3, right_b, dy1_low, qkv, come_right_a, come_side)
        )
    else:
        dattn3 = dattn3.reshape(rows, nctx, W).transpose(1, 0, 2)
    dattn_all = exchange(dattn3).reshape(S, W)
    wa, wb = CUT, FF - CUT

    def halves_of(v):
        a = v[:, : 2 * wa].reshape(v.shape[0], 2, 2, wa // 2)
        b = v[:, 2 * wa : 2 * FF].reshape(v.shape[0], 2, 2, wb // 2)
        return jnp.concatenate([v_.reshape(v.shape[0], -1) for i in range(2) for v_ in (a[:, :, i], b[:, :, i])], axis=1)

    if fast:
        come_right_b = swapped(right_b, "core", 2, 1)
        come_low = swapped(dy1_low, "core", 2, 1)
        by_chip = [(chip ^ e) * nz + k for e in range(nchip) for k in range(nz)]
        by_all = [k + 0 * chip for k in range(nchip * nz)]
        by_fsdp = [(chip ^ e) * nz + k for k in range(nz) for e in range(nchip)]
        orders_a = jnp.stack([jnp.stack(by_chip), jnp.stack(by_fsdp)]).astype(jnp.int32)
        orders_b = jnp.stack([jnp.stack(by_all), jnp.stack(by_fsdp)]).astype(jnp.int32)
        terms_a, downs_a = weight_terms(side_near, come_side, right_a, come_right_a, orders_a, None, None)
        terms_b, downs_b = weight_terms(side_near, come_side, right_b, come_right_b, orders_b, dy1_low, come_low)
        dattn_all, terms_b, downs_b = lax.optimization_barrier((dattn_all, terms_b, downs_b))
        qkv_arrays = [qkv, swapped(qkv, "core", 2, 1)]
        terms_a = [terms_a[0]] + [swapped(terms_a[e], "chip", nchip, e) for e in range(1, nchip)]
        terms_b = lax.all_to_all(terms_b, "chip", 0, 0, tiled=True)
        downs = [lax.psum_scatter(v, "z", scatter_dimension=0, tiled=True)[0] for v in (downs_a, downs_b)]
    else:
        chunk = lambda v, w: v.reshape(rows, 2, 3, w // 2)
        ra, rb = chunk(right_a, wa), chunk(right_b, wb)
        part = lambda i: jnp.concatenate([ra[:, :, i].reshape(rows, wa), rb[:, :, i].reshape(rows, wb)], axis=1)
        normed_two = jnp.stack([side_near[:, :HALF].reshape(rows, D // 256, 128), side_far[:, :HALF].reshape(rows, D // 256, 128)], axis=2).reshape(rows, D)
        terms = jnp.concatenate(
            [dot(attn3[0], dy1_low, TN), dot(normed_two, part(0), TN), dot(normed_two, part(1), TN), dot(og, part(2), TN)], axis=1
        ).astype(BF)
        share = lax.psum_scatter(terms, CTX, scatter_dimension=0, tiled=True)
        share = lax.psum_scatter(share, "z", scatter_dimension=0, tiled=True).astype(F32)
        out_share, gate_share, down_share = share[:, :D], share[:, D : D + 2 * FF], share[:, D + 2 * FF :]

    (dqkv_own,) = attn_bwd(qT, kn, kT, vn, dattn_all, attnT, lse, opening, jlo, spos, spos, cosT, sinT, None, **everything)
    if fast:
        dqkv_own, terms_a, terms_b, downs = lax.optimization_barrier((dqkv_own, terms_a, terms_b, downs))

        share = jnp.concatenate(
            [sum(v.astype(F32) for v in terms_a).astype(BF), sum(terms_b[k].astype(F32) for k in range(nchip)).astype(BF)], axis=1
        )
        dqkv_term, share = lax.optimization_barrier((dqkv_own, share))
        share = lax.psum_scatter(share, "z", scatter_dimension=0, tiled=True)
    dqkv3 = exchange(dqkv_own.reshape(nctx, rows, 3 * W))
    if fast:
        dqkv3, downs = lax.optimization_barrier((dqkv3, downs))
        downs = jnp.concatenate(downs, axis=1).reshape(nchip, own, FF + D)
        downs = [downs[0]] + [swapped(downs[e], "chip", nchip, e) for e in range(1, nchip)]
        down_share = sum(v[:, :FF].astype(F32) for v in downs)
        out_share = sum(v[:, FF:].astype(F32) for v in downs)
    if not fast:
        dqkv3 = dqkv3.reshape(nctx, rows, 3, W).transpose(1, 2, 0, 3).reshape(1, rows, 3 * D)

    term = dot(normed_all, dqkv_term if fast else dqkv_own, TN).astype(BF).reshape(nctx, nz, own, 3 * W)
    if fast:

        def slot(d):
            return lax.dynamic_index_in_dim(term, z ^ d, 1, keepdims=False)

        terms = [slot(0)] + [swapped(slot(d), "z", nz, d) for d in range(1, nz)]
    else:
        term = lax.psum_scatter(term.transpose(1, 0, 2, 3), "z", scatter_dimension=0, tiled=True)[0]
    input_grad, first_value_grad, qkv_rows = tail(dqkv3, x, dy1, gain_one, pos, qkv_arrays, qkv_pieces, keep)
    if fast:
        input_grad, share, *terms = lax.optimization_barrier((input_grad, share, *terms))
        term = sum(t.astype(F32) for t in terms).astype(BF)
        share = share.astype(F32)
        gate_share = halves_of(share)
    qkv_share = exchange(term).reshape(nctx, own, 3, W).transpose(1, 2, 0, 3).reshape(own, 3 * D).astype(F32)

    gain_own = lax.dynamic_slice_in_dim(gains, at, own, 1)
    if fast:
        _, rows_a, rows_b = lax.optimization_barrier((dqkv3, rows_a, rows_b))
        gate_rows = jnp.concatenate([rows_a[:, :wa], rows_b[:, :wb], rows_a[:, wa:], rows_b[:, wb:]], axis=1)
    else:
        qkv_rows = lax.dynamic_slice_in_dim(qkv_arrays[0], at, own, 0)
        gate_rows = lax.dynamic_slice_in_dim(arrays[1], at, own, 0)
    gain_one_share = jnp.sum(qkv_rows.astype(F32) * qkv_share, axis=1) / gain_own[0]
    gain_two_share = jnp.sum(gate_rows.astype(F32) * gate_share, axis=1) / gain_own[1]
    return (
        mixed_out[None],
        input_grad[None],
        first_value_grad[None],
        gain_one_share,
        qkv_share,
        out_share,
        gain_two_share,
        gate_share,
        down_share,
    )


def solution(mesh):
    ctx, fsdp = mesh.devices.shape
    split = Mesh(mesh.devices.reshape(ctx // 2, 2, fsdp), ("chip", "core", "z"))
    rows3 = P("z", CTX, None)
    weight = P("z", None)
    every = ("chip", "core", "z")
    return jax.shard_map(
        body,
        mesh=split,
        in_specs=(rows3, rows3, rows3, P("z"), weight, weight, P("z"), weight, weight, weight, P("z", CTX)),
        out_specs=(rows3, rows3, rows3, P(every), P(every, None), P(every, None), P(every), P(every, None), P(every, None)),
        check_vma=False,
    )
```
